128 devices in a mesh: dp: 8 (over x, y_lo), tensor: 16 (over y_hi, z, core).
Axes of the slice: x: 4, y: 4 (y_hi: 2, y_lo: 2; y = y_hi * 2 + y_lo), z: 4, core: 2. Of those that a mesh axis runs over, the one named last changes fastest.
Arguments:
- enc_tokens: bfloat16 [128, 128, 1024], P(('dp', 'tensor')), may hold values from -6 to 6
- src_lengths: int32 [128], replicated, may hold values from 1 to 128, as said below
- enc_gain: float32 [1024], replicated, may hold values from 0.1 to 1.9
- enc_query: bfloat16 [1024, 8192], P(None, 'tensor'), may hold values from -0.1875 to 0.1875
- enc_key: bfloat16 [1024, 8192], P(None, 'tensor'), may hold values from -0.1875 to 0.1875
- enc_value: bfloat16 [1024, 8192], P(None, 'tensor'), may hold values from -0.1875 to 0.1875
- enc_output: bfloat16 [8192, 1024], P('tensor'), may hold values from -0.0625 to 0.0625
- enc_bias: float32 [64, 33], P('tensor'), may hold values from -3 to 260
- mem_gain: float32 [1024], replicated, may hold values from 0.1 to 1.9
- dec_tokens: bfloat16 [128, 64, 1024], P(('dp', 'tensor')), may hold values from -6 to 6
- tgt_lengths: int32 [128], P(('dp', 'tensor')), may hold values from 1 to 64
- lang_tags: int32 [128], P('dp'), may hold values from 0 to 7
- lang_table: bfloat16 [8, 1024], replicated, may hold values from -6 to 6
- cross_gain: float32 [1024], replicated, may hold values from 0.1 to 1.9
- cross_query: bfloat16 [1024, 8192], P(None, 'tensor'), may hold values from -0.1875 to 0.1875
- cross_key: bfloat16 [1024, 8192], P(None, 'tensor'), may hold values from -0.1875 to 0.1875
- cross_value: bfloat16 [1024, 8192], P(None, 'tensor'), may hold values from -0.1875 to 0.1875
- cross_output: bfloat16 [8192, 1024], P('tensor'), may hold values from -0.0625 to 0.0625
- ffn_gain: float32 [1024], replicated, may hold values from 0.1 to 1.9
- ffn_in: bfloat16 [1024, 32768], P(None, 'tensor'), may hold values from -0.1875 to 0.1875
- ffn_out: bfloat16 [32768, 1024], P('tensor'), may hold values from -0.03125 to 0.03125
Outputs:
- enc_memory: bfloat16 [128, 128, 1024], P(('dp', 'tensor'))
- dec_out: bfloat16 [128, 64, 1024], P(('dp', 'tensor'))
The draws below stay inside these ranges and needn't reach their ends.
Inputs may be any that keep to these rules, and one draw needn't show every extreme that they name: `src_lengths`: never falling along the batch; the first is 1 and the last is 128.
All inputs are finite; a program needn't handle non-finite values.
Results may differ from the reference program's by a relative error of at most 0.014.
Values may be sent and summed in bfloat16 or wider, within the bound.
A program may use at most 128 MiB of HBM per device.

```python
import jax
import jax.numpy as jnp
from jax import lax

D = 1024
HD = 128
HEADS = 64
FF = 32768
SRC = 128
TGT = 64
MAXREL = 16
NB = 33
LANGS = 8
PER_PAIR = 2
BATCH = 128
N_DP = 8
N_TENSOR = 16


def bias_draw(key):
    base_key = jax.random.fold_in(key, 0)
    return jnp.clip(jax.random.normal(base_key, (HEADS, NB), jnp.float32), -3.0, 3.0)


def draw_enc_bias(key, part):
    return bias_draw(jax.random.fold_in(key, 11))


def draw_src_lengths(key, part):
    drawn = jax.random.randint(jax.random.fold_in(key, 5), (BATCH,), 1, SRC + 1)
    ordered = jnp.sort(drawn)
    return ordered.at[0].set(1).at[BATCH - 1].set(SRC)


def touch_ends(entries, stream_key, least, top_value):
    index_at = [jax.random.randint(jax.random.fold_in(stream_key, axis), (), 0, length) for axis, length in enumerate(entries.shape)]
    widest = entries.shape.index(max(entries.shape))
    beside = index_at[:widest] + [(index_at[widest] + 1) % entries.shape[widest]] + index_at[widest + 1:]
    return entries.at[tuple(index_at)].set(least).at[tuple(beside)].set(top_value)


def shard_levels(key, dims, pieces, smallest, top_value):
    def one(dim, parts):
        draws = jax.random.uniform(jax.random.fold_in(jax.random.fold_in(key, 6), dim), (parts,), jnp.float32, smallest / len(pieces), top_value / len(pieces))
        return jnp.repeat(jnp.exp(draws), dims[dim] // parts).reshape((-1,) + (1,) * (len(dims) - dim - 1))

    loudness = one(*pieces[0])
    for cut in pieces[1:]:
        loudness = loudness * one(*cut)
    return loudness


def scatter_about(stream_key, dims, width, reach, pieces=(), held_as=jnp.bfloat16):
    array = jax.random.normal(stream_key, dims, jnp.float32) * width
    if len(pieces) > 0:
        array = shard_levels(stream_key, dims, pieces, -0.22, 0.18) * array
    return jnp.clip(array, min=-reach, max=reach).astype(held_as)


def setup_inputs(seed: int = 0) -> dict:
    streams_of = jax.random.split(jax.random.key(seed), 22)
    enc_tokens = scatter_about(streams_of[0], (BATCH, SRC, D), 1.0, 6.0, ((0, 128),))
    src_lengths = draw_src_lengths(jax.random.fold_in(streams_of[21], 71), 0)
    enc_gain = jnp.clip(1.0 + 0.18 * jax.random.normal(streams_of[2], (D,), jnp.float32), 0.1, 1.9)
    enc_query = scatter_about(streams_of[3], (D, HEADS * HD), D ** -0.5, 0.1875, ((1, 16),))
    enc_key = scatter_about(streams_of[4], (D, HEADS * HD), D ** -0.5, 0.1875, ((1, 16),))
    enc_value = scatter_about(streams_of[5], (D, HEADS * HD), D ** -0.5, 0.1875, ((1, 16),))
    enc_output = scatter_about(streams_of[6], (HEADS * HD, D), (HEADS * HD) ** -0.5, 0.0625, ((0, 16),))
    enc_bias = draw_enc_bias(jax.random.fold_in(streams_of[21], 71), 0)
    mem_gain = jnp.clip(1.0 + 0.18 * jax.random.normal(streams_of[8], (D,), jnp.float32), 0.1, 1.9)
    dec_tokens = scatter_about(streams_of[9], (BATCH, TGT, D), 1.0, 6.0, ((0, 128),))
    tgt_lengths = touch_ends(jax.random.randint(streams_of[10], (BATCH,), 1, TGT + 1), jax.random.fold_in(streams_of[10], 1), 1, TGT).astype(jnp.int32)
    lang_tags = touch_ends(jax.random.randint(streams_of[11], (BATCH,), 0, LANGS), jax.random.fold_in(streams_of[11], 1), 0, LANGS - 1).astype(jnp.int32)
    lang_table = scatter_about(streams_of[12], (LANGS, D), 1.0, 6.0)
    cross_gain = jnp.clip(1.0 + 0.18 * jax.random.normal(streams_of[13], (D,), jnp.float32), 0.1, 1.9)
    cross_query = scatter_about(streams_of[14], (D, HEADS * HD), D ** -0.5, 0.1875, ((1, 16),))
    cross_key = scatter_about(streams_of[15], (D, HEADS * HD), D ** -0.5, 0.1875, ((1, 16),))
    cross_value = scatter_about(streams_of[16], (D, HEADS * HD), D ** -0.5, 0.1875, ((1, 16),))
    cross_output = scatter_about(streams_of[17], (HEADS * HD, D), (HEADS * HD) ** -0.5, 0.0625, ((0, 16),))
    ffn_gain = jnp.clip(1.0 + 0.18 * jax.random.normal(streams_of[18], (D,), jnp.float32), 0.1, 1.9)
    ffn_in = scatter_about(streams_of[19], (D, FF), D ** -0.5, 0.1875, ((1, 16),))
    ffn_out = scatter_about(streams_of[20], (FF, D), FF ** -0.5, 0.03125, ((0, 16),))
    return dict(enc_tokens=enc_tokens, src_lengths=src_lengths, enc_gain=enc_gain, enc_query=enc_query, enc_key=enc_key, enc_value=enc_value, enc_output=enc_output, enc_bias=enc_bias, mem_gain=mem_gain, dec_tokens=dec_tokens, tgt_lengths=tgt_lengths, lang_tags=lang_tags, lang_table=lang_table, cross_gain=cross_gain, cross_query=cross_query, cross_key=cross_key, cross_value=cross_value, cross_output=cross_output, ffn_gain=ffn_gain, ffn_in=ffn_in, ffn_out=ffn_out)


EPSILON = 1e-06
NEG_FILL = -1e+30

def rms_norm(values, norm_gain):
    mean_sq = lax.optimization_barrier(jnp.mean(values * values, axis=-1, keepdims=True))
    return values * lax.rsqrt(mean_sq + EPSILON) * norm_gain

def make_grid(bias_table, query_len, key_len):
    offset = jnp.arange(key_len)[None, :] - jnp.arange(query_len)[:, None]
    bucket = (jnp.clip(offset, -MAXREL, MAXREL) + MAXREL).reshape(1, query_len * key_len)
    onehot = (bucket == jnp.arange(NB)[:, None]).astype(jnp.float32)
    flat_grid = jnp.dot(bias_table, onehot, precision=lax.Precision.HIGHEST, preferred_element_type=jnp.float32)
    return flat_grid.reshape(bias_table.shape[0], query_len, key_len)

def project(rows, weight):
    return jnp.dot(rows, weight, preferred_element_type=jnp.float32).astype(jnp.bfloat16)

def attend_all(query_flat, key_flat, value_flat, bias_table, lengths, query_len, key_len):
    examples = lengths.shape[0]
    query_heads = query_flat.reshape(examples, query_len, HEADS, HD)
    key_heads = key_flat.reshape(examples, key_len, HEADS, HD)
    value_heads = value_flat.reshape(examples, key_len, HEADS, HD)
    if bias_table is None:
        bias_grid = jnp.zeros((HEADS, query_len, key_len), jnp.float32)
    else:
        bias_grid = make_grid(bias_table, query_len, key_len)

    def one_example(example_item):
        query_part, key_part, value_part, length = example_item
        scores = jnp.einsum('qhd,khd->hqk', query_part.astype(jnp.float32), key_part.astype(jnp.float32), precision=lax.Precision.HIGHEST)
        scores = scores * HD ** (-0.5) + bias_grid
        key_valid = jnp.arange(key_len) < length
        scores = jnp.where(key_valid[None, None, :], scores, NEG_FILL)
        row_max = lax.optimization_barrier(jnp.max(scores, axis=-1, keepdims=True))
        exponent = jnp.exp(scores - row_max)
        weights = (exponent / lax.optimization_barrier(jnp.sum(exponent, axis=-1, keepdims=True))).astype(jnp.bfloat16)
        context = jnp.einsum('hqk,khd->qhd', weights.astype(jnp.float32), value_part.astype(jnp.float32), precision=lax.Precision.HIGHEST)
        return context.astype(jnp.bfloat16)
    contexts = lax.map(one_example, (query_heads, key_heads, value_heads, lengths))
    return contexts.reshape(examples * query_len, HEADS * HD)

def group_sum(context, weight):
    group_width = context.shape[1] // N_TENSOR

    def add_group(running, group_index):
        first_row = (group_index * group_width).astype(jnp.int32)
        context_part = lax.dynamic_slice_in_dim(context, first_row, group_width, 1)
        rows_part = lax.dynamic_slice_in_dim(weight, first_row, group_width, 0)
        partial_value = jnp.dot(context_part, rows_part, preferred_element_type=jnp.float32).astype(jnp.bfloat16)
        partial_value = lax.optimization_barrier(partial_value)
        return (running + partial_value.astype(jnp.float32), None)
    start_value = jnp.zeros((context.shape[0], weight.shape[1]), jnp.float32)
    summed, _ = lax.scan(add_group, start_value, jnp.arange(N_TENSOR, dtype=jnp.int32))
    return summed

def ffn_sum(normed, weight_in, weight_out):
    group_width = weight_in.shape[1] // N_TENSOR

    def add_group(running, group_index):
        first_row = (group_index * group_width).astype(jnp.int32)
        in_cols = lax.dynamic_slice_in_dim(weight_in, first_row, group_width, 1)
        activated = jnp.maximum(jnp.dot(normed, in_cols, preferred_element_type=jnp.float32), 0.0).astype(jnp.bfloat16)
        out_rows = lax.dynamic_slice_in_dim(weight_out, first_row, group_width, 0)
        partial_value = jnp.dot(activated, out_rows, preferred_element_type=jnp.float32).astype(jnp.bfloat16)
        partial_value = lax.optimization_barrier(partial_value)
        return (running + partial_value.astype(jnp.float32), None)
    start_value = jnp.zeros((normed.shape[0], weight_out.shape[1]), jnp.float32)
    summed, _ = lax.scan(add_group, start_value, jnp.arange(N_TENSOR, dtype=jnp.int32))
    return summed

def restripe(values):
    shaped = values.reshape((N_DP, PER_PAIR, N_DP) + values.shape[1:])
    axes_order = (2, 0, 1) + tuple(range(3, shaped.ndim))
    return jnp.transpose(shaped, axes_order).reshape(values.shape)

def reference(enc_tokens, src_lengths, enc_gain, enc_query, enc_key, enc_value, enc_output, enc_bias, mem_gain, dec_tokens, tgt_lengths, lang_tags, lang_table, cross_gain, cross_query, cross_key, cross_value, cross_output, ffn_gain, ffn_in, ffn_out):
    examples = enc_tokens.shape[0]
    enc_input = enc_tokens.astype(jnp.float32).reshape(examples * SRC, D)
    enc_normed = rms_norm(enc_input, enc_gain).astype(jnp.bfloat16)
    enc_context = attend_all(project(enc_normed, enc_query), project(enc_normed, enc_key), project(enc_normed, enc_value), enc_bias, src_lengths, SRC, SRC)
    enc_hidden = enc_input + group_sum(enc_context, enc_output)
    enc_memory = rms_norm(enc_hidden, mem_gain).astype(jnp.bfloat16)
    dec_memory = restripe(enc_memory.reshape(examples, SRC, D)).reshape(examples * SRC, D)
    dec_src_len = restripe(src_lengths)
    lang_rows = lang_table[lang_tags].astype(jnp.float32)
    dec_input = (dec_tokens.astype(jnp.float32) + lang_rows[:, None, :]).reshape(examples * TGT, D)
    dec_normed = rms_norm(dec_input, cross_gain).astype(jnp.bfloat16)
    cross_context = attend_all(project(dec_normed, cross_query), project(dec_memory, cross_key), project(dec_memory, cross_value), None, dec_src_len, TGT, SRC)
    hidden_state = dec_input + group_sum(cross_context, cross_output)
    ffn_normed = rms_norm(hidden_state, ffn_gain).astype(jnp.bfloat16)
    dec_full = hidden_state + ffn_sum(ffn_normed, ffn_in, ffn_out)
    keep = jnp.arange(TGT)[None, :] < tgt_lengths[:, None]
    dec_out = jnp.where(keep[:, :, None], dec_full.reshape(examples, TGT, D), 0.0).astype(jnp.bfloat16)
    return (enc_memory.reshape(examples, SRC, D), dec_out)
```

```python
import functools

import jax
import jax.numpy as jnp
from jax import lax
from jax.experimental import pallas as pl
from jax.experimental.pallas import tpu as pltpu
from jax.sharding import PartitionSpec as P

D = 1024
HD = 128
SRC = 128
TGT = 64
MAXREL = 16
NB = 33
LANGS = 8
HEADS = 4
HW = HEADS * HD
FF = 2048
EPSILON = 1e-06
NEG_FILL = -1e30
SCALE = HD ** (-0.5)
MESH = pl.DeviceIdType.MESH
F32 = jnp.float32
BF16 = jnp.bfloat16

ORDER = ((0, 0), (0, 1), (0, 3), (1, 0), (0, 2), (1, 1), (1, 3), (1, 2))
DY_BITS = sum(dy << i for i, (dy, dz) in enumerate(ORDER))
DZ_BITS = sum(dz << (2 * i) for i, (dy, dz) in enumerate(ORDER))


def rms(values, gain):
    mean_sq = jnp.mean(values * values, axis=-1, keepdims=True)
    return values * lax.rsqrt(mean_sq + EPSILON) * gain


class Place:
    def __init__(self):
        self.me = lax.axis_index("tensor")
        self.dp = lax.axis_index("dp")
        self.core = self.me % 2
        self.z = (self.me // 2) % 4
        self.y = self.me // 8

    def chip(self, dy, dz):
        return ((self.y + dy) % 2) * 4 + (self.z + dz) % 4

    def slot(self, dy, dz, dk=0):
        return self.chip(dy, dz) * 2 + (self.core + dk) % 2

    def near(self):
        return (self.slot(0, 0, 1), self.slot(0, 1), self.slot(0, 3), self.slot(1, 0))


def send(src, dst, send_sem, recv_sem, device):
    pltpu.make_async_remote_copy(
        src_ref=src,
        dst_ref=dst,
        send_sem=send_sem,
        recv_sem=recv_sem,
        device_id=device,
        device_id_type=MESH,
    ).start()


def arrived(dst, recv_sem):
    pltpu.make_async_copy(dst, dst, recv_sem).wait()


class Gather:
    def __init__(self, place, buf, ssem, rsem, hsem):
        self.p, self.buf = place, buf
        self.ssem, self.rsem, self.hsem = ssem, rsem, hsem
        self.half = buf.shape[1] // 2
        self.sent = []

    def _send(self, src, recv_sem, target):
        sem = self.ssem.at[len(self.sent)]
        send(src, src, sem, recv_sem, {"tensor": target})
        self.sent.append(src.shape[0])

    def _full(self, slot, target):
        self._send(self.buf.at[slot], self.rsem.at[slot], target)

    def _half(self, slot, dy, which, target):
        part = self.buf.at[slot, pl.ds(which * self.half, self.half)]
        self._send(part, self.hsem.at[dy, which], target)

    def start(self):
        p = self.p
        for target in (p.slot(0, 1), p.slot(0, 3), p.slot(1, 0), p.slot(0, 0, 1)):
            self._full(p.me, target)

    def event(self, index):
        p = self.p
        dy, dz = ORDER[index]
        slot = p.slot(dy, dz)
        partner = p.slot(0, 0, 1)
        if dz == 2:
            for which in (0, 1):
                arrived(
                    self.buf.at[slot, pl.ds(which * self.half, self.half)], self.hsem.at[dy, which]
                )
        else:
            arrived(self.buf.at[slot], self.rsem.at[slot])
        if dz == 1:
            self._half(slot, dy, 1, p.slot(0, 3))
        elif dz == 3:
            self._half(slot, dy, 0, p.slot(0, 1))
        elif dz == 0:
            self._full(slot, p.slot(0, 1))
            self._full(slot, p.slot(0, 3))
        self._full(slot, partner)

    def partner_wait(self, chip):
        slot = chip * 2 + (self.p.core + 1) % 2
        arrived(self.buf.at[slot], self.rsem.at[slot])

    def drain(self):
        for index, rows in enumerate(self.sent):
            arrived(self.buf.at[0, pl.ds(0, rows)], self.ssem.at[index])


GATHER_SENDS = 17


def order_chip(place, index):
    dy = (DY_BITS >> index) & 1
    dz = (DZ_BITS >> (2 * index)) & 3
    return place.chip(dy, dz)


def scatter_chip(place, index):
    return place.chip(1 - index // 4, (2 - index % 4) % 4)


class Scatter:
    def __init__(self, place, part, xbuf, relay, fin, yrec, ysend, psem, xsem, ssem, zsem, fsem, ysem):
        self.p, self.part, self.xbuf, self.relay = place, part, xbuf, relay
        self.fin, self.yrec, self.ysend = fin, yrec, ysend
        self.psem, self.xsem, self.ssem = psem, xsem, ssem
        self.zsem, self.fsem, self.ysem = zsem, fsem, ysem
        self.half = part.shape[1] // 2
        self.sent = []

    def partner_send(self, chip):
        slot = chip * 2 + (self.p.core + 1) % 2
        send(
            self.part.at[slot],
            self.xbuf.at[chip],
            self.psem.at[chip],
            self.xsem.at[chip],
            {"tensor": self.p.slot(0, 0, 1)},
        )

    def partner_add(self, chip):
        arrived(self.xbuf.at[chip], self.xsem.at[chip])
        slot = chip * 2 + self.p.core
        self.part[slot] = self.part[slot] + self.xbuf[chip]

    def _send(self, src, dst, recv_sem, target):
        sem = self.ssem.at[len(self.sent)]
        send(src, dst, sem, recv_sem, {"tensor": target})
        self.sent.append(src.shape[0])

    def _rows(self, which):
        return pl.ds(which * self.half, self.half)

    def far(self, dy):
        p = self.p
        slot = p.slot(dy, 2)
        for which, dz in ((0, 1), (1, 3)):
            self._send(
                self.part.at[slot, self._rows(which)],
                self.relay.at[dy, which],
                self.zsem.at[dy, which],
                p.slot(0, dz),
            )

    def near_half(self, dy, way, which):
        p = self.p
        dz = (1, 3)[way]
        rows = self._rows(which)
        self._send(
            self.part.at[p.slot(dy, dz), rows],
            self.fin.at[dy, way, rows],
            self.fsem.at[dy, way, which],
            p.slot(0, dz),
        )

    def relay_add(self, dy, way):
        p = self.p
        arrived(self.relay.at[dy, way], self.zsem.at[dy, way])
        slot, rows = p.slot(dy, (1, 3)[way]), self._rows(way)
        self.part[slot, rows, :] = self.part[slot, rows, :] + self.relay[dy, way]

    def ring_sum(self, dy):
        for way in (0, 1):
            for which in (0, 1):
                arrived(self.fin.at[dy, way, self._rows(which)], self.fsem.at[dy, way, which])
        slot = self.p.slot(dy, 0)
        return (
            self.part[slot].astype(F32) + self.fin[dy, 0].astype(F32) + self.fin[dy, 1].astype(F32)
        )

    def finish(self):
        p = self.p
        for dy in (1, 0):
            self.far(dy)
            self.near_half(dy, 0, 1)
            self.near_half(dy, 1, 0)
        for dy in (1, 0):
            for way in (0, 1):
                self.relay_add(dy, way)
            for way in (0, 1):
                self.near_half(dy, way, way)
        self.ysend[...] = self.ring_sum(1).astype(BF16)
        own = self.ring_sum(0)
        self._send(self.ysend, self.yrec, self.ysem, p.slot(1, 0))
        arrived(self.yrec, self.ysem)
        return own + self.yrec[...].astype(F32)

    def drain(self):
        for chip in range(8):
            slot = chip * 2 + (self.p.core + 1) % 2
            arrived(self.part.at[slot], self.psem.at[chip])
        for index, rows in enumerate(self.sent):
            arrived(self.part.at[0, pl.ds(0, rows)], self.ssem.at[index])


def gather_scratch(rows):
    return [
        pltpu.VMEM((16, rows, D), BF16),
        pltpu.SemaphoreType.DMA((GATHER_SENDS,)),
        pltpu.SemaphoreType.DMA((16,)),
        pltpu.SemaphoreType.DMA((2, 2)),
    ]


def scatter_scratch(rows):
    return [
        pltpu.VMEM((16, rows, D), BF16),
        pltpu.VMEM((8, rows, D), BF16),
        pltpu.VMEM((2, 2, rows // 2, D), BF16),
        pltpu.VMEM((2, 2, rows, D), BF16),
        pltpu.VMEM((rows, D), BF16),
        pltpu.VMEM((rows, D), BF16),
        pltpu.SemaphoreType.DMA((8,)),
        pltpu.SemaphoreType.DMA((8,)),
        pltpu.SemaphoreType.DMA((13,)),
        pltpu.SemaphoreType.DMA((2, 2)),
        pltpu.SemaphoreType.DMA((2, 2, 2)),
        pltpu.SemaphoreType.DMA,
    ]


GATHER_N = 4
SCATTER_N = 12


def greet(devices):
    barrier = pltpu.get_barrier_semaphore()
    for device in devices:
        pl.semaphore_signal(barrier, inc=1, device_id=device, device_id_type=MESH)
    return barrier


def dot(left, right):
    return jnp.dot(left, right, preferred_element_type=F32)


def softmax_weights(scores):
    row_max = jnp.max(scores, axis=-1, keepdims=True)
    exponent = jnp.exp(scores - row_max)
    return (exponent * (1.0 / jnp.sum(exponent, axis=-1, keepdims=True))).astype(BF16)


def dot_t(left, right):
    return lax.dot_general(left, right, (((1,), (1,)), ((), ())), preferred_element_type=F32)


def enc_kernel(
    tokens, lengths, gain, wq_h, wk_h, wv_h, wo_h, bias, mem_gain, out, wq, wk, wv, wo, grid, ctx, wsem, *rest
):
    place = Place()
    gather = Gather(place, *rest[:GATHER_N])
    scatter = Scatter(place, *rest[GATHER_N:])
    buf, part = rest[0], rest[GATHER_N]
    loads = [
        pltpu.make_async_copy(src, dst, wsem.at[i])
        for i, (src, dst) in enumerate(((wq_h, wq), (wk_h, wk), (wv_h, wv), (wo_h, wo)))
    ]
    buf[place.me] = rms(tokens[0].astype(F32), gain[...]).astype(BF16)
    barrier = greet([{"tensor": t} for t in place.near()])
    for load in loads:
        load.start()
    pl.semaphore_wait(barrier, 4)
    gather.start()

    keys = lax.broadcasted_iota(jnp.int32, (SRC, SRC), 1)
    bucket = jnp.clip(keys - lax.broadcasted_iota(jnp.int32, (SRC, SRC), 0), -MAXREL, MAXREL) + MAXREL
    for head in range(HEADS):
        values = jnp.zeros((SRC, SRC), F32)
        for index in range(NB):
            values = jnp.where(bucket == index, bias[head, index], values)
        grid[head] = values
    for load in loads:
        load.wait()

    def step(index, carry):
        @pl.when(index == 1)
        def _():
            for event in (1, 2, 3):
                gather.event(event)

        @pl.when(index == 4)
        def _():
            for event in (4, 5, 6):
                gather.event(event)

        @pl.when(index == 7)
        def _():
            gather.event(7)

        chip = order_chip(place, index)
        gather.partner_wait(chip)
        rows = buf[pl.ds(chip * 2, 2)].reshape(2 * SRC, D)
        columns = lax.broadcasted_iota(jnp.int32, (SRC, SRC), 1)
        for pair in range(HEADS // 2):
            wide = slice(pair * 2 * HD, (pair + 1) * 2 * HD)
            q = dot(rows, wq[:, wide]).astype(BF16)
            k = dot(rows, wk[:, wide]).astype(BF16)
            v = dot(rows, wv[:, wide]).astype(BF16)
            for ex in range(2):
                length = lengths[place.dp * 16 + chip * 2 + ex]
                here = slice(ex * SRC, (ex + 1) * SRC)
                for head in range(2):
                    cols = slice(head * HD, (head + 1) * HD)
                    full = pair * 2 + head
                    scores = dot_t(q[here, cols], k[here, cols]) * SCALE + grid[full]
                    weights = softmax_weights(jnp.where(columns < length, scores, NEG_FILL))
                    ctx[chip * 2 + ex, :, full * HD : (full + 1) * HD] = dot(
                        weights, v[here, cols]
                    ).astype(BF16)
        return carry

    lax.fori_loop(0, 8, step, 0)

    def out_step(index, carry):
        @pl.when(index > 0)
        def _():
            scatter.partner_send(scatter_chip(place, index - 1))

        chip = scatter_chip(place, index)
        rows = ctx[pl.ds(chip * 2, 2)].reshape(2 * SRC, HW)
        part[pl.ds(chip * 2, 2)] = dot(rows, wo[...]).astype(BF16).reshape(2, SRC, D)
        return carry

    lax.fori_loop(0, 8, out_step, 0)
    scatter.partner_send(scatter_chip(place, 7))
    for index in range(8):
        scatter.partner_add(scatter_chip(place, index))
    total = tokens[0].astype(F32) + scatter.finish()
    out[0] = rms(total, mem_gain[...]).astype(BF16)
    gather.drain()
    scatter.drain()


def cross_kernel(
    memory,
    tokens,
    lengths,
    tags,
    table,
    gain,
    wq_h,
    wk_h,
    wv_h,
    wo_h,
    out,
    wq,
    wk,
    wv,
    wo,
    inp,
    q_all,
    ctx,
    wsem,
    swap_s,
    swap_r,
    *rest,
):
    place = Place()
    mem = Gather(place, *rest[:GATHER_N])
    dec = Gather(place, *rest[GATHER_N : 2 * GATHER_N])
    scatter = Scatter(place, *rest[2 * GATHER_N :])
    mem_buf, dec_buf, part = rest[0], rest[GATHER_N], rest[2 * GATHER_N]
    loads = [
        pltpu.make_async_copy(src, dst, wsem.at[i])
        for i, (src, dst) in enumerate(((wq_h, wq), (wk_h, wk), (wv_h, wv), (wo_h, wo)))
    ]
    x, y_lo = place.dp // 2, place.dp % 2
    other_dp = place.z * 2 + place.core
    other_t = place.y * 8 + x * 2 + y_lo
    stays = jnp.logical_and(other_dp == place.dp, other_t == place.me)
    moves = jnp.logical_not(stays)
    barrier = greet([{"tensor": t} for t in place.near()])

    @pl.when(moves)
    def _():
        pl.semaphore_signal(barrier, inc=1, device_id=(other_dp, other_t), device_id_type=MESH)

    tag = tags[place.me]
    lang = jnp.zeros((1, D), F32)
    for index in range(LANGS):
        lang = jnp.where(tag == index, table[index : index + 1, :].astype(F32), lang)
    value = tokens[0].astype(F32) + lang
    inp[...] = value
    dec_buf[place.me] = rms(value, gain[...]).astype(BF16)
    for load in loads:
        load.start()

    @pl.when(moves)
    def _():
        pl.semaphore_wait(barrier, 5)
        send(memory.at[0], mem_buf.at[other_t], swap_s, swap_r, (other_dp, other_t))

    @pl.when(stays)
    def _():
        pl.semaphore_wait(barrier, 4)
        pltpu.make_async_copy(memory.at[0], mem_buf.at[place.me], swap_r).start()

    dec.start()
    for event in range(1, 8):
        dec.event(event)
    for chip in range(8):
        dec.partner_wait(chip)
    arrived(mem_buf.at[place.me], swap_r)
    mem.start()
    for load in loads:
        load.wait()

    def q_step(index, carry):
        rows = dec_buf[pl.ds(index * 4, 4)].reshape(4 * TGT, D)
        q_all[pl.ds(index * 4, 4)] = dot(rows, wq[...]).astype(BF16).reshape(4, TGT, HW)
        return carry

    lax.fori_loop(0, 4, q_step, 0)

    def step(index, carry):
        @pl.when(index == 1)
        def _():
            for event in (1, 2, 3):
                mem.event(event)

        @pl.when(index == 4)
        def _():
            for event in (4, 5, 6):
                mem.event(event)

        @pl.when(index == 7)
        def _():
            mem.event(7)

        chip = order_chip(place, index)
        mem.partner_wait(chip)
        rows = mem_buf[pl.ds(chip * 2, 2)].reshape(2 * SRC, D)
        columns = lax.broadcasted_iota(jnp.int32, (TGT, SRC), 1)
        for pair in range(HEADS // 2):
            wide = slice(pair * 2 * HD, (pair + 1) * 2 * HD)
            k = dot(rows, wk[:, wide]).astype(BF16)
            v = dot(rows, wv[:, wide]).astype(BF16)
            for ex in range(2):
                row = (chip % 4) * 4 + ex * 2 + chip // 4
                length = lengths[(row // 2) * 16 + (row % 2) * 8 + place.dp]
                here = slice(ex * SRC, (ex + 1) * SRC)
                for head in range(2):
                    cols = slice(head * HD, (head + 1) * HD)
                    full = slice((pair * 2 + head) * HD, (pair * 2 + head + 1) * HD)
                    scores = dot_t(q_all[row, :, full], k[here, cols]) * SCALE
                    weights = softmax_weights(jnp.where(columns < length, scores, NEG_FILL))
                    ctx[row, :, full] = dot(weights, v[here, cols]).astype(BF16)
        return carry

    lax.fori_loop(0, 8, step, 0)

    def out_step(index, carry):
        @pl.when(index > 0)
        def _():
            scatter.partner_send(scatter_chip(place, index - 1))

        chip = scatter_chip(place, index)
        rows = ctx[pl.ds(chip * 2, 2)].reshape(2 * TGT, HW)
        part[pl.ds(chip * 2, 2)] = dot(rows, wo[...]).astype(BF16).reshape(2, TGT, D)
        return carry

    lax.fori_loop(0, 8, out_step, 0)
    scatter.partner_send(scatter_chip(place, 7))
    for index in range(8):
        scatter.partner_add(scatter_chip(place, index))
    out[...] = inp[...] + scatter.finish()

    @pl.when(moves)
    def _():
        pltpu.make_async_copy(memory.at[0], memory.at[0], swap_s).wait()

    mem.drain()
    dec.drain()
    scatter.drain()


def ffn_kernel(hidden, gain, tgt_length, win_h, wout_h, out, win, wout, act, wsem, *rest):
    place = Place()
    gather = Gather(place, *rest[:GATHER_N])
    scatter = Scatter(place, *rest[GATHER_N:])
    buf, part = rest[0], rest[GATHER_N]
    loads = [
        pltpu.make_async_copy(win_h, win, wsem.at[0]),
        pltpu.make_async_copy(wout_h, wout, wsem.at[1]),
    ]
    barrier = greet([{"tensor": t} for t in place.near()])
    for load in loads:
        load.start()
    buf[place.me] = rms(hidden[...], gain[...]).astype(BF16)
    pl.semaphore_wait(barrier, 4)
    gather.start()
    for load in loads:
        load.wait()

    def step(index, carry):
        for pair in range(4):

            @pl.when(index == pair)
            def _():
                for event in (2 * pair, 2 * pair + 1):
                    if event > 0:
                        gather.event(event)

        first, second = order_chip(place, index * 2), order_chip(place, index * 2 + 1)
        gather.partner_wait(first)
        gather.partner_wait(second)
        rows = jnp.concatenate(
            [
                buf[pl.ds(first * 2, 2)].reshape(2 * TGT, D),
                buf[pl.ds(second * 2, 2)].reshape(2 * TGT, D),
            ],
            axis=0,
        )
        for tile in range(FF // 512):
            cols = slice(tile * 512, (tile + 1) * 512)
            act[:, cols] = jnp.maximum(dot(rows, win[:, cols]), 0.0).astype(BF16)
        for tile in range(D // 256):
            cols = slice(tile * 256, (tile + 1) * 256)
            result = dot(act[...], wout[:, cols]).astype(BF16)
            part[pl.ds(first * 2, 2), :, cols] = result[: 2 * TGT].reshape(2, TGT, 256)
            part[pl.ds(second * 2, 2), :, cols] = result[2 * TGT :].reshape(2, TGT, 256)

        @pl.when(index > 0)
        def _():
            scatter.partner_send(order_chip(place, index * 2 - 2))
            scatter.partner_send(order_chip(place, index * 2 - 1))

        return carry

    lax.fori_loop(0, 4, step, 0)
    scatter.partner_send(order_chip(place, 6))
    scatter.partner_send(order_chip(place, 7))
    for index in range(8):
        scatter.partner_add(scatter_chip(place, index))
    total = hidden[...] + scatter.finish()
    keep = lax.broadcasted_iota(jnp.int32, (TGT, D), 0) < tgt_length[0]
    out[0] = jnp.where(keep, total, 0.0).astype(BF16)
    gather.drain()
    scatter.drain()


VM = pltpu.VMEM
SM = pltpu.SMEM


def call(kernel, ident, out_shape, spaces, scratch, flops, *operands):
    return pl.pallas_call(
        kernel,
        out_shape=out_shape,
        in_specs=[pl.BlockSpec(memory_space=space) for space in spaces],
        out_specs=pl.BlockSpec(memory_space=VM),
        scratch_shapes=scratch,
        compiler_params=pltpu.CompilerParams(
            collective_id=ident, has_side_effects=True, vmem_limit_bytes=58 * 2**20
        ),
        cost_estimate=pl.CostEstimate(flops=flops, bytes_accessed=8 * 2**20, transcendentals=0),
    )(*operands)


def on_device(
    enc_tokens,
    src_lengths,
    enc_gain,
    enc_query,
    enc_key,
    enc_value,
    enc_output,
    enc_bias,
    mem_gain,
    dec_tokens,
    tgt_lengths,
    lang_tags,
    lang_table,
    cross_gain,
    cross_query,
    cross_key,
    cross_value,
    cross_output,
    ffn_gain,
    ffn_in,
    ffn_out,
):
    weights = [
        pltpu.VMEM((D, HW), BF16),
        pltpu.VMEM((D, HW), BF16),
        pltpu.VMEM((D, HW), BF16),
        pltpu.VMEM((HW, D), BF16),
    ]
    enc_memory = call(
        enc_kernel,
        1,
        jax.ShapeDtypeStruct((1, SRC, D), BF16),
        (VM, SM, VM, pl.ANY, pl.ANY, pl.ANY, pl.ANY, SM, VM),
        weights
        + [
            pltpu.VMEM((HEADS, SRC, SRC), F32),
            pltpu.VMEM((16, SRC, HW), BF16),
            pltpu.SemaphoreType.DMA((4,)),
        ]
        + gather_scratch(SRC)
        + scatter_scratch(SRC),
        9 * 10**9,
        enc_tokens,
        src_lengths,
        enc_gain,
        enc_query,
        enc_key,
        enc_value,
        enc_output,
        enc_bias,
        mem_gain,
    )
    hidden = call(
        cross_kernel,
        2,
        jax.ShapeDtypeStruct((TGT, D), F32),
        (VM, VM, SM, SM, VM, VM, pl.ANY, pl.ANY, pl.ANY, pl.ANY),
        weights
        + [
            pltpu.VMEM((TGT, D), F32),
            pltpu.VMEM((16, TGT, HW), BF16),
            pltpu.VMEM((16, TGT, HW), BF16),
            pltpu.SemaphoreType.DMA((4,)),
            pltpu.SemaphoreType.DMA,
            pltpu.SemaphoreType.DMA,
        ]
        + gather_scratch(SRC)
        + gather_scratch(TGT)
        + scatter_scratch(TGT),
        7 * 10**9,
        enc_memory,
        dec_tokens,
        src_lengths,
        lang_tags,
        lang_table,
        cross_gain,
        cross_query,
        cross_key,
        cross_value,
        cross_output,
    )
    dec_out = call(
        ffn_kernel,
        3,
        jax.ShapeDtypeStruct((1, TGT, D), BF16),
        (VM, VM, SM, pl.ANY, pl.ANY),
        [
            pltpu.VMEM((D, FF), BF16),
            pltpu.VMEM((FF, D), BF16),
            pltpu.VMEM((4 * TGT, FF), BF16),
            pltpu.SemaphoreType.DMA((2,)),
        ]
        + gather_scratch(TGT)
        + scatter_scratch(TGT),
        9 * 10**9,
        hidden,
        ffn_gain,
        tgt_lengths,
        ffn_in,
        ffn_out,
    )
    return (enc_memory, dec_out)


def solution(mesh):
    in_specs = (
        P(("dp", "tensor"), None, None),
        P(),
        P(),
        P(None, "tensor"),
        P(None, "tensor"),
        P(None, "tensor"),
        P("tensor", None),
        P("tensor", None),
        P(),
        P(("dp", "tensor"), None, None),
        P(("dp", "tensor")),
        P("dp"),
        P(),
        P(),
        P(None, "tensor"),
        P(None, "tensor"),
        P(None, "tensor"),
        P("tensor", None),
        P(),
        P(None, "tensor"),
        P("tensor", None),
    )
    out_specs = (P(("dp", "tensor"), None, None), P(("dp", "tensor"), None, None))
    return jax.shard_map(
        on_device, mesh=mesh, in_specs=in_specs, out_specs=out_specs, check_vma=False
    )
```

```python
import functools

import jax
import jax.numpy as jnp
from jax import lax
from jax.experimental import pallas as pl
from jax.experimental.pallas import tpu as pltpu
from jax.sharding import PartitionSpec as P

D = 1024
HD = 128
SRC = 128
TGT = 64
MAXREL = 16
NB = 33
LANGS = 8
HEADS = 4
HW = HEADS * HD
FF = 2048
EPSILON = 1e-06
NEG_FILL = -1e30
SCALE = HD ** (-0.5)
MESH = pl.DeviceIdType.MESH
F32 = jnp.float32
BF16 = jnp.bfloat16

GATHER_ORDER = ((0, 0), (0, 1), (0, 3), (1, 0), (0, 2), (1, 1), (1, 3), (1, 2))
SCATTER_ORDER = ((1, 2), (1, 1), (1, 3), (0, 2), (0, 1), (0, 3), (1, 0), (0, 0))
ENC_CHUNKS = 4
MEM_CHUNKS = 2
DEC_CHUNKS = 2


def packed(order):
    return (
        sum(dy << i for i, (dy, dz) in enumerate(order)),
        sum(dz << (2 * i) for i, (dy, dz) in enumerate(order)),
    )


def chip_at(place, order, index):
    dy_bits, dz_bits = packed(order)
    return place.chip((dy_bits >> index) & 1, (dz_bits >> (2 * index)) & 3)


def rms(values, gain):
    mean_sq = jnp.mean(values * values, axis=-1, keepdims=True)
    return values * lax.rsqrt(mean_sq + EPSILON) * gain


class Place:
    def __init__(self):
        self.me = lax.axis_index("tensor")
        self.dp = lax.axis_index("dp")
        self.core = self.me % 2
        self.z = (self.me // 2) % 4
        self.y = self.me // 8
        self.x = self.dp // 2
        self.y_lo = self.dp % 2

    def chip(self, dy, dz):
        return ((self.y + dy) % 2) * 4 + (self.z + dz) % 4

    def slot(self, dy, dz, dk=0):
        return self.chip(dy, dz) * 2 + (self.core + dk) % 2


def send(src, dst, send_sem, recv_sem, device):
    pltpu.make_async_remote_copy(
        src_ref=src,
        dst_ref=dst,
        send_sem=send_sem,
        recv_sem=recv_sem,
        device_id=device,
        device_id_type=MESH,
    ).start()


def arrived(dst, recv_sem):
    pltpu.make_async_copy(dst, dst, recv_sem).wait()


class Gather:
    SENDS = 16

    def __init__(self, place, buf, ssem, rsem, hsem, chunk, chunks):
        self.p, self.buf, self.chunk = place, buf, chunk
        self.ssem, self.rsem, self.hsem = ssem, rsem, hsem
        self.rows = buf.shape[1] // chunks
        self.first = chunk * self.rows
        self.sent = []

    def _part(self, slot):
        return self.buf.at[slot, pl.ds(self.first, self.rows)]

    def _half_part(self, slot, which):
        half = self.rows // 2
        return self.buf.at[slot, pl.ds(self.first + which * half, half)]

    def _send(self, src, recv_sem, target):
        sem = self.ssem.at[self.chunk, len(self.sent)]
        send(src, src, sem, recv_sem, {"tensor": target})
        self.sent.append(src.shape[0])

    def _full(self, slot, target):
        self._send(self._part(slot), self.rsem.at[self.chunk, slot], target)

    def _half(self, slot, which, target):
        self._send(self._half_part(slot, which), self.hsem.at[self.chunk, which], target)

    def start(self):
        p = self.p
        for target in (p.slot(0, 1), p.slot(0, 3), p.slot(1, 0), p.slot(0, 0, 1)):
            self._full(p.me, target)

    def event(self, index):
        p = self.p
        dy, dz = GATHER_ORDER[index]
        slot = p.slot(dy, dz)
        if (dy, dz) == (0, 2):
            for which in (0, 1):
                arrived(self._half_part(slot, which), self.hsem.at[self.chunk, which])
            self._full(slot, p.slot(1, 0))
        else:
            arrived(self._part(slot), self.rsem.at[self.chunk, slot])
        if (dy, dz) == (0, 1):
            self._half(slot, 1, p.slot(0, 3))
        elif (dy, dz) == (0, 3):
            self._half(slot, 0, p.slot(0, 1))
        elif (dy, dz) == (1, 0):
            self._full(slot, p.slot(0, 1))
            self._full(slot, p.slot(0, 3))
        self._full(slot, p.slot(0, 0, 1))

    def partner_wait(self, chip):
        slot = chip * 2 + (self.p.core + 1) % 2
        arrived(self._part(slot), self.rsem.at[self.chunk, slot])

    def drain(self):
        for index, rows in enumerate(self.sent):
            arrived(self.buf.at[0, pl.ds(0, rows)], self.ssem.at[self.chunk, index])

    @staticmethod
    def scratch(rows, chunks):
        return [
            pltpu.VMEM((16, rows, D), BF16),
            pltpu.SemaphoreType.DMA((chunks, Gather.SENDS)),
            pltpu.SemaphoreType.DMA((chunks, 16)),
            pltpu.SemaphoreType.DMA((chunks, 2)),
        ]

    @staticmethod
    def make(place, refs, chunks):
        return [Gather(place, *refs, chunk, chunks) for chunk in range(chunks)]


class Scatter:
    SENDS = 10

    def __init__(self, place, chunks, part, xbuf, yfar, relay, fin, finy, ysend, yrec, *sems):
        self.p, self.chunks = place, chunks
        self.part, self.xbuf, self.yfar, self.relay = part, xbuf, yfar, relay
        self.fin, self.finy, self.ysend, self.yrec = fin, finy, ysend, yrec
        self.psem, self.xsem, self.ssem = sems[:3]
        self.yfar_sem, self.relay_sem, self.fin_sem, self.finy_sem, self.yrec_sem = sems[3:]
        self.rows = part.shape[1] // chunks
        self.half = self.rows // 2
        self.sent = []

    @staticmethod
    def scratch(rows, chunks):
        return [
            pltpu.VMEM((16, rows, D), BF16),
            pltpu.VMEM((8, rows, D), BF16),
            pltpu.VMEM((rows, D), BF16),
            pltpu.VMEM((2, rows // 2, D), BF16),
            pltpu.VMEM((2, rows, D), BF16),
            pltpu.VMEM((2, rows, D), BF16),
            pltpu.VMEM((rows, D), BF16),
            pltpu.VMEM((rows, D), BF16),
            pltpu.SemaphoreType.DMA((8,)),
            pltpu.SemaphoreType.DMA((8,)),
            pltpu.SemaphoreType.DMA((chunks * Scatter.SENDS,)),
            pltpu.SemaphoreType.DMA((chunks,)),
            pltpu.SemaphoreType.DMA((chunks, 2)),
            pltpu.SemaphoreType.DMA((chunks, 2, 2)),
            pltpu.SemaphoreType.DMA((chunks, 2)),
            pltpu.SemaphoreType.DMA((chunks,)),
        ]

    def partner_send(self, chip):
        slot = chip * 2 + (self.p.core + 1) % 2
        send(
            self.part.at[slot],
            self.xbuf.at[chip],
            self.psem.at[chip],
            self.xsem.at[chip],
            {"tensor": self.p.slot(0, 0, 1)},
        )

    def partner_add(self, chip):
        arrived(self.xbuf.at[chip], self.xsem.at[chip])
        slot = chip * 2 + self.p.core
        self.part[slot] = self.part[slot] + self.xbuf[chip]

    def _send(self, src, dst, recv_sem, target):
        sem = self.ssem.at[len(self.sent)]
        send(src, dst, sem, recv_sem, {"tensor": target})
        self.sent.append(src.shape[0])

    def all_rows(self, chunk):
        return pl.ds(chunk * self.rows, self.rows)

    def half_rows(self, chunk, which):
        return pl.ds(chunk * self.rows + which * self.half, self.half)

    def send_yfar(self):
        slot = self.p.slot(1, 2)
        for chunk in range(self.chunks):
            rows = self.all_rows(chunk)
            self._send(
                self.part.at[slot, rows],
                self.yfar.at[rows],
                self.yfar_sem.at[chunk],
                self.p.slot(1, 0),
            )

    def send_side(self, way):
        dz = (1, 3)[way]
        slot = self.p.slot(1, dz)
        for chunk in range(self.chunks):
            rows = self.all_rows(chunk)
            self._send(
                self.part.at[slot, rows],
                self.finy.at[way, rows],
                self.finy_sem.at[chunk, way],
                self.p.slot(0, dz),
            )

    def _near(self, chunk, way, which):
        dz = (1, 3)[way]
        rows = self.half_rows(chunk, which)
        self._send(
            self.part.at[self.p.slot(0, dz), rows],
            self.fin.at[way, rows],
            self.fin_sem.at[chunk, way, which],
            self.p.slot(0, dz),
        )

    def far(self, chunk):
        rows = self.all_rows(chunk)
        slot = self.p.slot(0, 2)
        arrived(self.yfar.at[rows], self.yfar_sem.at[chunk])
        self.part[slot, rows, :] = self.part[slot, rows, :] + self.yfar[rows, :]
        self._near(chunk, 0, 1)
        self._near(chunk, 1, 0)
        for way in (0, 1):
            self._send(
                self.part.at[slot, self.half_rows(chunk, way)],
                self.relay.at[way, pl.ds(chunk * self.half, self.half)],
                self.relay_sem.at[chunk, way],
                self.p.slot(0, (1, 3)[way]),
            )

    def cross_sum(self, chunk):
        rows = self.all_rows(chunk)
        for way in (0, 1):
            arrived(self.finy.at[way, rows], self.finy_sem.at[chunk, way])
        total = self.part[self.p.slot(1, 0), rows, :].astype(F32)
        total = total + self.finy[0, rows, :].astype(F32) + self.finy[1, rows, :].astype(F32)
        self.ysend[rows, :] = total.astype(BF16)

    def cross_send(self, chunk):
        rows = self.all_rows(chunk)
        self._send(
            self.ysend.at[rows], self.yrec.at[rows], self.yrec_sem.at[chunk], self.p.slot(1, 0)
        )

    def relay_add(self, chunk):
        for way in (0, 1):
            here = pl.ds(chunk * self.half, self.half)
            arrived(self.relay.at[way, here], self.relay_sem.at[chunk, way])
            slot, rows = self.p.slot(0, (1, 3)[way]), self.half_rows(chunk, way)
            self.part[slot, rows, :] = self.part[slot, rows, :] + self.relay[way, here, :]

    def relay_send(self, chunk):
        for way in (0, 1):
            self._near(chunk, way, way)

    def total(self, chunk):
        rows = self.all_rows(chunk)
        for way in (0, 1):
            for which in (0, 1):
                arrived(
                    self.fin.at[way, self.half_rows(chunk, which)],
                    self.fin_sem.at[chunk, way, which],
                )
        own = self.part[self.p.me, rows, :].astype(F32)
        own = own + self.fin[0, rows, :].astype(F32) + self.fin[1, rows, :].astype(F32)
        arrived(self.yrec.at[rows], self.yrec_sem.at[chunk])
        return own + self.yrec[rows, :].astype(F32)

    def run(self, *stages):
        steps = (
            self.far,
            self.cross_sum,
            lambda chunk: (self.cross_send(chunk), self.relay_add(chunk)),
            self.relay_send,
        ) + stages
        for time in range(self.chunks + len(steps) - 1):
            for index, stage in enumerate(steps):
                if 0 <= time - index < self.chunks:
                    stage(time - index)

    def drain(self):
        for chip in range(8):
            slot = chip * 2 + (self.p.core + 1) % 2
            arrived(self.part.at[slot], self.psem.at[chip])
        for index, rows in enumerate(self.sent):
            arrived(self.part.at[0, pl.ds(0, rows)], self.ssem.at[index])


def project_out(place, scatter, ctx, weight, also):
    rows = ctx.shape[1]

    def step(index, carry):
        @pl.when(index < 8)
        def _():
            chip = chip_at(place, SCATTER_ORDER, index)
            block = ctx[pl.ds(chip * 2, 2)].reshape(2 * rows, HW)
            scatter.part[pl.ds(chip * 2, 2)] = dot(block, weight[...]).astype(BF16).reshape(2, rows, D)

        @pl.when(jnp.logical_and(index > 0, index < 9))
        def _():
            scatter.partner_send(chip_at(place, SCATTER_ORDER, index - 1))

        @pl.when(index > 1)
        def _():
            scatter.partner_add(chip_at(place, SCATTER_ORDER, index - 2))

        for at, action in also:

            @pl.when(index == at)
            def _(action=action):
                action()

        return carry

    lax.fori_loop(0, 10, step, 0)


def dot(left, right):
    return jnp.dot(left, right, preferred_element_type=F32)


def dot_t(left, right):
    return lax.dot_general(left, right, (((1,), (1,)), ((), ())), preferred_element_type=F32)


def softmax_weights(scores):
    row_max = jnp.max(scores, axis=-1, keepdims=True)
    exponent = jnp.exp(scores - row_max)
    return (exponent * (1.0 / jnp.sum(exponent, axis=-1, keepdims=True))).astype(BF16)


def layer_kernel(*refs):
    refs = list(refs)

    def take(count):
        taken, refs[:count] = refs[:count], []
        return taken

    tokens, lengths, gain, bias, mem_gain = take(5)
    dec_tokens, tags, table, cross_gain, ffn_gain, tgt_length = take(6)
    hbm = take(10)
    memory_out, dec_out = take(2)
    weights = take(10)
    (weight_sem,) = take(1)
    wq, wk, wv, wo, cq, ck, cv, co, win, wout = weights
    grid, q_s, k_s, v_s, s_s, w_s, ctx = take(7)
    hop, hop_sem, swap_sem = take(3)
    inp, q_all, cross_ctx, act, hidden = take(5)
    place = Place()
    enc_refs, mem_refs, dec_refs, ffn_refs = take(4), take(4), take(4), take(4)
    (enc,) = Gather.make(place, enc_refs, 1)
    mem = Gather.make(place, mem_refs, MEM_CHUNKS)
    (dec,) = Gather.make(place, dec_refs, 1)
    ffn = Gather.make(place, ffn_refs, DEC_CHUNKS)
    enc_sum = Scatter(place, ENC_CHUNKS, *take(16))
    cross_sum = Scatter(place, DEC_CHUNKS, *take(16))
    ffn_sum = Scatter(place, DEC_CHUNKS, *take(16))

    loads = [
        pltpu.make_async_copy(src, dst, weight_sem.at[index])
        for index, (src, dst) in enumerate(zip(hbm, weights))
    ]
    shifted_to = place.slot(0, place.x)
    swap_dp = ((place.z + 4 - place.x) % 4) * 2 + place.core
    swap_t = place.y * 8 + place.z * 2 + place.y_lo
    stays = jnp.logical_and(swap_dp == place.dp, swap_t == place.me)
    moves = jnp.logical_not(stays)

    barrier = pltpu.get_barrier_semaphore()
    for target in (
        place.slot(0, 0, 1),
        place.slot(0, 1),
        place.slot(0, 3),
        place.slot(0, 2),
        place.slot(1, 0),
    ):
        pl.semaphore_signal(barrier, inc=1, device_id={"tensor": target}, device_id_type=MESH)

    @pl.when(moves)
    def _():
        pl.semaphore_signal(barrier, inc=1, device_id=(swap_dp, swap_t), device_id_type=MESH)

    enc_buf, mem_buf, dec_buf, ffn_buf = enc_refs[0], mem_refs[0], dec_refs[0], ffn_refs[0]
    enc_buf[place.me] = rms(tokens[0].astype(F32), gain[...]).astype(BF16)
    tag = tags[place.me]
    lang = jnp.zeros((1, D), F32)
    for index in range(LANGS):
        lang = jnp.where(tag == index, table[index : index + 1, :].astype(F32), lang)
    value = dec_tokens[0].astype(F32) + lang
    inp[...] = value
    dec_buf[place.me] = rms(value, cross_gain[...]).astype(BF16)
    for load in loads:
        load.start()

    @pl.when(moves)
    def _():
        pl.semaphore_wait(barrier, 6)

    @pl.when(stays)
    def _():
        pl.semaphore_wait(barrier, 5)

    enc.start()

    keys = lax.broadcasted_iota(jnp.int32, (SRC, SRC), 1)
    bucket = jnp.clip(keys - lax.broadcasted_iota(jnp.int32, (SRC, SRC), 0), -MAXREL, MAXREL) + MAXREL
    for head in range(HEADS):
        values = jnp.zeros((SRC, SRC), F32)
        for index in range(NB):
            values = jnp.where(bucket == index, bias[head, index], values)
        grid[head] = values
    for load in loads[:4]:
        load.wait()

    items = [(ex, head) for ex in range(2) for head in range(HEADS)]

    def enc_step(index, carry):
        @pl.when(index == 1)
        def _():
            for event in (1, 2, 3):
                enc.event(event)

        @pl.when(index == 4)
        def _():
            for event in (4, 5, 6):
                enc.event(event)

        @pl.when(index == 6)
        def _():
            dec.start()

        @pl.when(index == 7)
        def _():
            enc.event(7)

        chip = chip_at(place, GATHER_ORDER, index)
        enc.partner_wait(chip)
        rows = enc_buf[pl.ds(chip * 2, 2)].reshape(2 * SRC, D)
        q_s[...] = dot(rows, wq[...]).astype(BF16)
        k_s[...] = dot(rows, wk[...]).astype(BF16)
        v_s[...] = dot(rows, wv[...]).astype(BF16)
        columns = lax.broadcasted_iota(jnp.int32, (SRC, SRC), 1)
        for item, (ex, head) in enumerate(items):
            here, cols = slice(ex * SRC, (ex + 1) * SRC), slice(head * HD, (head + 1) * HD)
            s_s[item] = dot_t(q_s[here, cols], k_s[here, cols])
        for item, (ex, head) in enumerate(items):
            length = lengths[place.dp * 16 + chip * 2 + ex]
            scores = s_s[item] * SCALE + grid[head]
            w_s[item] = softmax_weights(jnp.where(columns < length, scores, NEG_FILL))
        for item, (ex, head) in enumerate(items):
            here, cols = slice(ex * SRC, (ex + 1) * SRC), slice(head * HD, (head + 1) * HD)
            ctx[chip * 2 + ex, :, cols] = dot(w_s[item], v_s[here, cols]).astype(BF16)
        return carry

    lax.fori_loop(0, 8, enc_step, 0)

    def dec_events(*events):
        def action():
            for event in events:
                dec.event(event)

        return action

    project_out(
        place,
        enc_sum,
        ctx,
        wo,
        (
            (1, dec_events(1, 2, 3)),
            (3, enc_sum.send_yfar),
            (4, functools.partial(enc_sum.send_side, 0)),
            (5, functools.partial(enc_sum.send_side, 1)),
            (9, dec_events(4, 5, 6, 7)),
        ),
    )

    def finish_memory(chunk):
        rows = enc_sum.all_rows(chunk)
        value = tokens[0, rows, :].astype(F32) + enc_sum.total(chunk)
        memory_out[0, rows, :] = rms(value, mem_gain[...]).astype(BF16)

    def shift_send(chunk):
        rows = enc_sum.all_rows(chunk)

        @pl.when(place.x == 0)
        def _():
            pltpu.make_async_copy(memory_out.at[0, rows], hop.at[rows], hop_sem.at[1, chunk]).start()

        @pl.when(place.x > 0)
        def _():
            send(
                memory_out.at[0, rows],
                hop.at[rows],
                hop_sem.at[0, chunk],
                hop_sem.at[1, chunk],
                {"tensor": shifted_to},
            )

    def swap_send(chunk):
        rows = enc_sum.all_rows(chunk)
        arrived(hop.at[rows], hop_sem.at[1, chunk])

        @pl.when(stays)
        def _():
            pltpu.make_async_copy(
                hop.at[rows], mem_buf.at[place.me, rows], swap_sem.at[1, chunk]
            ).start()

        @pl.when(moves)
        def _():
            send(
                hop.at[rows],
                mem_buf.at[swap_t, rows],
                swap_sem.at[0, chunk],
                swap_sem.at[1, chunk],
                (swap_dp, swap_t),
            )

    def spread(chunk):
        rows = enc_sum.all_rows(chunk)
        arrived(mem_buf.at[place.me, rows], swap_sem.at[1, chunk])
        each = ENC_CHUNKS // MEM_CHUNKS
        if chunk % each == each - 1:
            mem[chunk // each].start()

    enc_sum.run(finish_memory, shift_send, swap_send, spread)

    for chip in range(8):
        dec.partner_wait(chip)
    for load in loads[4:8]:
        load.wait()

    def q_step(index, carry):
        rows = dec_buf[pl.ds(index * 4, 4)].reshape(4 * TGT, D)
        q_all[pl.ds(index * 4, 4)] = dot(rows, cq[...]).astype(BF16).reshape(4, TGT, HW)
        return carry

    lax.fori_loop(0, 4, q_step, 0)

    def cross_step(index, carry):
        @pl.when(index == 1)
        def _():
            for gather in mem:
                for event in (1, 2, 3):
                    gather.event(event)

        @pl.when(index == 4)
        def _():
            for gather in mem:
                for event in (4, 5, 6):
                    gather.event(event)

        @pl.when(index == 7)
        def _():
            for gather in mem:
                gather.event(7)

        chip = chip_at(place, GATHER_ORDER, index)
        for gather in mem:
            gather.partner_wait(chip)
        rows = mem_buf[pl.ds(chip * 2, 2)].reshape(2 * SRC, D)
        k_s[...] = dot(rows, ck[...]).astype(BF16)
        v_s[...] = dot(rows, cv[...]).astype(BF16)
        columns = lax.broadcasted_iota(jnp.int32, (TGT, SRC), 1)
        base = ((chip % 4 + 4 - place.x) % 4) * 4 + chip // 4
        for item, (ex, head) in enumerate(items):
            here, cols = slice(ex * SRC, (ex + 1) * SRC), slice(head * HD, (head + 1) * HD)
            s_s[item, :TGT, :] = dot_t(q_all[base + 2 * ex, :, cols], k_s[here, cols])
        for item, (ex, head) in enumerate(items):
            row = base + 2 * ex
            length = lengths[(row // 2) * 16 + (row % 2) * 8 + place.dp]
            scores = s_s[item, :TGT, :] * SCALE
            w_s[item, :TGT, :] = softmax_weights(jnp.where(columns < length, scores, NEG_FILL))
        for item, (ex, head) in enumerate(items):
            here, cols = slice(ex * SRC, (ex + 1) * SRC), slice(head * HD, (head + 1) * HD)
            cross_ctx[base + 2 * ex, :, cols] = dot(w_s[item, :TGT, :], v_s[here, cols]).astype(BF16)
        return carry

    lax.fori_loop(0, 8, cross_step, 0)
    project_out(
        place,
        cross_sum,
        cross_ctx,
        co,
        (
            (3, cross_sum.send_yfar),
            (4, functools.partial(cross_sum.send_side, 0)),
            (5, functools.partial(cross_sum.send_side, 1)),
        ),
    )

    def finish_hidden(chunk):
        rows = cross_sum.all_rows(chunk)
        value = inp[rows, :] + cross_sum.total(chunk)
        hidden[rows, :] = value
        ffn_buf[place.me, rows, :] = rms(value, ffn_gain[...]).astype(BF16)

    cross_sum.run(finish_hidden, lambda chunk: ffn[chunk].start())
    for load in loads[8:]:
        load.wait()

    def ffn_step(index, carry):
        for pair in range(4):

            @pl.when(index == pair)
            def _(pair=pair):
                for gather in ffn:
                    for event in (2 * pair, 2 * pair + 1):
                        if event > 0:
                            gather.event(event)

        first = chip_at(place, GATHER_ORDER, index * 2)
        second = chip_at(place, GATHER_ORDER, index * 2 + 1)
        for gather in ffn:
            gather.partner_wait(first)
            gather.partner_wait(second)
        rows = jnp.concatenate(
            [
                ffn_buf[pl.ds(first * 2, 2)].reshape(2 * TGT, D),
                ffn_buf[pl.ds(second * 2, 2)].reshape(2 * TGT, D),
            ],
            axis=0,
        )
        for tile in range(FF // 512):
            cols = slice(tile * 512, (tile + 1) * 512)
            act[:, cols] = jnp.maximum(dot(rows, win[:, cols]), 0.0).astype(BF16)
        for tile in range(D // 256):
            cols = slice(tile * 256, (tile + 1) * 256)
            result = dot(act[...], wout[:, cols]).astype(BF16)
            ffn_sum.part[pl.ds(first * 2, 2), :, cols] = result[: 2 * TGT].reshape(2, TGT, 256)
            ffn_sum.part[pl.ds(second * 2, 2), :, cols] = result[2 * TGT :].reshape(2, TGT, 256)

        @pl.when(index > 0)
        def _():
            ffn_sum.partner_send(chip_at(place, GATHER_ORDER, index * 2 - 2))
            ffn_sum.partner_send(chip_at(place, GATHER_ORDER, index * 2 - 1))

        return carry

    lax.fori_loop(0, 4, ffn_step, 0)
    ffn_sum.partner_send(place.chip(*GATHER_ORDER[6]))
    ffn_sum.partner_send(place.chip(*GATHER_ORDER[7]))
    for index in range(8):
        ffn_sum.partner_add(place.chip(*SCATTER_ORDER[index]))
        if index == 0:
            ffn_sum.send_yfar()
        elif index < 3:
            ffn_sum.send_side(index - 1)

    def finish_out(chunk):
        rows = ffn_sum.all_rows(chunk)
        value = hidden[rows, :] + ffn_sum.total(chunk)
        position = lax.broadcasted_iota(jnp.int32, value.shape, 0) + chunk * ffn_sum.rows
        dec_out[0, rows, :] = jnp.where(position < tgt_length[0], value, 0.0).astype(BF16)

    ffn_sum.run(finish_out)

    for chunk in range(ENC_CHUNKS):
        rows = enc_sum.all_rows(chunk)

        @pl.when(place.x > 0)
        def _(rows=rows, chunk=chunk):
            arrived(hop.at[rows], hop_sem.at[0, chunk])

        @pl.when(moves)
        def _(rows=rows, chunk=chunk):
            arrived(hop.at[rows], swap_sem.at[0, chunk])

    for stage in [enc, dec, *mem, *ffn, enc_sum, cross_sum, ffn_sum]:
        stage.drain()


VM = pltpu.VMEM
SM = pltpu.SMEM


def on_device(
    enc_tokens,
    src_lengths,
    enc_gain,
    enc_query,
    enc_key,
    enc_value,
    enc_output,
    enc_bias,
    mem_gain,
    dec_tokens,
    tgt_lengths,
    lang_tags,
    lang_table,
    cross_gain,
    cross_query,
    cross_key,
    cross_value,
    cross_output,
    ffn_gain,
    ffn_in,
    ffn_out,
):
    weights = [
        enc_query,
        enc_key,
        enc_value,
        enc_output,
        cross_query,
        cross_key,
        cross_value,
        cross_output,
        ffn_in,
        ffn_out,
    ]
    spaces = [VM, SM, VM, SM, VM, VM, SM, VM, VM, VM, SM] + [pl.ANY] * len(weights)
    scratch = [pltpu.VMEM(weight.shape, BF16) for weight in weights]
    scratch += [
        pltpu.SemaphoreType.DMA((len(weights),)),
        pltpu.VMEM((HEADS, SRC, SRC), F32),
        pltpu.VMEM((2 * SRC, HW), BF16),
        pltpu.VMEM((2 * SRC, HW), BF16),
        pltpu.VMEM((2 * SRC, HW), BF16),
        pltpu.VMEM((2 * HEADS, SRC, SRC), F32),
        pltpu.VMEM((2 * HEADS, SRC, SRC), BF16),
        pltpu.VMEM((16, SRC, HW), BF16),
        pltpu.VMEM((SRC, D), BF16),
        pltpu.SemaphoreType.DMA((2, ENC_CHUNKS)),
        pltpu.SemaphoreType.DMA((2, ENC_CHUNKS)),
        pltpu.VMEM((TGT, D), F32),
        pltpu.VMEM((16, TGT, HW), BF16),
        pltpu.VMEM((16, TGT, HW), BF16),
        pltpu.VMEM((4 * TGT, FF), BF16),
        pltpu.VMEM((TGT, D), F32),
    ]
    scratch += Gather.scratch(SRC, 1)
    scratch += Gather.scratch(SRC, MEM_CHUNKS)
    scratch += Gather.scratch(TGT, 1)
    scratch += Gather.scratch(TGT, DEC_CHUNKS)
    scratch += Scatter.scratch(SRC, ENC_CHUNKS)
    scratch += Scatter.scratch(TGT, DEC_CHUNKS)
    scratch += Scatter.scratch(TGT, DEC_CHUNKS)
    return pl.pallas_call(
        layer_kernel,
        out_shape=(
            jax.ShapeDtypeStruct((1, SRC, D), BF16),
            jax.ShapeDtypeStruct((1, TGT, D), BF16),
        ),
        in_specs=[pl.BlockSpec(memory_space=space) for space in spaces],
        out_specs=(pl.BlockSpec(memory_space=VM), pl.BlockSpec(memory_space=VM)),
        scratch_shapes=scratch,
        compiler_params=pltpu.CompilerParams(
            collective_id=1, has_side_effects=True, vmem_limit_bytes=67_043_328
        ),
    )(
        enc_tokens,
        src_lengths,
        enc_gain,
        enc_bias,
        mem_gain,
        dec_tokens,
        lang_tags,
        lang_table,
        cross_gain,
        ffn_gain,
        tgt_lengths,
        *weights,
    )


def solution(mesh):
    in_specs = (
        P(("dp", "tensor"), None, None),
        P(),
        P(),
        P(None, "tensor"),
        P(None, "tensor"),
        P(None, "tensor"),
        P("tensor", None),
        P("tensor", None),
        P(),
        P(("dp", "tensor"), None, None),
        P(("dp", "tensor")),
        P("dp"),
        P(),
        P(),
        P(None, "tensor"),
        P(None, "tensor"),
        P(None, "tensor"),
        P("tensor", None),
        P(),
        P(None, "tensor"),
        P("tensor", None),
    )
    out_specs = (P(("dp", "tensor"), None, None), P(("dp", "tensor"), None, None))
    return jax.shard_map(
        on_device, mesh=mesh, in_specs=in_specs, out_specs=out_specs, check_vma=False
    )
```

```python
import functools

import jax
import jax.numpy as jnp
from jax import lax
from jax.experimental import pallas as pl
from jax.experimental.pallas import tpu as pltpu
from jax.sharding import PartitionSpec as P

D = 1024
HD = 128
SRC = 128
TGT = 64
MAXREL = 16
NB = 33
LANGS = 8
HEADS = 4
HW = HEADS * HD
FF = 2048
EPSILON = 1e-06
NEG_FILL = -1e30
SCALE = HD ** (-0.5)
MESH = pl.DeviceIdType.MESH
F32 = jnp.float32
BF16 = jnp.bfloat16

GATHER_ORDER = ((0, 0), (0, 1), (0, 3), (1, 0), (0, 2), (1, 1), (1, 3), (1, 2))
SCATTER_ORDER = ((1, 2), (1, 1), (1, 3), (0, 2), (0, 1), (0, 3), (1, 0), (0, 0))
FFN_ORDER = ((0, 0), (0, 1), (1, 2), (0, 2), (1, 1), (1, 3), (1, 0), (0, 3))
ROW_CHUNKS = 2
ENC_CHUNKS = 4
MEM_CHUNKS = 2
DEC_CHUNKS = 2


def packed(order):
    return (
        sum(dy << i for i, (dy, dz) in enumerate(order)),
        sum(dz << (2 * i) for i, (dy, dz) in enumerate(order)),
    )


def chip_at(place, order, index):
    dy_bits, dz_bits = packed(order)
    return place.chip((dy_bits >> index) & 1, (dz_bits >> (2 * index)) & 3)


def rms(values, gain):
    mean_sq = jnp.mean(values * values, axis=-1, keepdims=True)
    return values * lax.rsqrt(mean_sq + EPSILON) * gain


class Place:
    def __init__(self):
        self.me = lax.axis_index("tensor")
        self.dp = lax.axis_index("dp")
        self.core = self.me % 2
        self.z = (self.me // 2) % 4
        self.y = self.me // 8
        self.x = self.dp // 2
        self.y_lo = self.dp % 2

    def chip(self, dy, dz):
        return ((self.y + dy) % 2) * 4 + (self.z + dz) % 4

    def slot(self, dy, dz, dk=0):
        return self.chip(dy, dz) * 2 + (self.core + dk) % 2


def send(src, dst, send_sem, recv_sem, device):
    pltpu.make_async_remote_copy(
        src_ref=src,
        dst_ref=dst,
        send_sem=send_sem,
        recv_sem=recv_sem,
        device_id=device,
        device_id_type=MESH,
    ).start()


def arrived(dst, recv_sem):
    pltpu.make_async_copy(dst, dst, recv_sem).wait()


class Gather:
    SENDS = 16

    def __init__(self, place, buf, ssem, rsem, hsem, chunk, chunks, direct):
        self.p, self.buf, self.chunk, self.direct = place, buf, chunk, direct
        self.ssem, self.rsem, self.hsem = ssem, rsem, hsem
        self.rows = buf.shape[1] // chunks
        self.first = chunk * self.rows
        self.sent = []

    def _part(self, slot):
        return self.buf.at[slot, pl.ds(self.first, self.rows)]

    def _half_part(self, slot, which):
        half = self.rows // 2
        return self.buf.at[slot, pl.ds(self.first + which * half, half)]

    def _send(self, src, recv_sem, target):
        sem = self.ssem.at[self.chunk, len(self.sent)]
        send(src, src, sem, recv_sem, {"tensor": target})
        self.sent.append(src.shape[0])

    def _full(self, slot, target):
        self._send(self._part(slot), self.rsem.at[self.chunk, slot], target)

    def _half(self, slot, which, target):
        self._send(self._half_part(slot, which), self.hsem.at[self.chunk, which], target)

    def start(self):
        p = self.p
        for target in (p.slot(0, 1), p.slot(0, 3), p.slot(1, 0), p.slot(0, 0, 1)):
            self._full(p.me, target)
        if self.direct:
            self._full(p.me, p.slot(0, 2))

    def event(self, index):
        p = self.p
        dy, dz = GATHER_ORDER[index]
        slot = p.slot(dy, dz)
        if (dy, dz) == (0, 2) and not self.direct:
            for which in (0, 1):
                arrived(self._half_part(slot, which), self.hsem.at[self.chunk, which])
        else:
            arrived(self._part(slot), self.rsem.at[self.chunk, slot])
        if (dy, dz) == (0, 2):
            self._full(slot, p.slot(1, 0))
        elif (dy, dz) == (0, 1) and not self.direct:
            self._half(slot, 1, p.slot(0, 3))
        elif (dy, dz) == (0, 3) and not self.direct:
            self._half(slot, 0, p.slot(0, 1))
        elif (dy, dz) == (1, 0):
            self._full(slot, p.slot(0, 1))
            self._full(slot, p.slot(0, 3))
        self._full(slot, p.slot(0, 0, 1))

    def partner_wait(self, chip):
        slot = chip * 2 + (self.p.core + 1) % 2
        arrived(self._part(slot), self.rsem.at[self.chunk, slot])

    def drain(self):
        for index, rows in enumerate(self.sent):
            arrived(self.buf.at[0, pl.ds(0, rows)], self.ssem.at[self.chunk, index])

    @staticmethod
    def scratch(rows, chunks):
        return [
            pltpu.VMEM((16, rows, D), BF16),
            pltpu.SemaphoreType.DMA((chunks, Gather.SENDS)),
            pltpu.SemaphoreType.DMA((chunks, 16)),
            pltpu.SemaphoreType.DMA((chunks, 2)),
        ]

    @staticmethod
    def make(place, refs, chunks, direct=False):
        return [Gather(place, *refs, chunk, chunks, direct) for chunk in range(chunks)]


class Scatter:
    SENDS = 10

    def __init__(self, place, chunks, direct, part, xbuf, yfar, relay, fin, finy, ysend, yrec, *sems):
        self.p, self.chunks, self.direct = place, chunks, direct
        self.part, self.xbuf, self.yfar, self.relay = part, xbuf, yfar, relay
        self.fin, self.finy, self.ysend, self.yrec = fin, finy, ysend, yrec
        self.psem, self.xsem, self.ssem = sems[:3]
        self.yfar_sem, self.relay_sem, self.fin_sem, self.finy_sem, self.yrec_sem = sems[3:]
        self.rows = part.shape[1] // chunks
        self.half = self.rows // 2
        self.sent = []

    @staticmethod
    def scratch(rows, chunks):
        return [
            pltpu.VMEM((16, rows, D), BF16),
            pltpu.VMEM((8, rows, D), BF16),
            pltpu.VMEM((rows, D), BF16),
            pltpu.VMEM((rows, D), BF16),
            pltpu.VMEM((2, rows, D), BF16),
            pltpu.VMEM((2, rows, D), BF16),
            pltpu.VMEM((rows, D), BF16),
            pltpu.VMEM((rows, D), BF16),
            pltpu.SemaphoreType.DMA((8,)),
            pltpu.SemaphoreType.DMA((8,)),
            pltpu.SemaphoreType.DMA((chunks * Scatter.SENDS,)),
            pltpu.SemaphoreType.DMA((chunks,)),
            pltpu.SemaphoreType.DMA((chunks, 2)),
            pltpu.SemaphoreType.DMA((chunks, 2, 2)),
            pltpu.SemaphoreType.DMA((chunks, 2)),
            pltpu.SemaphoreType.DMA((chunks,)),
        ]

    def partner_send(self, chip):
        slot = chip * 2 + (self.p.core + 1) % 2
        send(
            self.part.at[slot],
            self.xbuf.at[chip],
            self.psem.at[chip],
            self.xsem.at[chip],
            {"tensor": self.p.slot(0, 0, 1)},
        )

    def partner_add(self, chip):
        arrived(self.xbuf.at[chip], self.xsem.at[chip])
        slot = chip * 2 + self.p.core
        self.part[slot] = self.part[slot] + self.xbuf[chip]

    def _send(self, src, dst, recv_sem, target):
        sem = self.ssem.at[len(self.sent)]
        send(src, dst, sem, recv_sem, {"tensor": target})
        self.sent.append(src.shape[0])

    def all_rows(self, chunk):
        return pl.ds(chunk * self.rows, self.rows)

    def half_rows(self, chunk, which):
        return pl.ds(chunk * self.rows + which * self.half, self.half)

    def send_yfar(self):
        slot = self.p.slot(1, 2)
        for chunk in range(self.chunks):
            rows = self.all_rows(chunk)
            self._send(
                self.part.at[slot, rows],
                self.yfar.at[rows],
                self.yfar_sem.at[chunk],
                self.p.slot(1, 0),
            )

    def send_side(self, way):
        dz = (1, 3)[way]
        slot = self.p.slot(1, dz)
        for chunk in range(self.chunks):
            rows = self.all_rows(chunk)
            self._send(
                self.part.at[slot, rows],
                self.finy.at[way, rows],
                self.finy_sem.at[chunk, way],
                self.p.slot(0, dz),
            )

    def _near(self, chunk, way, which):
        dz = (1, 3)[way]
        rows = self.half_rows(chunk, which)
        self._send(
            self.part.at[self.p.slot(0, dz), rows],
            self.fin.at[way, rows],
            self.fin_sem.at[chunk, way, which],
            self.p.slot(0, dz),
        )

    def send_near(self, way):
        for chunk in range(self.chunks):
            for which in (0, 1):
                self._near(chunk, way, which)

    def far(self, chunk):
        rows = self.all_rows(chunk)
        slot = self.p.slot(0, 2)
        arrived(self.yfar.at[rows], self.yfar_sem.at[chunk])
        self.part[slot, rows, :] = self.part[slot, rows, :] + self.yfar[rows, :]
        if self.direct:
            self._send(
                self.part.at[slot, rows], self.relay.at[rows], self.relay_sem.at[chunk, 0], slot
            )
            return
        self._near(chunk, 0, 1)
        self._near(chunk, 1, 0)
        for way in (0, 1):
            self._send(
                self.part.at[slot, self.half_rows(chunk, way)],
                self.relay.at[self.half_rows(chunk, way)],
                self.relay_sem.at[chunk, way],
                self.p.slot(0, (1, 3)[way]),
            )

    def cross_sum(self, chunk):
        rows = self.all_rows(chunk)
        for way in (0, 1):
            arrived(self.finy.at[way, rows], self.finy_sem.at[chunk, way])
        total = self.part[self.p.slot(1, 0), rows, :].astype(F32)
        total = total + self.finy[0, rows, :].astype(F32) + self.finy[1, rows, :].astype(F32)
        self.ysend[rows, :] = total.astype(BF16)

    def cross_send(self, chunk):
        rows = self.all_rows(chunk)
        self._send(
            self.ysend.at[rows], self.yrec.at[rows], self.yrec_sem.at[chunk], self.p.slot(1, 0)
        )

    def relay_add(self, chunk):
        for way in (0, 1):
            slot, rows = self.p.slot(0, (1, 3)[way]), self.half_rows(chunk, way)
            arrived(self.relay.at[rows], self.relay_sem.at[chunk, way])
            self.part[slot, rows, :] = self.part[slot, rows, :] + self.relay[rows, :]

    def relay_send(self, chunk):
        for way in (0, 1):
            self._near(chunk, way, way)

    def total(self, chunk):
        rows = self.all_rows(chunk)
        for way in (0, 1):
            for which in (0, 1):
                arrived(
                    self.fin.at[way, self.half_rows(chunk, which)],
                    self.fin_sem.at[chunk, way, which],
                )
        own = self.part[self.p.me, rows, :].astype(F32)
        own = own + self.fin[0, rows, :].astype(F32) + self.fin[1, rows, :].astype(F32)
        if self.direct:
            arrived(self.relay.at[rows], self.relay_sem.at[chunk, 0])
            own = own + self.relay[rows, :].astype(F32)
        arrived(self.yrec.at[rows], self.yrec_sem.at[chunk])
        return own + self.yrec[rows, :].astype(F32)

    def run(self, *stages):
        if self.direct:
            steps = (self.cross_sum, self.cross_send) + stages
        else:
            steps = (
                self.far,
                self.cross_sum,
                lambda chunk: (self.cross_send(chunk), self.relay_add(chunk)),
                self.relay_send,
            ) + stages
        for time in range(self.chunks + len(steps) - 1):
            for index, stage in enumerate(steps):
                if 0 <= time - index < self.chunks:
                    stage(time - index)

    def drain(self):
        for chip in range(8):
            slot = chip * 2 + (self.p.core + 1) % 2
            arrived(self.part.at[slot], self.psem.at[chip])
        for index, rows in enumerate(self.sent):
            arrived(self.part.at[0, pl.ds(0, rows)], self.ssem.at[index])


def project_out(place, scatter, ctx, weight, also):
    rows = ctx.shape[1]

    def step(index, carry):
        @pl.when(index < 8)
        def _():
            chip = chip_at(place, SCATTER_ORDER, index)
            block = ctx[pl.ds(chip * 2, 2)].reshape(2 * rows, HW)
            scatter.part[pl.ds(chip * 2, 2)] = dot(block, weight[...]).astype(BF16).reshape(2, rows, D)

        @pl.when(jnp.logical_and(index > 0, index < 9))
        def _():
            scatter.partner_send(chip_at(place, SCATTER_ORDER, index - 1))

        @pl.when(index > 1)
        def _():
            scatter.partner_add(chip_at(place, SCATTER_ORDER, index - 2))

        for at, action in also:

            @pl.when(index == at)
            def _(action=action):
                action()

        return carry

    lax.fori_loop(0, 10, step, 0)


def dot(left, right):
    return jnp.dot(left, right, preferred_element_type=F32)


def dot_t(left, right):
    return lax.dot_general(left, right, (((1,), (1,)), ((), ())), preferred_element_type=F32)


def softmax_weights(scores):
    row_max = jnp.max(scores, axis=-1, keepdims=True)
    exponent = jnp.exp(scores - row_max)
    return (exponent * (1.0 / jnp.sum(exponent, axis=-1, keepdims=True))).astype(BF16)


def layer_kernel(*refs):
    refs = list(refs)

    def take(count):
        taken, refs[:count] = refs[:count], []
        return taken

    tokens, lengths, gain, bias, mem_gain = take(5)
    dec_tokens, tags, table, cross_gain, ffn_gain, tgt_length = take(6)
    hbm = take(10)
    memory_out, dec_out = take(2)
    weights = take(10)
    (weight_sem,) = take(1)
    wq, wk, wv, wo, cq, ck, cv, co, win, wout = weights
    grid, q_s, k_s, v_s, s_s, w_s, ctx = take(7)
    hop, hop_sem, swap_sem = take(3)
    inp, q_all, cross_ctx, act, hidden = take(5)
    place = Place()
    enc_refs, mem_refs, dec_refs, ffn_refs = take(4), take(4), take(4), take(4)
    enc = Gather.make(place, enc_refs, ROW_CHUNKS)
    mem = Gather.make(place, mem_refs, MEM_CHUNKS)
    (dec,) = Gather.make(place, dec_refs, 1)
    ffn = Gather.make(place, ffn_refs, DEC_CHUNKS, True)
    enc_sum = Scatter(place, ENC_CHUNKS, False, *take(16))
    cross_sum = Scatter(place, DEC_CHUNKS, True, *take(16))
    ffn_sum = Scatter(place, DEC_CHUNKS, True, *take(16))

    def events(gathers, *numbers):
        for gather in gathers:
            for number in numbers:
                gather.event(number)

    loads = [
        pltpu.make_async_copy(src, dst, weight_sem.at[index])
        for index, (src, dst) in enumerate(zip(hbm, weights))
    ]
    shifted_to = place.slot(0, place.x)
    swap_dp = ((place.z + 4 - place.x) % 4) * 2 + place.core
    swap_t = place.y * 8 + place.z * 2 + place.y_lo
    stays = jnp.logical_and(swap_dp == place.dp, swap_t == place.me)
    moves = jnp.logical_not(stays)

    barrier = pltpu.get_barrier_semaphore()
    for target in (
        place.slot(0, 0, 1),
        place.slot(0, 1),
        place.slot(0, 3),
        place.slot(0, 2),
        place.slot(1, 0),
    ):
        pl.semaphore_signal(barrier, inc=1, device_id={"tensor": target}, device_id_type=MESH)

    @pl.when(moves)
    def _():
        pl.semaphore_signal(barrier, inc=1, device_id=(swap_dp, swap_t), device_id_type=MESH)

    enc_buf, mem_buf, dec_buf, ffn_buf = enc_refs[0], mem_refs[0], dec_refs[0], ffn_refs[0]
    enc_buf[place.me] = rms(tokens[0].astype(F32), gain[...]).astype(BF16)
    tag = tags[place.me]
    lang = jnp.zeros((1, D), F32)
    for index in range(LANGS):
        lang = jnp.where(tag == index, table[index : index + 1, :].astype(F32), lang)
    value = dec_tokens[0].astype(F32) + lang
    inp[...] = value
    dec_buf[place.me] = rms(value, cross_gain[...]).astype(BF16)
    for load in loads[:4]:
        load.start()

    @pl.when(moves)
    def _():
        pl.semaphore_wait(barrier, 6)

    @pl.when(stays)
    def _():
        pl.semaphore_wait(barrier, 5)

    for gather in enc:
        gather.start()

    keys = lax.broadcasted_iota(jnp.int32, (SRC, SRC), 1)
    bucket = jnp.clip(keys - lax.broadcasted_iota(jnp.int32, (SRC, SRC), 0), -MAXREL, MAXREL) + MAXREL
    for head in range(HEADS):
        values = jnp.zeros((SRC, SRC), F32)
        for index in range(NB):
            values = jnp.where(bucket == index, bias[head, index], values)
        grid[head] = values
    for load in loads[:4]:
        load.wait()

    items = [(ex, head) for ex in range(2) for head in range(HEADS)]

    def enc_step(index, carry):
        @pl.when(index == 1)
        def _():
            events(enc, 1, 2, 3)
            dec.start()
            for load in loads[4:]:
                load.start()

        @pl.when(index == 4)
        def _():
            events(enc, 4, 5, 6)

        @pl.when(index == 5)
        def _():
            events([dec], 1, 2, 3)

        @pl.when(index == 7)
        def _():
            events(enc, 7)

        chip = chip_at(place, GATHER_ORDER, index)
        for gather in enc:
            gather.partner_wait(chip)
        rows = enc_buf[pl.ds(chip * 2, 2)].reshape(2 * SRC, D)
        q_s[...] = dot(rows, wq[...]).astype(BF16)
        k_s[...] = dot(rows, wk[...]).astype(BF16)
        v_s[...] = dot(rows, wv[...]).astype(BF16)
        columns = lax.broadcasted_iota(jnp.int32, (SRC, SRC), 1)
        for item, (ex, head) in enumerate(items):
            here, cols = slice(ex * SRC, (ex + 1) * SRC), slice(head * HD, (head + 1) * HD)
            s_s[item] = dot_t(q_s[here, cols], k_s[here, cols])
        for item, (ex, head) in enumerate(items):
            length = lengths[place.dp * 16 + chip * 2 + ex]
            scores = s_s[item] * SCALE + grid[head]
            w_s[item] = softmax_weights(jnp.where(columns < length, scores, NEG_FILL))
        for item, (ex, head) in enumerate(items):
            here, cols = slice(ex * SRC, (ex + 1) * SRC), slice(head * HD, (head + 1) * HD)
            ctx[chip * 2 + ex, :, cols] = dot(w_s[item], v_s[here, cols]).astype(BF16)
        return carry

    lax.fori_loop(0, 8, enc_step, 0)

    project_out(
        place,
        enc_sum,
        ctx,
        wo,
        (
            (1, functools.partial(events, [dec], 4, 5, 6, 7)),
            (3, enc_sum.send_yfar),
            (4, functools.partial(enc_sum.send_side, 0)),
            (5, functools.partial(enc_sum.send_side, 1)),
        ),
    )

    def finish_memory(chunk):
        rows = enc_sum.all_rows(chunk)
        value = tokens[0, rows, :].astype(F32) + enc_sum.total(chunk)
        memory_out[0, rows, :] = rms(value, mem_gain[...]).astype(BF16)

    def shift_send(chunk):
        rows = enc_sum.all_rows(chunk)

        @pl.when(place.x == 0)
        def _():
            pltpu.make_async_copy(memory_out.at[0, rows], hop.at[rows], hop_sem.at[1, chunk]).start()

        @pl.when(place.x > 0)
        def _():
            send(
                memory_out.at[0, rows],
                hop.at[rows],
                hop_sem.at[0, chunk],
                hop_sem.at[1, chunk],
                {"tensor": shifted_to},
            )

    def swap_send(chunk):
        rows = enc_sum.all_rows(chunk)
        arrived(hop.at[rows], hop_sem.at[1, chunk])

        @pl.when(stays)
        def _():
            pltpu.make_async_copy(
                hop.at[rows], mem_buf.at[place.me, rows], swap_sem.at[1, chunk]
            ).start()

        @pl.when(moves)
        def _():
            send(
                hop.at[rows],
                mem_buf.at[swap_t, rows],
                swap_sem.at[0, chunk],
                swap_sem.at[1, chunk],
                (swap_dp, swap_t),
            )

    def spread(chunk):
        rows = enc_sum.all_rows(chunk)
        arrived(mem_buf.at[place.me, rows], swap_sem.at[1, chunk])
        each = ENC_CHUNKS // MEM_CHUNKS
        if chunk % each == each - 1:
            mem[chunk // each].start()

    enc_sum.run(finish_memory, shift_send, swap_send, spread)

    for chip in range(8):
        dec.partner_wait(chip)
    for load in loads[4:8]:
        load.wait()

    def q_step(index, carry):
        rows = dec_buf[pl.ds(index * 4, 4)].reshape(4 * TGT, D)
        q_all[pl.ds(index * 4, 4)] = dot(rows, cq[...]).astype(BF16).reshape(4, TGT, HW)
        return carry

    lax.fori_loop(0, 4, q_step, 0)

    def cross_step(index, carry):
        @pl.when(index == 1)
        def _():
            events(mem, 1, 2, 3)

        @pl.when(index == 4)
        def _():
            events(mem, 4, 5, 6)

        @pl.when(index == 7)
        def _():
            events(mem, 7)

        chip = chip_at(place, GATHER_ORDER, index)
        for gather in mem:
            gather.partner_wait(chip)
        rows = mem_buf[pl.ds(chip * 2, 2)].reshape(2 * SRC, D)
        k_s[...] = dot(rows, ck[...]).astype(BF16)
        v_s[...] = dot(rows, cv[...]).astype(BF16)
        columns = lax.broadcasted_iota(jnp.int32, (TGT, SRC), 1)
        base = ((chip % 4 + 4 - place.x) % 4) * 4 + chip // 4
        for item, (ex, head) in enumerate(items):
            here, cols = slice(ex * SRC, (ex + 1) * SRC), slice(head * HD, (head + 1) * HD)
            s_s[item, :TGT, :] = dot_t(q_all[base + 2 * ex, :, cols], k_s[here, cols])
        for item, (ex, head) in enumerate(items):
            row = base + 2 * ex
            length = lengths[(row // 2) * 16 + (row % 2) * 8 + place.dp]
            scores = s_s[item, :TGT, :] * SCALE
            w_s[item, :TGT, :] = softmax_weights(jnp.where(columns < length, scores, NEG_FILL))
        for item, (ex, head) in enumerate(items):
            here, cols = slice(ex * SRC, (ex + 1) * SRC), slice(head * HD, (head + 1) * HD)
            cross_ctx[base + 2 * ex, :, cols] = dot(w_s[item, :TGT, :], v_s[here, cols]).astype(BF16)
        return carry

    lax.fori_loop(0, 8, cross_step, 0)
    project_out(
        place,
        cross_sum,
        cross_ctx,
        co,
        (
            (3, cross_sum.send_yfar),
            (4, functools.partial(cross_sum.send_side, 0)),
            (5, functools.partial(cross_sum.send_side, 1)),
            (7, functools.partial(cross_sum.send_near, 0)),
            (8, functools.partial(cross_sum.send_near, 1)),
            (9, lambda: [cross_sum.far(chunk) for chunk in range(DEC_CHUNKS)]),
        ),
    )

    def finish_hidden(chunk):
        rows = cross_sum.all_rows(chunk)
        value = inp[rows, :] + cross_sum.total(chunk)
        hidden[rows, :] = value
        ffn_buf[place.me, rows, :] = rms(value, ffn_gain[...]).astype(BF16)

    cross_sum.run(finish_hidden, lambda chunk: ffn[chunk].start())
    for load in loads[8:]:
        load.wait()

    def ffn_step(index, carry):
        @pl.when(index == 0)
        def _():
            events(ffn, 1, 2, 3, 4)

        @pl.when(index == 1)
        def _():
            events(ffn, 5, 6, 7)

        first = chip_at(place, FFN_ORDER, index * 2)
        second = chip_at(place, FFN_ORDER, index * 2 + 1)

        @pl.when(index == 0)
        def _():
            for chip in range(2):
                for gather in ffn:
                    gather.partner_wait(place.chip(*FFN_ORDER[chip]))

        @pl.when(index == 1)
        def _():
            for chip in range(2, 8):
                for gather in ffn:
                    gather.partner_wait(place.chip(*FFN_ORDER[chip]))

        rows = jnp.concatenate(
            [
                ffn_buf[pl.ds(first * 2, 2)].reshape(2 * TGT, D),
                ffn_buf[pl.ds(second * 2, 2)].reshape(2 * TGT, D),
            ],
            axis=0,
        )
        for tile in range(FF // 512):
            cols = slice(tile * 512, (tile + 1) * 512)
            act[:, cols] = jnp.maximum(dot(rows, win[:, cols]), 0.0).astype(BF16)

        @pl.when(index > 0)
        def _():
            ffn_sum.partner_add(chip_at(place, FFN_ORDER, index * 2 - 2))
            ffn_sum.partner_add(chip_at(place, FFN_ORDER, index * 2 - 1))

        @pl.when(index == 1)
        def _():
            ffn_sum.send_near(0)

        @pl.when(index == 2)
        def _():
            ffn_sum.send_yfar()

        @pl.when(index == 3)
        def _():
            ffn_sum.send_side(0)
            ffn_sum.send_side(1)
            for chunk in range(DEC_CHUNKS):
                ffn_sum.far(chunk)

        for tile in range(D // 256):
            cols = slice(tile * 256, (tile + 1) * 256)
            result = dot(act[...], wout[:, cols]).astype(BF16)
            ffn_sum.part[pl.ds(first * 2, 2), :, cols] = result[: 2 * TGT].reshape(2, TGT, 256)
            ffn_sum.part[pl.ds(second * 2, 2), :, cols] = result[2 * TGT :].reshape(2, TGT, 256)
        ffn_sum.partner_send(first)
        ffn_sum.partner_send(second)
        return carry

    lax.fori_loop(0, 4, ffn_step, 0)
    for index in (6, 7):
        ffn_sum.partner_add(place.chip(*FFN_ORDER[index]))
    ffn_sum.send_near(1)

    def finish_out(chunk):
        rows = ffn_sum.all_rows(chunk)
        value = hidden[rows, :] + ffn_sum.total(chunk)
        position = lax.broadcasted_iota(jnp.int32, value.shape, 0) + chunk * ffn_sum.rows
        dec_out[0, rows, :] = jnp.where(position < tgt_length[0], value, 0.0).astype(BF16)

    ffn_sum.run(finish_out)

    for chunk in range(ENC_CHUNKS):
        rows = enc_sum.all_rows(chunk)

        @pl.when(place.x > 0)
        def _(rows=rows, chunk=chunk):
            arrived(hop.at[rows], hop_sem.at[0, chunk])

        @pl.when(moves)
        def _(rows=rows, chunk=chunk):
            arrived(hop.at[rows], swap_sem.at[0, chunk])

    for stage in [*enc, dec, *mem, *ffn, enc_sum, cross_sum, ffn_sum]:
        stage.drain()


def leave_kernel(memory, dec, memory_out, dec_out):
    memory_out[...] = memory[...]
    dec_out[...] = dec[...]


VM = pltpu.VMEM
SM = pltpu.SMEM


def on_device(
    enc_tokens,
    src_lengths,
    enc_gain,
    enc_query,
    enc_key,
    enc_value,
    enc_output,
    enc_bias,
    mem_gain,
    dec_tokens,
    tgt_lengths,
    lang_tags,
    lang_table,
    cross_gain,
    cross_query,
    cross_key,
    cross_value,
    cross_output,
    ffn_gain,
    ffn_in,
    ffn_out,
):
    weights = [
        enc_query,
        enc_key,
        enc_value,
        enc_output,
        cross_query,
        cross_key,
        cross_value,
        cross_output,
        ffn_in,
        ffn_out,
    ]
    spaces = [VM, SM, VM, SM, VM, VM, SM, VM, VM, VM, SM] + [pl.ANY] * len(weights)
    scratch = [pltpu.VMEM(weight.shape, BF16) for weight in weights]
    scratch += [
        pltpu.SemaphoreType.DMA((len(weights),)),
        pltpu.VMEM((HEADS, SRC, SRC), F32),
        pltpu.VMEM((2 * SRC, HW), BF16),
        pltpu.VMEM((2 * SRC, HW), BF16),
        pltpu.VMEM((2 * SRC, HW), BF16),
        pltpu.VMEM((2 * HEADS, SRC, SRC), F32),
        pltpu.VMEM((2 * HEADS, SRC, SRC), BF16),
        pltpu.VMEM((16, SRC, HW), BF16),
        pltpu.VMEM((SRC, D), BF16),
        pltpu.SemaphoreType.DMA((2, ENC_CHUNKS)),
        pltpu.SemaphoreType.DMA((2, ENC_CHUNKS)),
        pltpu.VMEM((TGT, D), F32),
        pltpu.VMEM((16, TGT, HW), BF16),
        pltpu.VMEM((16, TGT, HW), BF16),
        pltpu.VMEM((4 * TGT, FF), BF16),
        pltpu.VMEM((TGT, D), F32),
    ]
    scratch += Gather.scratch(SRC, ROW_CHUNKS)
    scratch += Gather.scratch(SRC, MEM_CHUNKS)
    scratch += Gather.scratch(TGT, 1)
    scratch += Gather.scratch(TGT, DEC_CHUNKS)
    scratch += Scatter.scratch(SRC, ENC_CHUNKS)
    scratch += Scatter.scratch(TGT, DEC_CHUNKS)
    scratch += Scatter.scratch(TGT, DEC_CHUNKS)
    memory, dec = pl.pallas_call(
        layer_kernel,
        out_shape=(
            jax.ShapeDtypeStruct((1, SRC, D), BF16),
            jax.ShapeDtypeStruct((1, TGT, D), BF16),
        ),
        in_specs=[pl.BlockSpec(memory_space=space) for space in spaces],
        out_specs=(pl.BlockSpec(memory_space=VM), pl.BlockSpec(memory_space=VM)),
        scratch_shapes=scratch,
        compiler_params=pltpu.CompilerParams(
            collective_id=1, has_side_effects=True, vmem_limit_bytes=67_043_328
        ),
    )(
        enc_tokens,
        src_lengths,
        enc_gain,
        enc_bias,
        mem_gain,
        dec_tokens,
        lang_tags,
        lang_table,
        cross_gain,
        ffn_gain,
        tgt_lengths,
        *weights,
    )
    return pl.pallas_call(
        leave_kernel,
        out_shape=(
            jax.ShapeDtypeStruct(memory.shape, BF16),
            jax.ShapeDtypeStruct(dec.shape, BF16),
        ),
        in_specs=[pl.BlockSpec(memory_space=VM)] * 2,
        out_specs=(pl.BlockSpec(memory_space=VM), pl.BlockSpec(memory_space=VM)),
    )(memory, dec)


def solution(mesh):
    in_specs = (
        P(("dp", "tensor"), None, None),
        P(),
        P(),
        P(None, "tensor"),
        P(None, "tensor"),
        P(None, "tensor"),
        P("tensor", None),
        P("tensor", None),
        P(),
        P(("dp", "tensor"), None, None),
        P(("dp", "tensor")),
        P("dp"),
        P(),
        P(),
        P(None, "tensor"),
        P(None, "tensor"),
        P(None, "tensor"),
        P("tensor", None),
        P(),
        P(None, "tensor"),
        P("tensor", None),
    )
    out_specs = (P(("dp", "tensor"), None, None), P(("dp", "tensor"), None, None))
    return jax.shard_map(
        on_device, mesh=mesh, in_specs=in_specs, out_specs=out_specs, check_vma=False
    )
```

```python
import functools

import jax
import jax.numpy as jnp
from jax import lax
from jax.experimental import pallas as pl
from jax.experimental.pallas import tpu as pltpu
from jax.sharding import PartitionSpec as P

D = 1024
HD = 128
SRC = 128
TGT = 64
MAXREL = 16
NB = 33
LANGS = 8
HEADS = 4
HW = HEADS * HD
FF = 2048
EPSILON = 1e-06
NEG_FILL = -1e30
SCALE = HD ** (-0.5)
MESH = pl.DeviceIdType.MESH
F32 = jnp.float32
BF16 = jnp.bfloat16

GATHER_ORDER = ((0, 0), (0, 1), (0, 3), (1, 0), (0, 2), (1, 1), (1, 3), (1, 2))
FFN_ORDER = ((0, 1), (1, 0), (1, 1), (1, 3), (1, 2), (0, 2))
PAIR_DZ = 0 << 6 | 1 << 10 | 3 << 12 | 2 << 14
PAIR_BEFORE = 0 << 10 | 1 << 12 | 3 << 14
ROW_CHUNKS = 2
ENC_CHUNKS = 4
MEM_CHUNKS = 2
DEC_CHUNKS = 2


def packed(order):
    return (
        sum(dy << i for i, (dy, dz) in enumerate(order)),
        sum(dz << (2 * i) for i, (dy, dz) in enumerate(order)),
    )


def chip_at(place, order, index):
    dy_bits, dz_bits = packed(order)
    return place.chip((dy_bits >> index) & 1, (dz_bits >> (2 * index)) & 3)


def rms(values, gain):
    mean_sq = jnp.mean(values * values, axis=-1, keepdims=True)
    return values * lax.rsqrt(mean_sq + EPSILON) * gain


class Place:
    def __init__(self):
        self.me = lax.axis_index("tensor")
        self.dp = lax.axis_index("dp")
        self.core = self.me % 2
        self.z = (self.me // 2) % 4
        self.y = self.me // 8
        self.x = self.dp // 2
        self.y_lo = self.dp % 2

    def chip(self, dy, dz):
        return ((self.y + dy) % 2) * 4 + (self.z + dz) % 4

    def slot(self, dy, dz, dk=0):
        return self.chip(dy, dz) * 2 + (self.core + dk) % 2


def send(src, dst, send_sem, recv_sem, device):
    pltpu.make_async_remote_copy(
        src_ref=src,
        dst_ref=dst,
        send_sem=send_sem,
        recv_sem=recv_sem,
        device_id=device,
        device_id_type=MESH,
    ).start()


def arrived(dst, recv_sem):
    pltpu.make_async_copy(dst, dst, recv_sem).wait()


class Gather:
    SENDS = 16

    def __init__(self, place, buf, ssem, rsem, hsem, chunk, chunks, direct):
        self.p, self.buf, self.chunk, self.direct = place, buf, chunk, direct
        self.ssem, self.rsem, self.hsem = ssem, rsem, hsem
        self.rows = buf.shape[1] // chunks
        self.first = chunk * self.rows
        self.sent = []

    def _part(self, slot):
        return self.buf.at[slot, pl.ds(self.first, self.rows)]

    def _half_part(self, slot, which):
        half = self.rows // 2
        return self.buf.at[slot, pl.ds(self.first + which * half, half)]

    def _send(self, src, recv_sem, target):
        sem = self.ssem.at[self.chunk, len(self.sent)]
        send(src, src, sem, recv_sem, {"tensor": target})
        self.sent.append(src.shape[0])

    def _full(self, slot, target):
        self._send(self._part(slot), self.rsem.at[self.chunk, slot], target)

    def _half(self, slot, which, target):
        self._send(self._half_part(slot, which), self.hsem.at[self.chunk, which], target)

    def start(self):
        p = self.p
        for target in (p.slot(0, 1), p.slot(0, 3), p.slot(1, 0), p.slot(0, 0, 1)):
            self._full(p.me, target)

    def start_far(self):
        self._full(self.p.me, self.p.slot(0, 2))

    def event(self, index):
        p = self.p
        dy, dz = GATHER_ORDER[index]
        slot = p.slot(dy, dz)
        if (dy, dz) == (0, 2) and not self.direct:
            for which in (0, 1):
                arrived(self._half_part(slot, which), self.hsem.at[self.chunk, which])
        else:
            arrived(self._part(slot), self.rsem.at[self.chunk, slot])
        if (dy, dz) == (0, 2):
            self._full(slot, p.slot(1, 0))
        elif (dy, dz) == (0, 1) and not self.direct:
            self._half(slot, 1, p.slot(0, 3))
        elif (dy, dz) == (0, 3) and not self.direct:
            self._half(slot, 0, p.slot(0, 1))
        elif (dy, dz) == (1, 0):
            self._full(slot, p.slot(0, 1))
            self._full(slot, p.slot(0, 3))
        self._full(slot, p.slot(0, 0, 1))

    def partner_wait(self, chip):
        slot = chip * 2 + (self.p.core + 1) % 2
        arrived(self._part(slot), self.rsem.at[self.chunk, slot])

    def drain(self):
        for index, rows in enumerate(self.sent):
            arrived(self.buf.at[0, pl.ds(0, rows)], self.ssem.at[self.chunk, index])

    @staticmethod
    def scratch(rows, chunks):
        return [
            pltpu.VMEM((16, rows, D), BF16),
            pltpu.SemaphoreType.DMA((chunks, Gather.SENDS)),
            pltpu.SemaphoreType.DMA((chunks, 16)),
            pltpu.SemaphoreType.DMA((chunks, 2)),
        ]

    @staticmethod
    def make(place, refs, chunks, direct=False):
        return [Gather(place, *refs, chunk, chunks, direct) for chunk in range(chunks)]


class Scatter:
    SENDS = 10

    def __init__(self, place, chunks, direct, part, xbuf, yfar, relay, fin, finy, ysend, yrec, *sems):
        self.p, self.chunks, self.direct = place, chunks, direct
        self.part, self.xbuf, self.yfar, self.relay = part, xbuf, yfar, relay
        self.fin, self.finy, self.ysend, self.yrec = fin, finy, ysend, yrec
        self.psem, self.xsem, self.ssem = sems[:3]
        self.yfar_sem, self.relay_sem, self.fin_sem, self.finy_sem, self.yrec_sem = sems[3:]
        self.rows = part.shape[1] // chunks
        self.half = self.rows // 2
        self.sent = {}

    @staticmethod
    def scratch(rows, chunks):
        return [
            pltpu.VMEM((16, rows, D), BF16),
            pltpu.VMEM((8, rows, D), BF16),
            pltpu.VMEM((rows, D), BF16),
            pltpu.VMEM((rows, D), BF16),
            pltpu.VMEM((2, rows, D), BF16),
            pltpu.VMEM((2, rows, D), BF16),
            pltpu.VMEM((rows, D), BF16),
            pltpu.VMEM((rows, D), BF16),
            pltpu.SemaphoreType.DMA((8,)),
            pltpu.SemaphoreType.DMA((8,)),
            pltpu.SemaphoreType.DMA((chunks * Scatter.SENDS,)),
            pltpu.SemaphoreType.DMA((chunks,)),
            pltpu.SemaphoreType.DMA((chunks, 2)),
            pltpu.SemaphoreType.DMA((chunks, 2, 2)),
            pltpu.SemaphoreType.DMA((chunks, 2)),
            pltpu.SemaphoreType.DMA((chunks,)),
        ]

    def partner_send(self, chip):
        slot = chip * 2 + (self.p.core + 1) % 2
        send(
            self.part.at[slot],
            self.xbuf.at[chip],
            self.psem.at[chip],
            self.xsem.at[chip],
            {"tensor": self.p.slot(0, 0, 1)},
        )

    def partner_add(self, chip):
        arrived(self.xbuf.at[chip], self.xsem.at[chip])
        slot = chip * 2 + self.p.core
        self.part[slot] = self.part[slot] + self.xbuf[chip]

    def _send(self, key, src, dst, recv_sem, target):
        index, _ = self.sent.setdefault(key, (len(self.sent), src.shape[0]))
        send(src, dst, self.ssem.at[index], recv_sem, {"tensor": target})

    def all_rows(self, chunk):
        return pl.ds(chunk * self.rows, self.rows)

    def half_rows(self, chunk, which):
        return pl.ds(chunk * self.rows + which * self.half, self.half)

    def send_yfar(self):
        slot = self.p.slot(1, 2)
        for chunk in range(self.chunks):
            rows = self.all_rows(chunk)
            self._send(
                ("yfar", chunk),
                self.part.at[slot, rows],
                self.yfar.at[rows],
                self.yfar_sem.at[chunk],
                self.p.slot(1, 0),
            )

    def send_side(self, way):
        dz = (1, 3)[way]
        slot = self.p.slot(1, dz)
        for chunk in range(self.chunks):
            rows = self.all_rows(chunk)
            self._send(
                ("side", chunk, way),
                self.part.at[slot, rows],
                self.finy.at[way, rows],
                self.finy_sem.at[chunk, way],
                self.p.slot(0, dz),
            )

    def _near(self, chunk, way, which):
        dz = (1, 3)[way]
        rows = self.half_rows(chunk, which)
        self._send(
            ("near", chunk, way, which),
            self.part.at[self.p.slot(0, dz), rows],
            self.fin.at[way, rows],
            self.fin_sem.at[chunk, way, which],
            self.p.slot(0, dz),
        )

    def send_near(self, chunk, ways=(0, 1)):
        for way in ways:
            for which in (0, 1):
                self._near(chunk, way, which)

    def send_role(self, chip):
        p = self.p
        dy, dz = (chip // 4 + p.y) % 2, (chip % 4 + 4 - p.z) % 4

        def when(row, column, action):
            @pl.when(jnp.logical_and(dy == row, dz == column))
            def _():
                action()

        when(1, 2, self.send_yfar)
        for way, column in ((0, 1), (1, 3)):
            when(1, column, functools.partial(self.send_side, way))
            when(0, column, lambda way=way: [self.send_near(c, (way,)) for c in range(self.chunks)])

    def far(self, chunk):
        rows = self.all_rows(chunk)
        slot = self.p.slot(0, 2)
        arrived(self.yfar.at[rows], self.yfar_sem.at[chunk])
        self.part[slot, rows, :] = self.part[slot, rows, :] + self.yfar[rows, :]
        if self.direct:
            self._send(
                ("far", chunk),
                self.part.at[slot, rows],
                self.relay.at[rows],
                self.relay_sem.at[chunk, 0],
                slot,
            )
            return
        self._near(chunk, 0, 1)
        self._near(chunk, 1, 0)
        for way in (0, 1):
            self._send(
                ("far", chunk, way),
                self.part.at[slot, self.half_rows(chunk, way)],
                self.relay.at[self.half_rows(chunk, way)],
                self.relay_sem.at[chunk, way],
                self.p.slot(0, (1, 3)[way]),
            )

    def cross_sum(self, chunk):
        rows = self.all_rows(chunk)
        for way in (0, 1):
            arrived(self.finy.at[way, rows], self.finy_sem.at[chunk, way])
        total = self.part[self.p.slot(1, 0), rows, :].astype(F32)
        total = total + self.finy[0, rows, :].astype(F32) + self.finy[1, rows, :].astype(F32)
        self.ysend[rows, :] = total.astype(BF16)

    def cross_send(self, chunk):
        rows = self.all_rows(chunk)
        self._send(
            ("cross", chunk),
            self.ysend.at[rows],
            self.yrec.at[rows],
            self.yrec_sem.at[chunk],
            self.p.slot(1, 0),
        )

    def relay_add(self, chunk):
        for way in (0, 1):
            slot, rows = self.p.slot(0, (1, 3)[way]), self.half_rows(chunk, way)
            arrived(self.relay.at[rows], self.relay_sem.at[chunk, way])
            self.part[slot, rows, :] = self.part[slot, rows, :] + self.relay[rows, :]

    def relay_send(self, chunk):
        for way in (0, 1):
            self._near(chunk, way, way)

    def total(self, chunk):
        rows = self.all_rows(chunk)
        for way in (0, 1):
            for which in (0, 1):
                arrived(
                    self.fin.at[way, self.half_rows(chunk, which)],
                    self.fin_sem.at[chunk, way, which],
                )
        own = self.part[self.p.me, rows, :].astype(F32)
        own = own + self.fin[0, rows, :].astype(F32) + self.fin[1, rows, :].astype(F32)
        if self.direct:
            arrived(self.relay.at[rows], self.relay_sem.at[chunk, 0])
            own = own + self.relay[rows, :].astype(F32)
        arrived(self.yrec.at[rows], self.yrec_sem.at[chunk])
        return own + self.yrec[rows, :].astype(F32)

    def run(self, *stages):
        if self.direct:
            steps = (self.cross_sum, self.cross_send) + stages
        else:
            steps = (
                self.far,
                self.cross_sum,
                lambda chunk: (self.cross_send(chunk), self.relay_add(chunk)),
                self.relay_send,
            ) + stages
        for time in range(self.chunks + len(steps) - 1):
            for index, stage in enumerate(steps):
                if 0 <= time - index < self.chunks:
                    stage(time - index)

    def drain(self):
        for chip in range(8):
            slot = chip * 2 + (self.p.core + 1) % 2
            arrived(self.part.at[slot], self.psem.at[chip])
        for index, rows in self.sent.values():
            arrived(self.part.at[0, pl.ds(0, rows)], self.ssem.at[index])


def dot(left, right):
    return jnp.dot(left, right, preferred_element_type=F32)


def dot_t(left, right):
    return lax.dot_general(left, right, (((1,), (1,)), ((), ())), preferred_element_type=F32)


def softmax_weights(scores):
    row_max = jnp.max(scores, axis=-1, keepdims=True)
    exponent = jnp.exp(scores - row_max)
    return (exponent * (1.0 / jnp.sum(exponent, axis=-1, keepdims=True))).astype(BF16)


def layer_kernel(*refs):
    refs = list(refs)

    def take(count):
        taken, refs[:count] = refs[:count], []
        return taken

    small_hbm, hbm = take(11), take(10)
    memory_out, dec_out = take(2)
    small = take(10)
    lengths, gain, bias, mem_gain, dec_tokens = small[:5]
    tags, table, cross_gain, ffn_gain, tgt_length = small[5:]
    (small_sem,) = take(1)
    weights = take(10)
    (weight_sem,) = take(1)
    wq, wk, wv, wo, cq, ck, cv, co, win, wout = weights
    grid, q_s, k_s, v_s, s_s, w_s, ctx = take(7)
    hop, back_sem, swap_sem = take(3)
    inp, q_all, cross_ctx, act, hidden = take(5)
    place = Place()
    enc_refs, mem_refs, dec_refs, ffn_refs = take(4), take(4), take(4), take(4)
    enc = Gather.make(place, enc_refs, ROW_CHUNKS)
    mem = Gather.make(place, mem_refs, MEM_CHUNKS)
    (dec,) = Gather.make(place, dec_refs, 1)
    ffn = Gather.make(place, ffn_refs, DEC_CHUNKS, True)
    enc_sum = Scatter(place, ENC_CHUNKS, True, *take(16))
    cross_sum = Scatter(place, DEC_CHUNKS, True, *take(16))
    ffn_sum = Scatter(place, DEC_CHUNKS, True, *take(16))

    def events(gathers, *numbers):
        for gather in gathers:
            for number in numbers:
                gather.event(number)

    loads = [
        pltpu.make_async_copy(src, dst, weight_sem.at[index])
        for index, (src, dst) in enumerate(zip(hbm, weights))
    ]
    owner = place.slot(0, 4 - place.x)
    enc_buf, mem_buf, dec_buf, ffn_buf = enc_refs[0], mem_refs[0], dec_refs[0], ffn_refs[0]
    fetch = [
        pltpu.make_async_copy(src, dst, small_sem.at[index])
        for index, (src, dst) in enumerate(zip(small_hbm[1:], small))
    ]
    own_rows = pltpu.make_async_copy(small_hbm[0].at[0], enc_buf.at[place.me], small_sem.at[10])
    own_rows.start()
    for copy in fetch:
        copy.start()
    for load in loads[:4]:
        load.start()
    swap_dp = ((place.z + 4 - place.x) % 4) * 2 + place.core
    swap_t = place.y * 8 + place.z * 2 + place.y_lo
    stays = jnp.logical_and(swap_dp == place.dp, swap_t == place.me)
    moves = jnp.logical_not(stays)

    barrier = pltpu.get_barrier_semaphore()
    for target in (
        place.slot(0, 0, 1),
        place.slot(0, 1),
        place.slot(0, 3),
        place.slot(0, 2),
        place.slot(1, 0),
    ):
        pl.semaphore_signal(barrier, inc=1, device_id={"tensor": target}, device_id_type=MESH)

    @pl.when(moves)
    def _():
        pl.semaphore_signal(barrier, inc=1, device_id=(swap_dp, swap_t), device_id_type=MESH)

    own_rows.wait()

    @pl.when(moves)
    def _():
        pl.semaphore_wait(barrier, 6)

    @pl.when(stays)
    def _():
        pl.semaphore_wait(barrier, 5)

    for gather in enc:
        gather.start()
    for copy in fetch:
        copy.wait()
    tag = tags[place.me]
    lang = jnp.zeros((1, D), F32)
    for index in range(LANGS):
        lang = jnp.where(tag == index, table[index : index + 1, :].astype(F32), lang)
    value = dec_tokens[0].astype(F32) + lang
    inp[...] = value
    dec_buf[place.me] = rms(value, cross_gain[...]).astype(BF16)

    keys = lax.broadcasted_iota(jnp.int32, (SRC, SRC), 1)
    bucket = jnp.clip(keys - lax.broadcasted_iota(jnp.int32, (SRC, SRC), 0), -MAXREL, MAXREL) + MAXREL
    for head in range(HEADS):
        values = jnp.zeros((SRC, SRC), F32)
        for index in range(NB):
            values = jnp.where(bucket == index, bias[head, index], values)
        grid[head] = values
    for load in loads[:4]:
        load.wait()

    items = [(ex, head) for ex in range(2) for head in range(HEADS)]

    def sum_chip(index):
        chip = chip_at(place, GATHER_ORDER, index)
        return chip // 4 * 4 + (chip % 4 + place.x) % 4

    def enc_step(index, carry):
        @pl.when(index == 1)
        def _():
            events(enc, 1, 2, 3)
            for load in loads[4:]:
                load.start()

        @pl.when(index == 4)
        def _():
            events(enc, 4, 5, 6)

        @pl.when(index == 7)
        def _():
            events(enc, 7)

        def attend():
            chip = chip_at(place, GATHER_ORDER, index)
            for gather in enc:
                gather.partner_wait(chip)
            raw = enc_buf[pl.ds(chip * 2, 2)].reshape(2 * SRC, D)
            rows = rms(raw.astype(F32), gain[...]).astype(BF16)
            q_s[...] = dot(rows, wq[...]).astype(BF16)
            k_s[...] = dot(rows, wk[...]).astype(BF16)
            v_s[...] = dot(rows, wv[...]).astype(BF16)
            columns = lax.broadcasted_iota(jnp.int32, (SRC, SRC), 1)
            for item, (ex, head) in enumerate(items):
                here, cols = slice(ex * SRC, (ex + 1) * SRC), slice(head * HD, (head + 1) * HD)
                s_s[item] = dot_t(q_s[here, cols], k_s[here, cols])
            for item, (ex, head) in enumerate(items):
                length = lengths[place.dp * 16 + chip * 2 + ex]
                scores = s_s[item] * SCALE + grid[head]
                w_s[item] = softmax_weights(jnp.where(columns < length, scores, NEG_FILL))
            for item, (ex, head) in enumerate(items):
                here, cols = slice(ex * SRC, (ex + 1) * SRC), slice(head * HD, (head + 1) * HD)
                ctx[here, cols] = dot(w_s[item], v_s[here, cols]).astype(BF16)

        attend()

        @pl.when(index > 1)
        def _():
            done = sum_chip(index - 2)
            enc_sum.partner_add(done)
            enc_sum.send_role(done)

        terms = dot(ctx[...], wo[...]).astype(BF16).reshape(2, SRC, D)
        enc_sum.part[pl.ds(sum_chip(index) * 2, 2)] = terms

        @pl.when(index > 0)
        def _():
            enc_sum.partner_send(sum_chip(index - 1))

        return carry

    lax.fori_loop(0, 8, enc_step, 0)
    enc_sum.partner_send(sum_chip(7))
    for index in (6, 7):
        done = sum_chip(index)
        enc_sum.partner_add(done)
        enc_sum.send_role(done)
    for chunk in range(ENC_CHUNKS):
        enc_sum.far(chunk)
    dec.start()

    def finish_memory(chunk):
        rows = enc_sum.all_rows(chunk)
        value = enc_buf[owner, rows, :].astype(F32) + enc_sum.total(chunk)
        hop[rows, :] = rms(value, mem_gain[...]).astype(BF16)

    def give_back():
        @pl.when(place.x == 0)
        def _():
            pltpu.make_async_copy(hop, memory_out.at[0], back_sem.at[1]).start()

        @pl.when(place.x > 0)
        def _():
            send(hop, memory_out.at[0], back_sem.at[0], back_sem.at[1], {"tensor": owner})

    def swap_send(chunk):
        rows = enc_sum.all_rows(chunk)

        if chunk == ENC_CHUNKS - 1:
            events([dec], 1, 2, 3)

        @pl.when(stays)
        def _():
            pltpu.make_async_copy(
                hop.at[rows], mem_buf.at[place.me, rows], swap_sem.at[1, chunk]
            ).start()

        @pl.when(moves)
        def _():
            send(
                hop.at[rows],
                mem_buf.at[swap_t, rows],
                swap_sem.at[0, chunk],
                swap_sem.at[1, chunk],
                (swap_dp, swap_t),
            )

    def spread(chunk):
        rows = enc_sum.all_rows(chunk)
        arrived(mem_buf.at[place.me, rows], swap_sem.at[1, chunk])
        each = ENC_CHUNKS // MEM_CHUNKS
        if chunk % each == each - 1:
            mem[chunk // each].start()

    enc_sum.run(finish_memory, swap_send, spread)
    events([dec], 4, 5, 6, 7)

    for chip in range(8):
        dec.partner_wait(chip)
    for load in loads[4:8]:
        load.wait()

    def q_step(index, carry):
        rows = dec_buf[pl.ds(index * 4, 4)].reshape(4 * TGT, D)
        q_all[pl.ds(index * 4, 4)] = dot(rows, cq[...]).astype(BF16).reshape(4, TGT, HW)
        return carry

    lax.fori_loop(0, 4, q_step, 0)

    def cross_chip(dz):
        return (place.z + dz + 4 - place.x) % 4 * 2

    def sum_cross(dz):
        for chip in (cross_chip(dz), cross_chip(dz) + 1):
            cross_sum.partner_add(chip)
            cross_sum.send_role(chip)

    def cross_step(index, carry):
        @pl.when(index == 1)
        def _():
            events(mem, 1, 2, 3)

        @pl.when(index == 4)
        def _():
            events(mem, 4, 5, 6)

        @pl.when(index == 7)
        def _():
            events(mem, 7)

        chip = chip_at(place, GATHER_ORDER, index)
        for gather in mem:
            gather.partner_wait(chip)
        rows = mem_buf[pl.ds(chip * 2, 2)].reshape(2 * SRC, D)
        k_s[...] = dot(rows, ck[...]).astype(BF16)
        v_s[...] = dot(rows, cv[...]).astype(BF16)
        columns = lax.broadcasted_iota(jnp.int32, (TGT, SRC), 1)
        base = ((chip % 4 + 4 - place.x) % 4) * 4 + chip // 4
        for item, (ex, head) in enumerate(items):
            here, cols = slice(ex * SRC, (ex + 1) * SRC), slice(head * HD, (head + 1) * HD)
            s_s[item, :TGT, :] = dot_t(q_all[base + 2 * ex, :, cols], k_s[here, cols])
        for item, (ex, head) in enumerate(items):
            row = base + 2 * ex
            length = lengths[(row // 2) * 16 + (row % 2) * 8 + place.dp]
            scores = s_s[item, :TGT, :] * SCALE
            w_s[item, :TGT, :] = softmax_weights(jnp.where(columns < length, scores, NEG_FILL))
        for item, (ex, head) in enumerate(items):
            here, cols = slice(ex * SRC, (ex + 1) * SRC), slice(head * HD, (head + 1) * HD)
            cross_ctx[base + 2 * ex, :, cols] = dot(w_s[item, :TGT, :], v_s[here, cols]).astype(BF16)

        @pl.when(jnp.logical_or(index == 3, index > 4))
        def _():
            @pl.when(index > 3)
            def _():
                sum_cross((PAIR_BEFORE >> (2 * index)) & 3)

            first = cross_chip((PAIR_DZ >> (2 * index)) & 3)
            block = cross_ctx[pl.ds(first * 2, 4)].reshape(4 * TGT, HW)
            cross_sum.part[pl.ds(first * 2, 4)] = dot(block, co[...]).astype(BF16).reshape(4, TGT, D)
            cross_sum.partner_send(first)
            cross_sum.partner_send(first + 1)

        return carry

    lax.fori_loop(0, 8, cross_step, 0)
    sum_cross(2)
    for chunk in range(DEC_CHUNKS):
        cross_sum.far(chunk)

    def finish_hidden(chunk):
        rows = cross_sum.all_rows(chunk)
        value = inp[rows, :] + cross_sum.total(chunk)
        hidden[rows, :] = value
        ffn_buf[place.me, rows, :] = rms(value, ffn_gain[...]).astype(BF16)

    cross_sum.run(finish_hidden, lambda chunk: ffn[chunk].start())
    for gather in ffn:
        gather.start_far()
    for load in loads[8:]:
        load.wait()

    def ffn_chips(chips):
        rows = [ffn_buf[pl.ds(chip * 2, 2)].reshape(2 * TGT, D) for chip in chips]
        rows = rows[0] if len(chips) == 1 else jnp.concatenate(rows, axis=0)
        count = rows.shape[0]
        for tile in range(FF // 512):
            cols = slice(tile * 512, (tile + 1) * 512)
            act[:count, cols] = jnp.maximum(dot(rows, win[:, cols]), 0.0).astype(BF16)
        yield
        for tile in range(D // 256):
            cols = slice(tile * 256, (tile + 1) * 256)
            result = dot(act[:count, :], wout[:, cols]).astype(BF16)
            for index, chip in enumerate(chips):
                here = slice(index * 2 * TGT, (index + 1) * 2 * TGT)
                ffn_sum.part[pl.ds(chip * 2, 2), :, cols] = result[here].reshape(2, TGT, 256)
        for chip in chips:
            ffn_sum.partner_send(chip)

    def ready(*chips):
        for chip in chips:
            for gather in ffn:
                gather.partner_wait(chip)

    own = place.chip(0, 0)
    ready(own)
    for _ in ffn_chips([own]):
        pass

    def ffn_step(index, carry):
        @pl.when(index == 0)
        def _():
            events(ffn, 1, 2, 3)

        @pl.when(index == 1)
        def _():
            events(ffn, 4, 5, 6)

        @pl.when(index == 2)
        def _():
            events(ffn, 7)
            ready(place.chip(0, 3))

        chips = [chip_at(place, FFN_ORDER, index * 2 + item) for item in range(2)]
        ready(*chips)
        halfway = ffn_chips(chips)
        next(halfway)

        @pl.when(index == 0)
        def _():
            ffn_sum.partner_add(own)

        @pl.when(index > 0)
        def _():
            for item in range(2):
                ffn_sum.partner_add(chip_at(place, FFN_ORDER, index * 2 - 2 + item))

        @pl.when(index == 1)
        def _():
            for chunk in range(DEC_CHUNKS):
                ffn_sum.send_near(chunk, (0,))

        @pl.when(index == 2)
        def _():
            ffn_sum.send_side(0)
            ffn_sum.send_side(1)

        for _ in halfway:
            pass
        return carry

    lax.fori_loop(0, 3, ffn_step, 0)
    last = ffn_chips([place.chip(0, 3)])
    next(last)
    for item in (4, 5):
        ffn_sum.partner_add(place.chip(*FFN_ORDER[item]))
    ffn_sum.send_yfar()
    for _ in last:
        pass
    for chunk in range(DEC_CHUNKS):
        ffn_sum.far(chunk)
    ffn_sum.partner_add(place.chip(0, 3))
    for chunk in range(DEC_CHUNKS):
        ffn_sum.send_near(chunk, (1,))
    give_back()

    def finish_out(chunk):
        rows = ffn_sum.all_rows(chunk)
        value = hidden[rows, :] + ffn_sum.total(chunk)
        position = lax.broadcasted_iota(jnp.int32, value.shape, 0) + chunk * ffn_sum.rows
        dec_out[0, rows, :] = jnp.where(position < tgt_length[0], value, 0.0).astype(BF16)

    ffn_sum.run(finish_out)

    arrived(memory_out.at[0], back_sem.at[1])

    @pl.when(place.x > 0)
    def _():
        arrived(hop, back_sem.at[0])

    @pl.when(moves)
    def _():
        for chunk in range(ENC_CHUNKS):
            arrived(hop.at[enc_sum.all_rows(chunk)], swap_sem.at[0, chunk])

    for stage in [*enc, dec, *mem, *ffn, enc_sum, cross_sum, ffn_sum]:
        stage.drain()


def leave_kernel(memory, dec, memory_out, dec_out):
    memory_out[...] = memory[...]
    dec_out[...] = dec[...]


VM = pltpu.VMEM
SM = pltpu.SMEM


def on_device(
    enc_tokens,
    src_lengths,
    enc_gain,
    enc_query,
    enc_key,
    enc_value,
    enc_output,
    enc_bias,
    mem_gain,
    dec_tokens,
    tgt_lengths,
    lang_tags,
    lang_table,
    cross_gain,
    cross_query,
    cross_key,
    cross_value,
    cross_output,
    ffn_gain,
    ffn_in,
    ffn_out,
):
    weights = [
        enc_query,
        enc_key,
        enc_value,
        enc_output,
        cross_query,
        cross_key,
        cross_value,
        cross_output,
        ffn_in,
        ffn_out,
    ]
    small = [
        enc_tokens,
        src_lengths,
        enc_gain,
        enc_bias,
        mem_gain,
        dec_tokens,
        lang_tags,
        lang_table,
        cross_gain,
        ffn_gain,
        tgt_lengths,
    ]
    spaces = [SM, VM, SM, VM, VM, SM, VM, VM, VM, SM]
    scratch = [space(value.shape, value.dtype) for space, value in zip(spaces, small[1:])]
    scratch += [pltpu.SemaphoreType.DMA((len(small),))]
    scratch += [pltpu.VMEM(weight.shape, BF16) for weight in weights]
    scratch += [
        pltpu.SemaphoreType.DMA((len(weights),)),
        pltpu.VMEM((HEADS, SRC, SRC), F32),
        pltpu.VMEM((2 * SRC, HW), BF16),
        pltpu.VMEM((2 * SRC, HW), BF16),
        pltpu.VMEM((2 * SRC, HW), BF16),
        pltpu.VMEM((2 * HEADS, SRC, SRC), F32),
        pltpu.VMEM((2 * HEADS, SRC, SRC), BF16),
        pltpu.VMEM((2 * SRC, HW), BF16),
        pltpu.VMEM((SRC, D), BF16),
        pltpu.SemaphoreType.DMA((2,)),
        pltpu.SemaphoreType.DMA((2, ENC_CHUNKS)),
        pltpu.VMEM((TGT, D), F32),
        pltpu.VMEM((16, TGT, HW), BF16),
        pltpu.VMEM((16, TGT, HW), BF16),
        pltpu.VMEM((4 * TGT, FF), BF16),
        pltpu.VMEM((TGT, D), F32),
    ]
    scratch += Gather.scratch(SRC, ROW_CHUNKS)
    scratch += Gather.scratch(SRC, MEM_CHUNKS)
    scratch += Gather.scratch(TGT, 1)
    scratch += Gather.scratch(TGT, DEC_CHUNKS)
    scratch += Scatter.scratch(SRC, ENC_CHUNKS)
    scratch += Scatter.scratch(TGT, DEC_CHUNKS)
    scratch += Scatter.scratch(TGT, DEC_CHUNKS)
    memory, dec = pl.pallas_call(
        layer_kernel,
        out_shape=(
            jax.ShapeDtypeStruct((1, SRC, D), BF16),
            jax.ShapeDtypeStruct((1, TGT, D), BF16),
        ),
        in_specs=[pl.BlockSpec(memory_space=pl.ANY)] * (len(small) + len(weights)),
        out_specs=(pl.BlockSpec(memory_space=VM), pl.BlockSpec(memory_space=VM)),
        scratch_shapes=scratch,
        compiler_params=pltpu.CompilerParams(
            collective_id=1, has_side_effects=True, vmem_limit_bytes=67_043_328
        ),
    )(*small, *weights)
    return pl.pallas_call(
        leave_kernel,
        out_shape=(
            jax.ShapeDtypeStruct(memory.shape, BF16),
            jax.ShapeDtypeStruct(dec.shape, BF16),
        ),
        in_specs=[pl.BlockSpec(memory_space=VM)] * 2,
        out_specs=(pl.BlockSpec(memory_space=VM), pl.BlockSpec(memory_space=VM)),
    )(memory, dec)


def solution(mesh):
    in_specs = (
        P(("dp", "tensor"), None, None),
        P(),
        P(),
        P(None, "tensor"),
        P(None, "tensor"),
        P(None, "tensor"),
        P("tensor", None),
        P("tensor", None),
        P(),
        P(("dp", "tensor"), None, None),
        P(("dp", "tensor")),
        P("dp"),
        P(),
        P(),
        P(None, "tensor"),
        P(None, "tensor"),
        P(None, "tensor"),
        P("tensor", None),
        P(),
        P(None, "tensor"),
        P("tensor", None),
    )
    out_specs = (P(("dp", "tensor"), None, None), P(("dp", "tensor"), None, None))
    return jax.shard_map(
        on_device, mesh=mesh, in_specs=in_specs, out_specs=out_specs, check_vma=False
    )
```

```python
import functools

import jax
import jax.numpy as jnp
from jax import lax
from jax.experimental import pallas as pl
from jax.experimental.pallas import tpu as pltpu
from jax.sharding import PartitionSpec as P

D = 1024
HD = 128
SRC = 128
TGT = 64
MAXREL = 16
NB = 33
LANGS = 8
HEADS = 4
HW = HEADS * HD
FF = 2048
EPSILON = 1e-06
NEG_FILL = -1e30
SCALE = HD ** (-0.5)
MESH = pl.DeviceIdType.MESH
F32 = jnp.float32
BF16 = jnp.bfloat16

GATHER_ORDER = ((0, 0), (0, 1), (0, 3), (1, 0), (0, 2), (1, 1), (1, 3), (1, 2))
FFN_ORDER = ((0, 1), (1, 0), (1, 1), (1, 3), (1, 2), (0, 2))
PAIR_DZ = 0 << 6 | 1 << 10 | 3 << 12 | 2 << 14
PAIR_BEFORE = 0 << 10 | 1 << 12 | 3 << 14
ROW_CHUNKS = 2
ENC_CHUNKS = 4
MEM_CHUNKS = 2
DEC_CHUNKS = 2


def packed(order):
    return (
        sum(dy << i for i, (dy, dz) in enumerate(order)),
        sum(dz << (2 * i) for i, (dy, dz) in enumerate(order)),
    )


def chip_at(place, order, index):
    dy_bits, dz_bits = packed(order)
    return place.chip((dy_bits >> index) & 1, (dz_bits >> (2 * index)) & 3)


def rms(values, gain):
    mean_sq = jnp.mean(values * values, axis=-1, keepdims=True)
    return values * lax.rsqrt(mean_sq + EPSILON) * gain


class Place:
    def __init__(self):
        self.me = lax.axis_index("tensor")
        self.dp = lax.axis_index("dp")
        self.core = self.me % 2
        self.z = (self.me // 2) % 4
        self.y = self.me // 8
        self.x = self.dp // 2
        self.y_lo = self.dp % 2

    def chip(self, dy, dz):
        return ((self.y + dy) % 2) * 4 + (self.z + dz) % 4

    def slot(self, dy, dz, dk=0):
        return self.chip(dy, dz) * 2 + (self.core + dk) % 2


def send(src, dst, send_sem, recv_sem, device):
    pltpu.make_async_remote_copy(
        src_ref=src,
        dst_ref=dst,
        send_sem=send_sem,
        recv_sem=recv_sem,
        device_id=device,
        device_id_type=MESH,
    ).start()


def arrived(dst, recv_sem):
    pltpu.make_async_copy(dst, dst, recv_sem).wait()


class Gather:
    SENDS = 16

    def __init__(self, place, buf, ssem, rsem, hsem, chunk, chunks, direct):
        self.p, self.buf, self.chunk, self.direct = place, buf, chunk, direct
        self.ssem, self.rsem, self.hsem = ssem, rsem, hsem
        self.rows = buf.shape[1] // chunks
        self.first = chunk * self.rows
        self.sent = []

    def _part(self, slot):
        return self.buf.at[slot, pl.ds(self.first, self.rows)]

    def _half_part(self, slot, which):
        half = self.rows // 2
        return self.buf.at[slot, pl.ds(self.first + which * half, half)]

    def _send(self, src, recv_sem, target):
        sem = self.ssem.at[self.chunk, len(self.sent)]
        send(src, src, sem, recv_sem, {"tensor": target})
        self.sent.append(src.shape[0])

    def _full(self, slot, target):
        self._send(self._part(slot), self.rsem.at[self.chunk, slot], target)

    def _half(self, slot, which, target):
        self._send(self._half_part(slot, which), self.hsem.at[self.chunk, which], target)

    def start(self):
        p = self.p
        for target in (p.slot(0, 1), p.slot(0, 3), p.slot(1, 0), p.slot(0, 0, 1)):
            self._full(p.me, target)

    def start_far(self):
        self._full(self.p.me, self.p.slot(0, 2))

    def event(self, index):
        p = self.p
        dy, dz = GATHER_ORDER[index]
        slot = p.slot(dy, dz)
        if (dy, dz) == (0, 2) and not self.direct:
            for which in (0, 1):
                arrived(self._half_part(slot, which), self.hsem.at[self.chunk, which])
        else:
            arrived(self._part(slot), self.rsem.at[self.chunk, slot])
        if (dy, dz) == (0, 2):
            self._full(slot, p.slot(1, 0))
        elif (dy, dz) == (0, 1) and not self.direct:
            self._half(slot, 1, p.slot(0, 3))
        elif (dy, dz) == (0, 3) and not self.direct:
            self._half(slot, 0, p.slot(0, 1))
        elif (dy, dz) == (1, 0):
            self._full(slot, p.slot(0, 1))
            self._full(slot, p.slot(0, 3))
        self._full(slot, p.slot(0, 0, 1))

    def partner_wait(self, chip):
        slot = chip * 2 + (self.p.core + 1) % 2
        arrived(self._part(slot), self.rsem.at[self.chunk, slot])

    def drain(self):
        for index, rows in enumerate(self.sent):
            arrived(self.buf.at[0, pl.ds(0, rows)], self.ssem.at[self.chunk, index])

    @staticmethod
    def scratch(rows, chunks):
        return [
            pltpu.VMEM((16, rows, D), BF16),
            pltpu.SemaphoreType.DMA((chunks, Gather.SENDS)),
            pltpu.SemaphoreType.DMA((chunks, 16)),
            pltpu.SemaphoreType.DMA((chunks, 2)),
        ]

    @staticmethod
    def make(place, refs, chunks, direct=False):
        return [Gather(place, *refs, chunk, chunks, direct) for chunk in range(chunks)]


class Scatter:
    SENDS = 10

    def __init__(self, place, chunks, direct, part, xbuf, yfar, relay, fin, finy, ysend, yrec, *sems):
        self.p, self.chunks, self.direct = place, chunks, direct
        self.part, self.xbuf, self.yfar, self.relay = part, xbuf, yfar, relay
        self.fin, self.finy, self.ysend, self.yrec = fin, finy, ysend, yrec
        self.psem, self.xsem, self.ssem = sems[:3]
        self.yfar_sem, self.relay_sem, self.fin_sem, self.finy_sem, self.yrec_sem = sems[3:]
        self.rows = part.shape[1] // chunks
        self.half = self.rows // 2
        self.sent = {}

    @staticmethod
    def scratch(rows, chunks):
        return [
            pltpu.VMEM((16, rows, D), BF16),
            pltpu.VMEM((8, rows, D), BF16),
            pltpu.VMEM((rows, D), BF16),
            pltpu.VMEM((rows, D), BF16),
            pltpu.VMEM((2, rows, D), BF16),
            pltpu.VMEM((2, rows, D), BF16),
            pltpu.VMEM((rows, D), BF16),
            pltpu.VMEM((rows, D), BF16),
            pltpu.SemaphoreType.DMA((8,)),
            pltpu.SemaphoreType.DMA((8,)),
            pltpu.SemaphoreType.DMA((chunks * Scatter.SENDS,)),
            pltpu.SemaphoreType.DMA((chunks,)),
            pltpu.SemaphoreType.DMA((chunks, 2)),
            pltpu.SemaphoreType.DMA((chunks, 2, 2)),
            pltpu.SemaphoreType.DMA((chunks, 2)),
            pltpu.SemaphoreType.DMA((chunks,)),
        ]

    def partner_send(self, chip):
        slot = chip * 2 + (self.p.core + 1) % 2
        send(
            self.part.at[slot],
            self.xbuf.at[chip],
            self.psem.at[chip],
            self.xsem.at[chip],
            {"tensor": self.p.slot(0, 0, 1)},
        )

    def partner_add(self, chip):
        arrived(self.xbuf.at[chip], self.xsem.at[chip])
        slot = chip * 2 + self.p.core
        self.part[slot] = self.part[slot] + self.xbuf[chip]

    def _send(self, key, src, dst, recv_sem, target):
        index, _ = self.sent.setdefault(key, (len(self.sent), src.shape[0]))
        send(src, dst, self.ssem.at[index], recv_sem, {"tensor": target})

    def all_rows(self, chunk):
        return pl.ds(chunk * self.rows, self.rows)

    def half_rows(self, chunk, which):
        return pl.ds(chunk * self.rows + which * self.half, self.half)

    def send_yfar(self):
        slot = self.p.slot(1, 2)
        for chunk in range(self.chunks):
            rows = self.all_rows(chunk)
            self._send(
                ("yfar", chunk),
                self.part.at[slot, rows],
                self.yfar.at[rows],
                self.yfar_sem.at[chunk],
                self.p.slot(1, 0),
            )

    def send_side(self, way):
        dz = (1, 3)[way]
        slot = self.p.slot(1, dz)
        for chunk in range(self.chunks):
            rows = self.all_rows(chunk)
            self._send(
                ("side", chunk, way),
                self.part.at[slot, rows],
                self.finy.at[way, rows],
                self.finy_sem.at[chunk, way],
                self.p.slot(0, dz),
            )

    def _near(self, chunk, way, which):
        dz = (1, 3)[way]
        rows = self.half_rows(chunk, which)
        self._send(
            ("near", chunk, way, which),
            self.part.at[self.p.slot(0, dz), rows],
            self.fin.at[way, rows],
            self.fin_sem.at[chunk, way, which],
            self.p.slot(0, dz),
        )

    def send_near(self, chunk, ways=(0, 1)):
        for way in ways:
            for which in (0, 1):
                self._near(chunk, way, which)

    def send_role(self, chip):
        p = self.p
        dy, dz = (chip // 4 + p.y) % 2, (chip % 4 + 4 - p.z) % 4

        def when(row, column, action):
            @pl.when(jnp.logical_and(dy == row, dz == column))
            def _():
                action()

        when(1, 2, self.send_yfar)
        for way, column in ((0, 1), (1, 3)):
            when(1, column, functools.partial(self.send_side, way))
            when(0, column, lambda way=way: [self.send_near(c, (way,)) for c in range(self.chunks)])

    def far(self, chunk):
        rows = self.all_rows(chunk)
        slot = self.p.slot(0, 2)
        arrived(self.yfar.at[rows], self.yfar_sem.at[chunk])
        self.part[slot, rows, :] = self.part[slot, rows, :] + self.yfar[rows, :]
        if self.direct:
            self._send(
                ("far", chunk),
                self.part.at[slot, rows],
                self.relay.at[rows],
                self.relay_sem.at[chunk, 0],
                slot,
            )
            return
        self._near(chunk, 0, 1)
        self._near(chunk, 1, 0)
        for way in (0, 1):
            self._send(
                ("far", chunk, way),
                self.part.at[slot, self.half_rows(chunk, way)],
                self.relay.at[self.half_rows(chunk, way)],
                self.relay_sem.at[chunk, way],
                self.p.slot(0, (1, 3)[way]),
            )

    def cross_sum(self, chunk):
        rows = self.all_rows(chunk)
        for way in (0, 1):
            arrived(self.finy.at[way, rows], self.finy_sem.at[chunk, way])
        total = self.part[self.p.slot(1, 0), rows, :].astype(F32)
        total = total + self.finy[0, rows, :].astype(F32) + self.finy[1, rows, :].astype(F32)
        self.ysend[rows, :] = total.astype(BF16)

    def cross_send(self, chunk):
        rows = self.all_rows(chunk)
        self._send(
            ("cross", chunk),
            self.ysend.at[rows],
            self.yrec.at[rows],
            self.yrec_sem.at[chunk],
            self.p.slot(1, 0),
        )

    def relay_add(self, chunk):
        for way in (0, 1):
            slot, rows = self.p.slot(0, (1, 3)[way]), self.half_rows(chunk, way)
            arrived(self.relay.at[rows], self.relay_sem.at[chunk, way])
            self.part[slot, rows, :] = self.part[slot, rows, :] + self.relay[rows, :]

    def relay_send(self, chunk):
        for way in (0, 1):
            self._near(chunk, way, way)

    def total(self, chunk):
        rows = self.all_rows(chunk)
        for way in (0, 1):
            for which in (0, 1):
                arrived(
                    self.fin.at[way, self.half_rows(chunk, which)],
                    self.fin_sem.at[chunk, way, which],
                )
        own = self.part[self.p.me, rows, :].astype(F32)
        own = own + self.fin[0, rows, :].astype(F32) + self.fin[1, rows, :].astype(F32)
        if self.direct:
            arrived(self.relay.at[rows], self.relay_sem.at[chunk, 0])
            own = own + self.relay[rows, :].astype(F32)
        arrived(self.yrec.at[rows], self.yrec_sem.at[chunk])
        return own + self.yrec[rows, :].astype(F32)

    def run(self, *stages):
        if self.direct:
            steps = (self.cross_sum, self.cross_send) + stages
        else:
            steps = (
                self.far,
                self.cross_sum,
                lambda chunk: (self.cross_send(chunk), self.relay_add(chunk)),
                self.relay_send,
            ) + stages
        for time in range(self.chunks + len(steps) - 1):
            for index, stage in enumerate(steps):
                if 0 <= time - index < self.chunks:
                    stage(time - index)

    def drain(self):
        for chip in range(8):
            slot = chip * 2 + (self.p.core + 1) % 2
            arrived(self.part.at[slot], self.psem.at[chip])
        for index, rows in self.sent.values():
            arrived(self.part.at[0, pl.ds(0, rows)], self.ssem.at[index])


def dot(left, right):
    return jnp.dot(left, right, preferred_element_type=F32)


def dot_t(left, right):
    return lax.dot_general(left, right, (((1,), (1,)), ((), ())), preferred_element_type=F32)


def softmax_weights(scores):
    row_max = jnp.max(scores, axis=-1, keepdims=True)
    exponent = jnp.exp(scores - row_max)
    return (exponent * (1.0 / jnp.sum(exponent, axis=-1, keepdims=True))).astype(BF16)


def layer_kernel(*refs):
    refs = list(refs)

    def take(count):
        taken, refs[:count] = refs[:count], []
        return taken

    small_hbm, hbm = take(11), take(10)
    memory_out, dec_out = take(2)
    small = take(10)
    lengths, gain, bias, mem_gain, dec_tokens = small[:5]
    tags, table, cross_gain, ffn_gain, tgt_length = small[5:]
    (small_sem,) = take(1)
    weights = take(10)
    (weight_sem,) = take(1)
    wq, wk, wv, wo, cq, ck, cv, co, win, wout = weights
    grid, q_s, k_s, v_s, s_s, w_s, ctx = take(7)
    hop, back_sem, swap_sem = take(3)
    inp, q_all, cross_ctx, act, hidden = take(5)
    place = Place()
    enc_refs, mem_refs, dec_refs, ffn_refs = take(4), take(4), take(4), take(4)
    enc = Gather.make(place, enc_refs, ROW_CHUNKS)
    mem = Gather.make(place, mem_refs, MEM_CHUNKS)
    (dec,) = Gather.make(place, dec_refs, 1, True)
    ffn = Gather.make(place, ffn_refs, DEC_CHUNKS, True)
    enc_sum = Scatter(place, ENC_CHUNKS, True, *take(16))
    cross_sum = Scatter(place, DEC_CHUNKS, True, *take(16))
    ffn_sum = Scatter(place, DEC_CHUNKS, True, *take(16))

    def events(gathers, *numbers):
        for number in numbers:
            for gather in gathers:
                gather.event(number)

    loads = [
        pltpu.make_async_copy(src, dst, weight_sem.at[index])
        for index, (src, dst) in enumerate(zip(hbm, weights))
    ]
    owner = place.slot(0, 4 - place.x)
    enc_buf, mem_buf, dec_buf, ffn_buf = enc_refs[0], mem_refs[0], dec_refs[0], ffn_refs[0]
    fetch = [
        pltpu.make_async_copy(src, dst, small_sem.at[index])
        for index, (src, dst) in enumerate(zip(small_hbm[1:], small))
    ]
    own_rows = pltpu.make_async_copy(small_hbm[0].at[0], enc_buf.at[place.me], small_sem.at[10])
    own_rows.start()
    for copy in fetch:
        copy.start()
    for load in loads[:4]:
        load.start()
    swap_dp = ((place.z + 4 - place.x) % 4) * 2 + place.core
    swap_t = place.y * 8 + place.z * 2 + place.y_lo
    stays = jnp.logical_and(swap_dp == place.dp, swap_t == place.me)
    moves = jnp.logical_not(stays)

    barrier = pltpu.get_barrier_semaphore()
    for target in (
        place.slot(0, 0, 1),
        place.slot(0, 1),
        place.slot(0, 3),
        place.slot(0, 2),
        place.slot(1, 0),
    ):
        pl.semaphore_signal(barrier, inc=1, device_id={"tensor": target}, device_id_type=MESH)

    @pl.when(moves)
    def _():
        pl.semaphore_signal(barrier, inc=1, device_id=(swap_dp, swap_t), device_id_type=MESH)

    own_rows.wait()

    @pl.when(moves)
    def _():
        pl.semaphore_wait(barrier, 6)

    @pl.when(stays)
    def _():
        pl.semaphore_wait(barrier, 5)

    for gather in enc:
        gather.start()
    for copy in fetch:
        copy.wait()
    tag = tags[place.me]
    lang = jnp.zeros((1, D), F32)
    for index in range(LANGS):
        lang = jnp.where(tag == index, table[index : index + 1, :].astype(F32), lang)
    value = dec_tokens[0].astype(F32) + lang
    inp[...] = value
    dec_buf[place.me] = rms(value, cross_gain[...]).astype(BF16)

    keys = lax.broadcasted_iota(jnp.int32, (SRC, SRC), 1)
    bucket = jnp.clip(keys - lax.broadcasted_iota(jnp.int32, (SRC, SRC), 0), -MAXREL, MAXREL) + MAXREL
    for head in range(HEADS):
        values = jnp.zeros((SRC, SRC), F32)
        for index in range(NB):
            values = jnp.where(bucket == index, bias[head, index], values)
        grid[head] = values
    for load in loads[:4]:
        load.wait()

    items = [(ex, head) for ex in range(2) for head in range(HEADS)]

    def sum_chip(index):
        chip = chip_at(place, GATHER_ORDER, index)
        return chip // 4 * 4 + (chip % 4 + place.x) % 4

    def enc_step(index, carry):
        @pl.when(index == 1)
        def _():
            events(enc, 1, 2, 3)
            for load in loads[4:]:
                load.start()

        @pl.when(index == 4)
        def _():
            events(enc, 4, 5, 6)

        @pl.when(index == 7)
        def _():
            events(enc, 7)

        def attend():
            chip = chip_at(place, GATHER_ORDER, index)
            for gather in enc:
                gather.partner_wait(chip)
            raw = enc_buf[pl.ds(chip * 2, 2)].reshape(2 * SRC, D)
            rows = rms(raw.astype(F32), gain[...]).astype(BF16)
            q_s[...] = dot(rows, wq[...]).astype(BF16)
            k_s[...] = dot(rows, wk[...]).astype(BF16)
            v_s[...] = dot(rows, wv[...]).astype(BF16)
            columns = lax.broadcasted_iota(jnp.int32, (SRC, SRC), 1)
            for item, (ex, head) in enumerate(items):
                here, cols = slice(ex * SRC, (ex + 1) * SRC), slice(head * HD, (head + 1) * HD)
                s_s[item] = dot_t(q_s[here, cols], k_s[here, cols])
            for item, (ex, head) in enumerate(items):
                length = lengths[place.dp * 16 + chip * 2 + ex]
                scores = s_s[item] * SCALE + grid[head]
                w_s[item] = softmax_weights(jnp.where(columns < length, scores, NEG_FILL))
            for item, (ex, head) in enumerate(items):
                here, cols = slice(ex * SRC, (ex + 1) * SRC), slice(head * HD, (head + 1) * HD)
                ctx[here, cols] = dot(w_s[item], v_s[here, cols]).astype(BF16)

        attend()

        @pl.when(index > 1)
        def _():
            done = sum_chip(index - 2)
            enc_sum.partner_add(done)
            enc_sum.send_role(done)

        terms = dot(ctx[...], wo[...]).astype(BF16).reshape(2, SRC, D)
        enc_sum.part[pl.ds(sum_chip(index) * 2, 2)] = terms

        @pl.when(index > 0)
        def _():
            enc_sum.partner_send(sum_chip(index - 1))

        return carry

    lax.fori_loop(0, 8, enc_step, 0)
    enc_sum.partner_send(sum_chip(7))
    for index in (6, 7):
        done = sum_chip(index)
        enc_sum.partner_add(done)
        enc_sum.send_role(done)
    for chunk in range(ENC_CHUNKS):
        enc_sum.far(chunk)
    dec.start_far()
    dec.start()

    def finish_memory(chunk):
        rows = enc_sum.all_rows(chunk)
        value = enc_buf[owner, rows, :].astype(F32) + enc_sum.total(chunk)
        hop[rows, :] = rms(value, mem_gain[...]).astype(BF16)

    def give_back():
        @pl.when(place.x == 0)
        def _():
            pltpu.make_async_copy(hop, memory_out.at[0], back_sem.at[1]).start()

        @pl.when(place.x > 0)
        def _():
            send(hop, memory_out.at[0], back_sem.at[0], back_sem.at[1], {"tensor": owner})

    def swap_send(chunk):
        rows = enc_sum.all_rows(chunk)

        if chunk == ENC_CHUNKS - 2:
            events([dec], 4, 1, 2, 3)

        @pl.when(stays)
        def _():
            pltpu.make_async_copy(
                hop.at[rows], mem_buf.at[place.me, rows], swap_sem.at[1, chunk]
            ).start()

        @pl.when(moves)
        def _():
            send(
                hop.at[rows],
                mem_buf.at[swap_t, rows],
                swap_sem.at[0, chunk],
                swap_sem.at[1, chunk],
                (swap_dp, swap_t),
            )

    def spread(chunk):
        rows = enc_sum.all_rows(chunk)
        if chunk == ENC_CHUNKS - 1:
            events([dec], 5, 6, 7)
        arrived(mem_buf.at[place.me, rows], swap_sem.at[1, chunk])
        each = ENC_CHUNKS // MEM_CHUNKS
        if chunk % each == each - 1:
            mem[chunk // each].start()

    enc_sum.run(finish_memory, swap_send, spread)

    for chip in range(8):
        dec.partner_wait(chip)
    for load in loads[4:8]:
        load.wait()

    def q_step(index, carry):
        rows = dec_buf[pl.ds(index * 4, 4)].reshape(4 * TGT, D)
        q_all[pl.ds(index * 4, 4)] = dot(rows, cq[...]).astype(BF16).reshape(4, TGT, HW)
        return carry

    lax.fori_loop(0, 4, q_step, 0)

    def cross_chip(dz):
        return (place.z + dz + 4 - place.x) % 4 * 2

    def sum_cross(dz):
        for chip in (cross_chip(dz), cross_chip(dz) + 1):
            cross_sum.partner_add(chip)
            cross_sum.send_role(chip)

    def cross_step(index, carry):
        @pl.when(index == 1)
        def _():
            events(mem, 1, 2, 3)

        @pl.when(index == 4)
        def _():
            events(mem, 4, 5, 6)

        @pl.when(index == 7)
        def _():
            events(mem, 7)

        chip = chip_at(place, GATHER_ORDER, index)
        for gather in mem:
            gather.partner_wait(chip)
        rows = mem_buf[pl.ds(chip * 2, 2)].reshape(2 * SRC, D)
        k_s[...] = dot(rows, ck[...]).astype(BF16)
        v_s[...] = dot(rows, cv[...]).astype(BF16)
        columns = lax.broadcasted_iota(jnp.int32, (TGT, SRC), 1)
        base = ((chip % 4 + 4 - place.x) % 4) * 4 + chip // 4
        for item, (ex, head) in enumerate(items):
            here, cols = slice(ex * SRC, (ex + 1) * SRC), slice(head * HD, (head + 1) * HD)
            s_s[item, :TGT, :] = dot_t(q_all[base + 2 * ex, :, cols], k_s[here, cols])
        for item, (ex, head) in enumerate(items):
            row = base + 2 * ex
            length = lengths[(row // 2) * 16 + (row % 2) * 8 + place.dp]
            scores = s_s[item, :TGT, :] * SCALE
            w_s[item, :TGT, :] = softmax_weights(jnp.where(columns < length, scores, NEG_FILL))
        for item, (ex, head) in enumerate(items):
            here, cols = slice(ex * SRC, (ex + 1) * SRC), slice(head * HD, (head + 1) * HD)
            cross_ctx[base + 2 * ex, :, cols] = dot(w_s[item, :TGT, :], v_s[here, cols]).astype(BF16)

        @pl.when(jnp.logical_or(index == 3, index > 4))
        def _():
            @pl.when(index > 3)
            def _():
                sum_cross((PAIR_BEFORE >> (2 * index)) & 3)

            first = cross_chip((PAIR_DZ >> (2 * index)) & 3)
            block = cross_ctx[pl.ds(first * 2, 4)].reshape(4 * TGT, HW)
            cross_sum.part[pl.ds(first * 2, 4)] = dot(block, co[...]).astype(BF16).reshape(4, TGT, D)
            cross_sum.partner_send(first)
            cross_sum.partner_send(first + 1)

        return carry

    lax.fori_loop(0, 8, cross_step, 0)
    sum_cross(2)
    for chunk in range(DEC_CHUNKS):
        cross_sum.far(chunk)

    def finish_hidden(chunk):
        rows = cross_sum.all_rows(chunk)
        value = inp[rows, :] + cross_sum.total(chunk)
        hidden[rows, :] = value
        ffn_buf[place.me, rows, :] = rms(value, ffn_gain[...]).astype(BF16)

    cross_sum.run(finish_hidden, lambda chunk: ffn[chunk].start())
    for gather in ffn:
        gather.start_far()
    for load in loads[8:]:
        load.wait()

    def ffn_chips(chips):
        rows = [ffn_buf[pl.ds(chip * 2, 2)].reshape(2 * TGT, D) for chip in chips]
        rows = rows[0] if len(chips) == 1 else jnp.concatenate(rows, axis=0)
        count = rows.shape[0]
        for tile in range(FF // 512):
            cols = slice(tile * 512, (tile + 1) * 512)
            act[:count, cols] = jnp.maximum(dot(rows, win[:, cols]), 0.0).astype(BF16)
        yield
        for tile in range(D // 256):
            cols = slice(tile * 256, (tile + 1) * 256)
            result = dot(act[:count, :], wout[:, cols]).astype(BF16)
            for index, chip in enumerate(chips):
                here = slice(index * 2 * TGT, (index + 1) * 2 * TGT)
                ffn_sum.part[pl.ds(chip * 2, 2), :, cols] = result[here].reshape(2, TGT, 256)
        for chip in chips:
            ffn_sum.partner_send(chip)

    def ready(*chips):
        for chip in chips:
            for gather in ffn:
                gather.partner_wait(chip)

    own = place.chip(0, 0)
    ready(own)
    for _ in ffn_chips([own]):
        pass

    def ffn_step(index, carry):
        @pl.when(index == 0)
        def _():
            events(ffn, 1, 2, 3)

        @pl.when(index == 1)
        def _():
            events(ffn, 4, 5, 6)
            give_back()

        @pl.when(index == 2)
        def _():
            events(ffn, 7)
            ready(place.chip(0, 3))

        chips = [chip_at(place, FFN_ORDER, index * 2 + item) for item in range(2)]
        ready(*chips)
        halfway = ffn_chips(chips)
        next(halfway)

        @pl.when(index == 0)
        def _():
            ffn_sum.partner_add(own)

        @pl.when(index > 0)
        def _():
            for item in range(2):
                ffn_sum.partner_add(chip_at(place, FFN_ORDER, index * 2 - 2 + item))

        @pl.when(index == 1)
        def _():
            for chunk in range(DEC_CHUNKS):
                ffn_sum.send_near(chunk, (0,))

        @pl.when(index == 2)
        def _():
            ffn_sum.send_side(0)
            ffn_sum.send_side(1)

        for _ in halfway:
            pass
        return carry

    lax.fori_loop(0, 3, ffn_step, 0)
    last = ffn_chips([place.chip(0, 3)])
    next(last)
    for item in (4, 5):
        ffn_sum.partner_add(place.chip(*FFN_ORDER[item]))
    ffn_sum.send_yfar()
    for _ in last:
        pass
    for chunk in range(DEC_CHUNKS):
        ffn_sum.far(chunk)
    ffn_sum.partner_add(place.chip(0, 3))
    for chunk in range(DEC_CHUNKS):
        ffn_sum.send_near(chunk, (1,))

    def finish_out(chunk):
        rows = ffn_sum.all_rows(chunk)
        value = hidden[rows, :] + ffn_sum.total(chunk)
        position = lax.broadcasted_iota(jnp.int32, value.shape, 0) + chunk * ffn_sum.rows
        dec_out[0, rows, :] = jnp.where(position < tgt_length[0], value, 0.0).astype(BF16)

    ffn_sum.run(finish_out)

    arrived(memory_out.at[0], back_sem.at[1])

    @pl.when(place.x > 0)
    def _():
        arrived(hop, back_sem.at[0])

    @pl.when(moves)
    def _():
        for chunk in range(ENC_CHUNKS):
            arrived(hop.at[enc_sum.all_rows(chunk)], swap_sem.at[0, chunk])

    for stage in [*enc, dec, *mem, *ffn, enc_sum, cross_sum, ffn_sum]:
        stage.drain()


def leave_kernel(memory, dec, memory_out, dec_out):
    memory_out[...] = memory[...]
    dec_out[...] = dec[...]


VM = pltpu.VMEM
SM = pltpu.SMEM


def on_device(
    enc_tokens,
    src_lengths,
    enc_gain,
    enc_query,
    enc_key,
    enc_value,
    enc_output,
    enc_bias,
    mem_gain,
    dec_tokens,
    tgt_lengths,
    lang_tags,
    lang_table,
    cross_gain,
    cross_query,
    cross_key,
    cross_value,
    cross_output,
    ffn_gain,
    ffn_in,
    ffn_out,
):
    weights = [
        enc_query,
        enc_key,
        enc_value,
        enc_output,
        cross_query,
        cross_key,
        cross_value,
        cross_output,
        ffn_in,
        ffn_out,
    ]
    small = [
        enc_tokens,
        src_lengths,
        enc_gain,
        enc_bias,
        mem_gain,
        dec_tokens,
        lang_tags,
        lang_table,
        cross_gain,
        ffn_gain,
        tgt_lengths,
    ]
    spaces = [SM, VM, SM, VM, VM, SM, VM, VM, VM, SM]
    scratch = [space(value.shape, value.dtype) for space, value in zip(spaces, small[1:])]
    scratch += [pltpu.SemaphoreType.DMA((len(small),))]
    scratch += [pltpu.VMEM(weight.shape, BF16) for weight in weights]
    scratch += [
        pltpu.SemaphoreType.DMA((len(weights),)),
        pltpu.VMEM((HEADS, SRC, SRC), F32),
        pltpu.VMEM((2 * SRC, HW), BF16),
        pltpu.VMEM((2 * SRC, HW), BF16),
        pltpu.VMEM((2 * SRC, HW), BF16),
        pltpu.VMEM((2 * HEADS, SRC, SRC), F32),
        pltpu.VMEM((2 * HEADS, SRC, SRC), BF16),
        pltpu.VMEM((2 * SRC, HW), BF16),
        pltpu.VMEM((SRC, D), BF16),
        pltpu.SemaphoreType.DMA((2,)),
        pltpu.SemaphoreType.DMA((2, ENC_CHUNKS)),
        pltpu.VMEM((TGT, D), F32),
        pltpu.VMEM((16, TGT, HW), BF16),
        pltpu.VMEM((16, TGT, HW), BF16),
        pltpu.VMEM((4 * TGT, FF), BF16),
        pltpu.VMEM((TGT, D), F32),
    ]
    scratch += Gather.scratch(SRC, ROW_CHUNKS)
    scratch += Gather.scratch(SRC, MEM_CHUNKS)
    scratch += Gather.scratch(TGT, 1)
    scratch += Gather.scratch(TGT, DEC_CHUNKS)
    scratch += Scatter.scratch(SRC, ENC_CHUNKS)
    scratch += Scatter.scratch(TGT, DEC_CHUNKS)
    scratch += Scatter.scratch(TGT, DEC_CHUNKS)
    memory, dec = pl.pallas_call(
        layer_kernel,
        out_shape=(
            jax.ShapeDtypeStruct((1, SRC, D), BF16),
            jax.ShapeDtypeStruct((1, TGT, D), BF16),
        ),
        in_specs=[pl.BlockSpec(memory_space=pl.ANY)] * (len(small) + len(weights)),
        out_specs=(pl.BlockSpec(memory_space=VM), pl.BlockSpec(memory_space=VM)),
        scratch_shapes=scratch,
        compiler_params=pltpu.CompilerParams(
            collective_id=1, has_side_effects=True, vmem_limit_bytes=67_043_328
        ),
    )(*small, *weights)
    return pl.pallas_call(
        leave_kernel,
        out_shape=(
            jax.ShapeDtypeStruct(memory.shape, BF16),
            jax.ShapeDtypeStruct(dec.shape, BF16),
        ),
        in_specs=[pl.BlockSpec(memory_space=VM)] * 2,
        out_specs=(pl.BlockSpec(memory_space=VM), pl.BlockSpec(memory_space=VM)),
    )(memory, dec)


def solution(mesh):
    in_specs = (
        P(("dp", "tensor"), None, None),
        P(),
        P(),
        P(None, "tensor"),
        P(None, "tensor"),
        P(None, "tensor"),
        P("tensor", None),
        P("tensor", None),
        P(),
        P(("dp", "tensor"), None, None),
        P(("dp", "tensor")),
        P("dp"),
        P(),
        P(),
        P(None, "tensor"),
        P(None, "tensor"),
        P(None, "tensor"),
        P("tensor", None),
        P(),
        P(None, "tensor"),
        P("tensor", None),
    )
    out_specs = (P(("dp", "tensor"), None, None), P(("dp", "tensor"), None, None))
    return jax.shard_map(
        on_device, mesh=mesh, in_specs=in_specs, out_specs=out_specs, check_vma=False
    )
```

```python
import functools

import jax
import jax.numpy as jnp
from jax import lax
from jax.experimental import pallas as pl
from jax.experimental.pallas import tpu as pltpu
from jax.sharding import PartitionSpec as P

D = 1024
HD = 128
SRC = 128
TGT = 64
MAXREL = 16
NB = 33
LANGS = 8
HEADS = 4
HW = HEADS * HD
FF = 2048
EPSILON = 1e-06
NEG_FILL = -1e30
SCALE = HD ** (-0.5)
MESH = pl.DeviceIdType.MESH
F32 = jnp.float32
BF16 = jnp.bfloat16

GATHER_ORDER = ((0, 0), (0, 1), (0, 3), (1, 0), (0, 2), (1, 1), (1, 3), (1, 2))
FFN_ORDER = ((0, 1), (1, 0), (1, 1), (1, 3), (1, 2), (0, 2))
PAIR_DZ = 0 << 6 | 1 << 10 | 3 << 12 | 2 << 14
PAIR_BEFORE = 0 << 10 | 1 << 12 | 3 << 14
ROW_CHUNKS = 1
ENC_CHUNKS = 4
MEM_CHUNKS = 2
DEC_CHUNKS = 1


def packed(order):
    return (
        sum(dy << i for i, (dy, dz) in enumerate(order)),
        sum(dz << (2 * i) for i, (dy, dz) in enumerate(order)),
    )


def chip_at(place, order, index):
    dy_bits, dz_bits = packed(order)
    return place.chip((dy_bits >> index) & 1, (dz_bits >> (2 * index)) & 3)


def rms(values, gain):
    mean_sq = jnp.mean(values * values, axis=-1, keepdims=True)
    return values * lax.rsqrt(mean_sq + EPSILON) * gain


class Place:
    def __init__(self):
        self.me = lax.axis_index("tensor")
        self.dp = lax.axis_index("dp")
        self.core = self.me % 2
        self.z = (self.me // 2) % 4
        self.y = self.me // 8
        self.x = self.dp // 2
        self.y_lo = self.dp % 2

    def chip(self, dy, dz):
        return ((self.y + dy) % 2) * 4 + (self.z + dz) % 4

    def slot(self, dy, dz, dk=0):
        return self.chip(dy, dz) * 2 + (self.core + dk) % 2


def send(src, dst, send_sem, recv_sem, device):
    pltpu.make_async_remote_copy(
        src_ref=src,
        dst_ref=dst,
        send_sem=send_sem,
        recv_sem=recv_sem,
        device_id=device,
        device_id_type=MESH,
    ).start()


def arrived(dst, recv_sem):
    pltpu.make_async_copy(dst, dst, recv_sem).wait()


class Gather:
    SENDS = 16

    def __init__(self, place, buf, ssem, rsem, hsem, chunk, chunks, direct):
        self.p, self.buf, self.chunk, self.direct = place, buf, chunk, direct
        self.ssem, self.rsem, self.hsem = ssem, rsem, hsem
        self.rows = buf.shape[1] // chunks
        self.first = chunk * self.rows
        self.sent = []

    def _part(self, slot):
        return self.buf.at[slot, pl.ds(self.first, self.rows)]

    def _half_part(self, slot, which):
        half = self.rows // 2
        return self.buf.at[slot, pl.ds(self.first + which * half, half)]

    def _send(self, src, recv_sem, target):
        sem = self.ssem.at[self.chunk, len(self.sent)]
        send(src, src, sem, recv_sem, {"tensor": target})
        self.sent.append(src.shape[0])

    def _full(self, slot, target):
        self._send(self._part(slot), self.rsem.at[self.chunk, slot], target)

    def _half(self, slot, which, target):
        self._send(self._half_part(slot, which), self.hsem.at[self.chunk, which], target)

    def start(self):
        p = self.p
        for target in (p.slot(0, 1), p.slot(0, 3), p.slot(1, 0), p.slot(0, 0, 1)):
            self._full(p.me, target)

    def start_far(self):
        self._full(self.p.me, self.p.slot(0, 2))

    def event(self, index):
        p = self.p
        dy, dz = GATHER_ORDER[index]
        slot = p.slot(dy, dz)
        if (dy, dz) == (0, 2) and not self.direct:
            for which in (0, 1):
                arrived(self._half_part(slot, which), self.hsem.at[self.chunk, which])
        else:
            arrived(self._part(slot), self.rsem.at[self.chunk, slot])
        if (dy, dz) == (0, 2):
            self._full(slot, p.slot(1, 0))
        elif (dy, dz) == (0, 1) and not self.direct:
            self._half(slot, 1, p.slot(0, 3))
        elif (dy, dz) == (0, 3) and not self.direct:
            self._half(slot, 0, p.slot(0, 1))
        elif (dy, dz) == (1, 0):
            self._full(slot, p.slot(0, 1))
            self._full(slot, p.slot(0, 3))
        self._full(slot, p.slot(0, 0, 1))

    def partner_wait(self, chip):
        slot = chip * 2 + (self.p.core + 1) % 2
        arrived(self._part(slot), self.rsem.at[self.chunk, slot])

    def drain(self):
        for index, rows in enumerate(self.sent):
            arrived(self.buf.at[0, pl.ds(0, rows)], self.ssem.at[self.chunk, index])

    @staticmethod
    def scratch(rows, chunks):
        return [
            pltpu.VMEM((16, rows, D), BF16),
            pltpu.SemaphoreType.DMA((chunks, Gather.SENDS)),
            pltpu.SemaphoreType.DMA((chunks, 16)),
            pltpu.SemaphoreType.DMA((chunks, 2)),
        ]

    @staticmethod
    def make(place, refs, chunks, direct=False):
        return [Gather(place, *refs, chunk, chunks, direct) for chunk in range(chunks)]


class Scatter:
    SENDS = 10

    def __init__(self, place, chunks, direct, part, xbuf, yfar, relay, fin, finy, ysend, yrec, *sems):
        self.p, self.chunks, self.direct = place, chunks, direct
        self.part, self.xbuf, self.yfar, self.relay = part, xbuf, yfar, relay
        self.fin, self.finy, self.ysend, self.yrec = fin, finy, ysend, yrec
        self.psem, self.xsem, self.ssem = sems[:3]
        self.yfar_sem, self.relay_sem, self.fin_sem, self.finy_sem, self.yrec_sem = sems[3:]
        self.rows = part.shape[1] // chunks
        self.half = self.rows // 2
        self.sent = {}

    @staticmethod
    def scratch(rows, chunks):
        return [
            pltpu.VMEM((16, rows, D), BF16),
            pltpu.VMEM((8, rows, D), BF16),
            pltpu.VMEM((rows, D), BF16),
            pltpu.VMEM((rows, D), BF16),
            pltpu.VMEM((2, rows, D), BF16),
            pltpu.VMEM((2, rows, D), BF16),
            pltpu.VMEM((rows, D), BF16),
            pltpu.VMEM((rows, D), BF16),
            pltpu.SemaphoreType.DMA((8,)),
            pltpu.SemaphoreType.DMA((8,)),
            pltpu.SemaphoreType.DMA((chunks * Scatter.SENDS,)),
            pltpu.SemaphoreType.DMA((chunks,)),
            pltpu.SemaphoreType.DMA((chunks, 2)),
            pltpu.SemaphoreType.DMA((chunks, 2, 2)),
            pltpu.SemaphoreType.DMA((chunks, 2)),
            pltpu.SemaphoreType.DMA((chunks,)),
        ]

    def partner_send(self, chip):
        slot = chip * 2 + (self.p.core + 1) % 2
        send(
            self.part.at[slot],
            self.xbuf.at[chip],
            self.psem.at[chip],
            self.xsem.at[chip],
            {"tensor": self.p.slot(0, 0, 1)},
        )

    def partner_add(self, chip):
        arrived(self.xbuf.at[chip], self.xsem.at[chip])
        slot = chip * 2 + self.p.core
        self.part[slot] = self.part[slot] + self.xbuf[chip]

    def _send(self, key, src, dst, recv_sem, target):
        index, _ = self.sent.setdefault(key, (len(self.sent), src.shape[0]))
        send(src, dst, self.ssem.at[index], recv_sem, {"tensor": target})

    def all_rows(self, chunk):
        return pl.ds(chunk * self.rows, self.rows)

    def half_rows(self, chunk, which):
        return pl.ds(chunk * self.rows + which * self.half, self.half)

    def send_yfar(self):
        slot = self.p.slot(1, 2)
        for chunk in range(self.chunks):
            rows = self.all_rows(chunk)
            self._send(
                ("yfar", chunk),
                self.part.at[slot, rows],
                self.yfar.at[rows],
                self.yfar_sem.at[chunk],
                self.p.slot(1, 0),
            )

    def send_side(self, way):
        dz = (1, 3)[way]
        slot = self.p.slot(1, dz)
        for chunk in range(self.chunks):
            rows = self.all_rows(chunk)
            self._send(
                ("side", chunk, way),
                self.part.at[slot, rows],
                self.finy.at[way, rows],
                self.finy_sem.at[chunk, way],
                self.p.slot(0, dz),
            )

    def _near(self, chunk, way, which):
        dz = (1, 3)[way]
        rows = self.half_rows(chunk, which)
        self._send(
            ("near", chunk, way, which),
            self.part.at[self.p.slot(0, dz), rows],
            self.fin.at[way, rows],
            self.fin_sem.at[chunk, way, which],
            self.p.slot(0, dz),
        )

    def send_near(self, chunk, ways=(0, 1)):
        for way in ways:
            for which in (0, 1):
                self._near(chunk, way, which)

    def send_role(self, chip):
        p = self.p
        dy, dz = (chip // 4 + p.y) % 2, (chip % 4 + 4 - p.z) % 4

        def when(row, column, action):
            @pl.when(jnp.logical_and(dy == row, dz == column))
            def _():
                action()

        when(1, 2, self.send_yfar)
        for way, column in ((0, 1), (1, 3)):
            when(1, column, functools.partial(self.send_side, way))
            when(0, column, lambda way=way: [self.send_near(c, (way,)) for c in range(self.chunks)])

    def far(self, chunk):
        rows = self.all_rows(chunk)
        slot = self.p.slot(0, 2)
        arrived(self.yfar.at[rows], self.yfar_sem.at[chunk])
        self.part[slot, rows, :] = self.part[slot, rows, :] + self.yfar[rows, :]
        if self.direct:
            self._send(
                ("far", chunk),
                self.part.at[slot, rows],
                self.relay.at[rows],
                self.relay_sem.at[chunk, 0],
                slot,
            )
            return
        self._near(chunk, 0, 1)
        self._near(chunk, 1, 0)
        for way in (0, 1):
            self._send(
                ("far", chunk, way),
                self.part.at[slot, self.half_rows(chunk, way)],
                self.relay.at[self.half_rows(chunk, way)],
                self.relay_sem.at[chunk, way],
                self.p.slot(0, (1, 3)[way]),
            )

    def cross_sum(self, chunk):
        rows = self.all_rows(chunk)
        for way in (0, 1):
            arrived(self.finy.at[way, rows], self.finy_sem.at[chunk, way])
        total = self.part[self.p.slot(1, 0), rows, :].astype(F32)
        total = total + self.finy[0, rows, :].astype(F32) + self.finy[1, rows, :].astype(F32)
        self.ysend[rows, :] = total.astype(BF16)

    def cross_send(self, chunk):
        rows = self.all_rows(chunk)
        self._send(
            ("cross", chunk),
            self.ysend.at[rows],
            self.yrec.at[rows],
            self.yrec_sem.at[chunk],
            self.p.slot(1, 0),
        )

    def relay_add(self, chunk):
        for way in (0, 1):
            slot, rows = self.p.slot(0, (1, 3)[way]), self.half_rows(chunk, way)
            arrived(self.relay.at[rows], self.relay_sem.at[chunk, way])
            self.part[slot, rows, :] = self.part[slot, rows, :] + self.relay[rows, :]

    def relay_send(self, chunk):
        for way in (0, 1):
            self._near(chunk, way, way)

    def total(self, chunk):
        rows = self.all_rows(chunk)
        for way in (0, 1):
            for which in (0, 1):
                arrived(
                    self.fin.at[way, self.half_rows(chunk, which)],
                    self.fin_sem.at[chunk, way, which],
                )
        own = self.part[self.p.me, rows, :].astype(F32)
        own = own + self.fin[0, rows, :].astype(F32) + self.fin[1, rows, :].astype(F32)
        if self.direct:
            arrived(self.relay.at[rows], self.relay_sem.at[chunk, 0])
            own = own + self.relay[rows, :].astype(F32)
        arrived(self.yrec.at[rows], self.yrec_sem.at[chunk])
        return own + self.yrec[rows, :].astype(F32)

    def run(self, *stages):
        if self.direct:
            steps = (self.cross_sum, self.cross_send) + stages
        else:
            steps = (
                self.far,
                self.cross_sum,
                lambda chunk: (self.cross_send(chunk), self.relay_add(chunk)),
                self.relay_send,
            ) + stages
        for time in range(self.chunks + len(steps) - 1):
            for index, stage in enumerate(steps):
                if 0 <= time - index < self.chunks:
                    stage(time - index)

    def drain(self):
        for chip in range(8):
            slot = chip * 2 + (self.p.core + 1) % 2
            arrived(self.part.at[slot], self.psem.at[chip])
        for index, rows in self.sent.values():
            arrived(self.part.at[0, pl.ds(0, rows)], self.ssem.at[index])


def dot(left, right):
    return jnp.dot(left, right, preferred_element_type=F32)


def dot_t(left, right):
    return lax.dot_general(left, right, (((1,), (1,)), ((), ())), preferred_element_type=F32)


def softmax_weights(scores):
    row_max = jnp.max(scores, axis=-1, keepdims=True)
    exponent = jnp.exp(scores - row_max)
    return (exponent * (1.0 / jnp.sum(exponent, axis=-1, keepdims=True))).astype(BF16)


def layer_kernel(*refs):
    refs = list(refs)

    def take(count):
        taken, refs[:count] = refs[:count], []
        return taken

    small_hbm, hbm = take(11), take(10)
    memory_out, dec_out = take(2)
    small = take(10)
    lengths, gain, bias, mem_gain, dec_tokens = small[:5]
    tags, table, cross_gain, ffn_gain, tgt_length = small[5:]
    (small_sem,) = take(1)
    weights = take(10)
    (weight_sem,) = take(1)
    wq, wk, wv, wo, cq, ck, cv, co, win, wout = weights
    grid, q_s, k_s, v_s, s_s, w_s, ctx = take(7)
    hop, back_sem, swap_sem = take(3)
    inp, q_all, cross_ctx, act, hidden = take(5)
    place = Place()
    enc_refs, mem_refs, dec_refs, ffn_refs = take(4), take(4), take(4), take(4)
    enc = Gather.make(place, enc_refs, ROW_CHUNKS)
    mem = Gather.make(place, mem_refs, MEM_CHUNKS)
    (dec,) = Gather.make(place, dec_refs, 1, True)
    ffn = Gather.make(place, ffn_refs, DEC_CHUNKS, True)
    enc_sum = Scatter(place, ENC_CHUNKS, True, *take(16))
    cross_sum = Scatter(place, DEC_CHUNKS, True, *take(16))
    ffn_sum = Scatter(place, DEC_CHUNKS, True, *take(16))

    def events(gathers, *numbers):
        for number in numbers:
            for gather in gathers:
                gather.event(number)

    loads = [
        pltpu.make_async_copy(src, dst, weight_sem.at[index])
        for index, (src, dst) in enumerate(zip(hbm, weights))
    ]
    owner = place.slot(0, 4 - place.x)
    enc_buf, mem_buf, dec_buf, ffn_buf = enc_refs[0], mem_refs[0], dec_refs[0], ffn_refs[0]
    fetch = [
        pltpu.make_async_copy(src, dst, small_sem.at[index])
        for index, (src, dst) in enumerate(zip(small_hbm[1:], small))
    ]
    own_rows = pltpu.make_async_copy(small_hbm[0].at[0], enc_buf.at[place.me], small_sem.at[10])
    own_rows.start()
    for copy in fetch:
        copy.start()
    for load in loads[:4]:
        load.start()
    swap_dp = ((place.z + 4 - place.x) % 4) * 2 + place.core
    swap_t = place.y * 8 + place.z * 2 + place.y_lo
    stays = jnp.logical_and(swap_dp == place.dp, swap_t == place.me)
    moves = jnp.logical_not(stays)

    barrier = pltpu.get_barrier_semaphore()
    for target in (
        place.slot(0, 0, 1),
        place.slot(0, 1),
        place.slot(0, 3),
        place.slot(0, 2),
        place.slot(1, 0),
    ):
        pl.semaphore_signal(barrier, inc=1, device_id={"tensor": target}, device_id_type=MESH)

    @pl.when(moves)
    def _():
        pl.semaphore_signal(barrier, inc=1, device_id=(swap_dp, swap_t), device_id_type=MESH)

    own_rows.wait()

    @pl.when(moves)
    def _():
        pl.semaphore_wait(barrier, 6)

    @pl.when(stays)
    def _():
        pl.semaphore_wait(barrier, 5)

    for gather in enc:
        gather.start()
    for copy in fetch:
        copy.wait()
    tag = tags[place.me]
    lang = jnp.zeros((1, D), F32)
    for index in range(LANGS):
        lang = jnp.where(tag == index, table[index : index + 1, :].astype(F32), lang)
    value = dec_tokens[0].astype(F32) + lang
    inp[...] = value
    dec_buf[place.me] = rms(value, cross_gain[...]).astype(BF16)

    keys = lax.broadcasted_iota(jnp.int32, (SRC, SRC), 1)
    bucket = jnp.clip(keys - lax.broadcasted_iota(jnp.int32, (SRC, SRC), 0), -MAXREL, MAXREL) + MAXREL
    for head in range(HEADS):
        values = jnp.zeros((SRC, SRC), F32)
        for index in range(NB):
            values = jnp.where(bucket == index, bias[head, index], values)
        grid[head] = values
    for load in loads[:4]:
        load.wait()

    items = [(ex, head) for ex in range(2) for head in range(HEADS)]

    def sum_chip(index):
        chip = chip_at(place, GATHER_ORDER, index)
        return chip // 4 * 4 + (chip % 4 + place.x) % 4

    def enc_step(index, carry):
        @pl.when(index == 1)
        def _():
            events(enc, 1, 2, 3)
            for load in loads[4:]:
                load.start()

        @pl.when(index == 4)
        def _():
            events(enc, 4, 5, 6)

        @pl.when(index == 7)
        def _():
            events(enc, 7)

        def attend():
            chip = chip_at(place, GATHER_ORDER, index)
            for gather in enc:
                gather.partner_wait(chip)
            raw = enc_buf[pl.ds(chip * 2, 2)].reshape(2 * SRC, D)
            rows = rms(raw.astype(F32), gain[...]).astype(BF16)
            q_s[...] = dot(rows, wq[...]).astype(BF16)
            k_s[...] = dot(rows, wk[...]).astype(BF16)
            v_s[...] = dot(rows, wv[...]).astype(BF16)
            columns = lax.broadcasted_iota(jnp.int32, (SRC, SRC), 1)
            for item, (ex, head) in enumerate(items):
                here, cols = slice(ex * SRC, (ex + 1) * SRC), slice(head * HD, (head + 1) * HD)
                s_s[item] = dot_t(q_s[here, cols], k_s[here, cols])
            for item, (ex, head) in enumerate(items):
                length = lengths[place.dp * 16 + chip * 2 + ex]
                scores = s_s[item] * SCALE + grid[head]
                w_s[item] = softmax_weights(jnp.where(columns < length, scores, NEG_FILL))
            for item, (ex, head) in enumerate(items):
                here, cols = slice(ex * SRC, (ex + 1) * SRC), slice(head * HD, (head + 1) * HD)
                ctx[here, cols] = dot(w_s[item], v_s[here, cols]).astype(BF16)

        attend()

        @pl.when(index > 1)
        def _():
            done = sum_chip(index - 2)
            enc_sum.partner_add(done)
            enc_sum.send_role(done)

        terms = dot(ctx[...], wo[...]).astype(BF16).reshape(2, SRC, D)
        enc_sum.part[pl.ds(sum_chip(index) * 2, 2)] = terms

        @pl.when(index > 0)
        def _():
            enc_sum.partner_send(sum_chip(index - 1))

        return carry

    lax.fori_loop(0, 8, enc_step, 0)
    enc_sum.partner_send(sum_chip(7))
    for index in (6, 7):
        done = sum_chip(index)
        enc_sum.partner_add(done)
        enc_sum.send_role(done)
    for chunk in range(ENC_CHUNKS):
        enc_sum.far(chunk)
    dec.start_far()
    dec.start()

    def finish_memory(chunk):
        rows = enc_sum.all_rows(chunk)
        value = enc_buf[owner, rows, :].astype(F32) + enc_sum.total(chunk)
        hop[rows, :] = rms(value, mem_gain[...]).astype(BF16)

    def give_back():
        @pl.when(place.x == 0)
        def _():
            pltpu.make_async_copy(hop, memory_out.at[0], back_sem.at[1]).start()

        @pl.when(place.x > 0)
        def _():
            send(hop, memory_out.at[0], back_sem.at[0], back_sem.at[1], {"tensor": owner})

    def swap_send(chunk):
        rows = enc_sum.all_rows(chunk)

        if chunk == ENC_CHUNKS - 2:
            events([dec], 4, 1, 2, 3)

        @pl.when(stays)
        def _():
            pltpu.make_async_copy(
                hop.at[rows], mem_buf.at[place.me, rows], swap_sem.at[1, chunk]
            ).start()

        @pl.when(moves)
        def _():
            send(
                hop.at[rows],
                mem_buf.at[swap_t, rows],
                swap_sem.at[0, chunk],
                swap_sem.at[1, chunk],
                (swap_dp, swap_t),
            )

    def spread(chunk):
        rows = enc_sum.all_rows(chunk)
        if chunk == ENC_CHUNKS - 1:
            events([dec], 5, 6, 7)
        arrived(mem_buf.at[place.me, rows], swap_sem.at[1, chunk])
        each = ENC_CHUNKS // MEM_CHUNKS
        if chunk % each == each - 1:
            mem[chunk // each].start()

    enc_sum.run(finish_memory, swap_send, spread)

    for chip in range(8):
        dec.partner_wait(chip)
    for load in loads[4:8]:
        load.wait()

    def q_step(index, carry):
        rows = dec_buf[pl.ds(index * 4, 4)].reshape(4 * TGT, D)
        q_all[pl.ds(index * 4, 4)] = dot(rows, cq[...]).astype(BF16).reshape(4, TGT, HW)
        return carry

    lax.fori_loop(0, 4, q_step, 0)

    def cross_chip(dz):
        return (place.z + dz + 4 - place.x) % 4 * 2

    def sum_cross(dz):
        for chip in (cross_chip(dz), cross_chip(dz) + 1):
            cross_sum.partner_add(chip)
            cross_sum.send_role(chip)

    def cross_step(index, carry):
        @pl.when(index == 1)
        def _():
            events(mem, 1, 2, 3)

        @pl.when(index == 4)
        def _():
            events(mem, 4, 5, 6)

        @pl.when(index == 7)
        def _():
            events(mem, 7)

        chip = chip_at(place, GATHER_ORDER, index)
        for gather in mem:
            gather.partner_wait(chip)
        rows = mem_buf[pl.ds(chip * 2, 2)].reshape(2 * SRC, D)
        k_s[...] = dot(rows, ck[...]).astype(BF16)
        v_s[...] = dot(rows, cv[...]).astype(BF16)
        columns = lax.broadcasted_iota(jnp.int32, (TGT, SRC), 1)
        base = ((chip % 4 + 4 - place.x) % 4) * 4 + chip // 4
        for item, (ex, head) in enumerate(items):
            here, cols = slice(ex * SRC, (ex + 1) * SRC), slice(head * HD, (head + 1) * HD)
            s_s[item, :TGT, :] = dot_t(q_all[base + 2 * ex, :, cols], k_s[here, cols])
        for item, (ex, head) in enumerate(items):
            row = base + 2 * ex
            length = lengths[(row // 2) * 16 + (row % 2) * 8 + place.dp]
            scores = s_s[item, :TGT, :] * SCALE
            w_s[item, :TGT, :] = softmax_weights(jnp.where(columns < length, scores, NEG_FILL))
        for item, (ex, head) in enumerate(items):
            here, cols = slice(ex * SRC, (ex + 1) * SRC), slice(head * HD, (head + 1) * HD)
            cross_ctx[base + 2 * ex, :, cols] = dot(w_s[item, :TGT, :], v_s[here, cols]).astype(BF16)

        @pl.when(jnp.logical_or(index == 3, index > 4))
        def _():
            @pl.when(index > 3)
            def _():
                sum_cross((PAIR_BEFORE >> (2 * index)) & 3)

            first = cross_chip((PAIR_DZ >> (2 * index)) & 3)
            block = cross_ctx[pl.ds(first * 2, 4)].reshape(4 * TGT, HW)
            cross_sum.part[pl.ds(first * 2, 4)] = dot(block, co[...]).astype(BF16).reshape(4, TGT, D)
            cross_sum.partner_send(first)
            cross_sum.partner_send(first + 1)

        return carry

    lax.fori_loop(0, 8, cross_step, 0)
    sum_cross(2)
    for chunk in range(DEC_CHUNKS):
        cross_sum.far(chunk)

    def finish_hidden(chunk):
        rows = cross_sum.all_rows(chunk)
        value = inp[rows, :] + cross_sum.total(chunk)
        hidden[rows, :] = value
        ffn_buf[place.me, rows, :] = rms(value, ffn_gain[...]).astype(BF16)

    cross_sum.run(finish_hidden, lambda chunk: ffn[chunk].start())
    for gather in ffn:
        gather.start_far()
    for load in loads[8:]:
        load.wait()

    def ffn_chips(chips):
        rows = [ffn_buf[pl.ds(chip * 2, 2)].reshape(2 * TGT, D) for chip in chips]
        rows = rows[0] if len(chips) == 1 else jnp.concatenate(rows, axis=0)
        count = rows.shape[0]
        for tile in range(FF // 512):
            cols = slice(tile * 512, (tile + 1) * 512)
            act[:count, cols] = jnp.maximum(dot(rows, win[:, cols]), 0.0).astype(BF16)
        yield
        for tile in range(D // 256):
            cols = slice(tile * 256, (tile + 1) * 256)
            result = dot(act[:count, :], wout[:, cols]).astype(BF16)
            for index, chip in enumerate(chips):
                here = slice(index * 2 * TGT, (index + 1) * 2 * TGT)
                ffn_sum.part[pl.ds(chip * 2, 2), :, cols] = result[here].reshape(2, TGT, 256)
        for chip in chips:
            ffn_sum.partner_send(chip)

    def ready(*chips):
        for chip in chips:
            for gather in ffn:
                gather.partner_wait(chip)

    own = place.chip(0, 0)
    ready(own)
    for _ in ffn_chips([own]):
        pass

    def ffn_step(index, carry):
        @pl.when(index == 0)
        def _():
            events(ffn, 1, 2, 3)

        @pl.when(index == 1)
        def _():
            events(ffn, 4, 5, 6)
            give_back()

        @pl.when(index == 2)
        def _():
            events(ffn, 7)
            ready(place.chip(0, 3))

        chips = [chip_at(place, FFN_ORDER, index * 2 + item) for item in range(2)]
        ready(*chips)
        halfway = ffn_chips(chips)
        next(halfway)

        @pl.when(index == 0)
        def _():
            ffn_sum.partner_add(own)

        @pl.when(index > 0)
        def _():
            for item in range(2):
                ffn_sum.partner_add(chip_at(place, FFN_ORDER, index * 2 - 2 + item))

        @pl.when(index == 1)
        def _():
            for chunk in range(DEC_CHUNKS):
                ffn_sum.send_near(chunk, (0,))

        @pl.when(index == 2)
        def _():
            ffn_sum.send_side(0)
            ffn_sum.send_side(1)

        for _ in halfway:
            pass
        return carry

    lax.fori_loop(0, 3, ffn_step, 0)
    last = ffn_chips([place.chip(0, 3)])
    next(last)
    for item in (4, 5):
        ffn_sum.partner_add(place.chip(*FFN_ORDER[item]))
    ffn_sum.send_yfar()
    for _ in last:
        pass
    for chunk in range(DEC_CHUNKS):
        ffn_sum.far(chunk)
    ffn_sum.partner_add(place.chip(0, 3))
    for chunk in range(DEC_CHUNKS):
        ffn_sum.send_near(chunk, (1,))

    def finish_out(chunk):
        rows = ffn_sum.all_rows(chunk)
        value = hidden[rows, :] + ffn_sum.total(chunk)
        position = lax.broadcasted_iota(jnp.int32, value.shape, 0) + chunk * ffn_sum.rows
        dec_out[0, rows, :] = jnp.where(position < tgt_length[0], value, 0.0).astype(BF16)

    ffn_sum.run(finish_out)

    arrived(memory_out.at[0], back_sem.at[1])

    @pl.when(place.x > 0)
    def _():
        arrived(hop, back_sem.at[0])

    @pl.when(moves)
    def _():
        for chunk in range(ENC_CHUNKS):
            arrived(hop.at[enc_sum.all_rows(chunk)], swap_sem.at[0, chunk])

    for stage in [*enc, dec, *mem, *ffn, enc_sum, cross_sum, ffn_sum]:
        stage.drain()


def leave_kernel(memory, dec, memory_out, dec_out):
    memory_out[...] = memory[...]
    dec_out[...] = dec[...]


VM = pltpu.VMEM
SM = pltpu.SMEM


def on_device(
    enc_tokens,
    src_lengths,
    enc_gain,
    enc_query,
    enc_key,
    enc_value,
    enc_output,
    enc_bias,
    mem_gain,
    dec_tokens,
    tgt_lengths,
    lang_tags,
    lang_table,
    cross_gain,
    cross_query,
    cross_key,
    cross_value,
    cross_output,
    ffn_gain,
    ffn_in,
    ffn_out,
):
    weights = [
        enc_query,
        enc_key,
        enc_value,
        enc_output,
        cross_query,
        cross_key,
        cross_value,
        cross_output,
        ffn_in,
        ffn_out,
    ]
    small = [
        enc_tokens,
        src_lengths,
        enc_gain,
        enc_bias,
        mem_gain,
        dec_tokens,
        lang_tags,
        lang_table,
        cross_gain,
        ffn_gain,
        tgt_lengths,
    ]
    spaces = [SM, VM, SM, VM, VM, SM, VM, VM, VM, SM]
    scratch = [space(value.shape, value.dtype) for space, value in zip(spaces, small[1:])]
    scratch += [pltpu.SemaphoreType.DMA((len(small),))]
    scratch += [pltpu.VMEM(weight.shape, BF16) for weight in weights]
    scratch += [
        pltpu.SemaphoreType.DMA((len(weights),)),
        pltpu.VMEM((HEADS, SRC, SRC), F32),
        pltpu.VMEM((2 * SRC, HW), BF16),
        pltpu.VMEM((2 * SRC, HW), BF16),
        pltpu.VMEM((2 * SRC, HW), BF16),
        pltpu.VMEM((2 * HEADS, SRC, SRC), F32),
        pltpu.VMEM((2 * HEADS, SRC, SRC), BF16),
        pltpu.VMEM((2 * SRC, HW), BF16),
        pltpu.VMEM((SRC, D), BF16),
        pltpu.SemaphoreType.DMA((2,)),
        pltpu.SemaphoreType.DMA((2, ENC_CHUNKS)),
        pltpu.VMEM((TGT, D), F32),
        pltpu.VMEM((16, TGT, HW), BF16),
        pltpu.VMEM((16, TGT, HW), BF16),
        pltpu.VMEM((4 * TGT, FF), BF16),
        pltpu.VMEM((TGT, D), F32),
    ]
    scratch += Gather.scratch(SRC, ROW_CHUNKS)
    scratch += Gather.scratch(SRC, MEM_CHUNKS)
    scratch += Gather.scratch(TGT, 1)
    scratch += Gather.scratch(TGT, DEC_CHUNKS)
    scratch += Scatter.scratch(SRC, ENC_CHUNKS)
    scratch += Scatter.scratch(TGT, DEC_CHUNKS)
    scratch += Scatter.scratch(TGT, DEC_CHUNKS)
    memory, dec = pl.pallas_call(
        layer_kernel,
        out_shape=(
            jax.ShapeDtypeStruct((1, SRC, D), BF16),
            jax.ShapeDtypeStruct((1, TGT, D), BF16),
        ),
        in_specs=[pl.BlockSpec(memory_space=pl.ANY)] * (len(small) + len(weights)),
        out_specs=(pl.BlockSpec(memory_space=VM), pl.BlockSpec(memory_space=VM)),
        scratch_shapes=scratch,
        compiler_params=pltpu.CompilerParams(
            collective_id=1, has_side_effects=True, vmem_limit_bytes=67_043_328
        ),
    )(*small, *weights)
    return pl.pallas_call(
        leave_kernel,
        out_shape=(
            jax.ShapeDtypeStruct(memory.shape, BF16),
            jax.ShapeDtypeStruct(dec.shape, BF16),
        ),
        in_specs=[pl.BlockSpec(memory_space=VM)] * 2,
        out_specs=(pl.BlockSpec(memory_space=VM), pl.BlockSpec(memory_space=VM)),
    )(memory, dec)


def solution(mesh):
    in_specs = (
        P(("dp", "tensor"), None, None),
        P(),
        P(),
        P(None, "tensor"),
        P(None, "tensor"),
        P(None, "tensor"),
        P("tensor", None),
        P("tensor", None),
        P(),
        P(("dp", "tensor"), None, None),
        P(("dp", "tensor")),
        P("dp"),
        P(),
        P(),
        P(None, "tensor"),
        P(None, "tensor"),
        P(None, "tensor"),
        P("tensor", None),
        P(),
        P(None, "tensor"),
        P("tensor", None),
    )
    out_specs = (P(("dp", "tensor"), None, None), P(("dp", "tensor"), None, None))
    return jax.shard_map(
        on_device, mesh=mesh, in_specs=in_specs, out_specs=out_specs, check_vma=False
    )
```

```python
import functools

import jax
import jax.numpy as jnp
from jax import lax
from jax.experimental import pallas as pl
from jax.experimental.pallas import tpu as pltpu
from jax.sharding import PartitionSpec as P

D = 1024
HD = 128
SRC = 128
TGT = 64
MAXREL = 16
NB = 33
LANGS = 8
HEADS = 4
HW = HEADS * HD
FF = 2048
EPSILON = 1e-06
NEG_FILL = -1e30
SCALE = HD ** (-0.5)
MESH = pl.DeviceIdType.MESH
F32 = jnp.float32
BF16 = jnp.bfloat16

GATHER_ORDER = ((0, 0), (0, 1), (0, 3), (1, 0), (0, 2), (1, 1), (1, 3), (1, 2))
FFN_ORDER = ((0, 1), (1, 0), (1, 1), (1, 3), (1, 2), (0, 2))
PAIR_DZ = 0 << 6 | 1 << 10 | 3 << 12 | 2 << 14
PAIR_BEFORE = 0 << 10 | 1 << 12 | 3 << 14
ROW_CHUNKS = 1
ENC_CHUNKS = 4
MEM_CHUNKS = 2
DEC_CHUNKS = 1


def packed(order):
    return (
        sum(dy << i for i, (dy, dz) in enumerate(order)),
        sum(dz << (2 * i) for i, (dy, dz) in enumerate(order)),
    )


def chip_at(place, order, index):
    dy_bits, dz_bits = packed(order)
    return place.chip((dy_bits >> index) & 1, (dz_bits >> (2 * index)) & 3)


def rms(values, gain):
    mean_sq = jnp.mean(values * values, axis=-1, keepdims=True)
    return values * lax.rsqrt(mean_sq + EPSILON) * gain


class Place:
    def __init__(self):
        self.me = lax.axis_index("tensor")
        self.dp = lax.axis_index("dp")
        self.core = self.me % 2
        self.z = (self.me // 2) % 4
        self.y = self.me // 8
        self.x = self.dp // 2
        self.y_lo = self.dp % 2

    def chip(self, dy, dz):
        return ((self.y + dy) % 2) * 4 + (self.z + dz) % 4

    def slot(self, dy, dz, dk=0):
        return self.chip(dy, dz) * 2 + (self.core + dk) % 2


def send(src, dst, send_sem, recv_sem, device):
    pltpu.make_async_remote_copy(
        src_ref=src,
        dst_ref=dst,
        send_sem=send_sem,
        recv_sem=recv_sem,
        device_id=device,
        device_id_type=MESH,
    ).start()


def arrived(dst, recv_sem):
    pltpu.make_async_copy(dst, dst, recv_sem).wait()


class Gather:
    SENDS = 16

    def __init__(self, place, buf, ssem, rsem, hsem, chunk, chunks, direct):
        self.p, self.buf, self.chunk, self.direct = place, buf, chunk, direct
        self.ssem, self.rsem, self.hsem = ssem, rsem, hsem
        self.rows = buf.shape[1] // chunks
        self.first = chunk * self.rows
        self.sent = []

    def _part(self, slot):
        return self.buf.at[slot, pl.ds(self.first, self.rows)]

    def _half_part(self, slot, which):
        half = self.rows // 2
        return self.buf.at[slot, pl.ds(self.first + which * half, half)]

    def _send(self, src, recv_sem, target):
        sem = self.ssem.at[self.chunk, len(self.sent)]
        send(src, src, sem, recv_sem, {"tensor": target})
        self.sent.append(src.shape[0])

    def _full(self, slot, target):
        self._send(self._part(slot), self.rsem.at[self.chunk, slot], target)

    def _half(self, slot, which, target):
        self._send(self._half_part(slot, which), self.hsem.at[self.chunk, which], target)

    def start(self):
        p = self.p
        for target in (p.slot(0, 1), p.slot(0, 3), p.slot(1, 0), p.slot(0, 0, 1)):
            self._full(p.me, target)

    def start_far(self):
        self._full(self.p.me, self.p.slot(0, 2))

    def event(self, index):
        p = self.p
        dy, dz = GATHER_ORDER[index]
        slot = p.slot(dy, dz)
        if (dy, dz) == (0, 2) and not self.direct:
            for which in (0, 1):
                arrived(self._half_part(slot, which), self.hsem.at[self.chunk, which])
        else:
            arrived(self._part(slot), self.rsem.at[self.chunk, slot])
        if (dy, dz) == (0, 2):
            self._full(slot, p.slot(1, 0))
        elif (dy, dz) == (0, 1) and not self.direct:
            self._half(slot, 1, p.slot(0, 3))
        elif (dy, dz) == (0, 3) and not self.direct:
            self._half(slot, 0, p.slot(0, 1))
        elif (dy, dz) == (1, 0):
            self._full(slot, p.slot(0, 1))
            self._full(slot, p.slot(0, 3))
        self._full(slot, p.slot(0, 0, 1))

    def partner_wait(self, chip):
        slot = chip * 2 + (self.p.core + 1) % 2
        arrived(self._part(slot), self.rsem.at[self.chunk, slot])

    def drain(self):
        for index, rows in enumerate(self.sent):
            arrived(self.buf.at[0, pl.ds(0, rows)], self.ssem.at[self.chunk, index])

    @staticmethod
    def scratch(rows, chunks):
        return [
            pltpu.VMEM((16, rows, D), BF16),
            pltpu.SemaphoreType.DMA((chunks, Gather.SENDS)),
            pltpu.SemaphoreType.DMA((chunks, 16)),
            pltpu.SemaphoreType.DMA((chunks, 2)),
        ]

    @staticmethod
    def make(place, refs, chunks, direct=False):
        return [Gather(place, *refs, chunk, chunks, direct) for chunk in range(chunks)]


class Scatter:
    SENDS = 10

    def __init__(self, place, chunks, direct, part, xbuf, yfar, relay, fin, finy, ysend, yrec, *sems):
        self.p, self.chunks, self.direct = place, chunks, direct
        self.part, self.xbuf, self.yfar, self.relay = part, xbuf, yfar, relay
        self.fin, self.finy, self.ysend, self.yrec = fin, finy, ysend, yrec
        self.psem, self.xsem, self.ssem = sems[:3]
        self.yfar_sem, self.relay_sem, self.fin_sem, self.finy_sem, self.yrec_sem = sems[3:]
        self.rows = part.shape[1] // chunks
        self.half = self.rows // 2
        self.sent = {}

    @staticmethod
    def scratch(rows, chunks):
        return [
            pltpu.VMEM((16, rows, D), BF16),
            pltpu.VMEM((8, rows, D), BF16),
            pltpu.VMEM((rows, D), BF16),
            pltpu.VMEM((rows, D), BF16),
            pltpu.VMEM((2, rows, D), BF16),
            pltpu.VMEM((2, rows, D), BF16),
            pltpu.VMEM((rows, D), BF16),
            pltpu.VMEM((rows, D), BF16),
            pltpu.SemaphoreType.DMA((8,)),
            pltpu.SemaphoreType.DMA((8,)),
            pltpu.SemaphoreType.DMA((chunks * Scatter.SENDS,)),
            pltpu.SemaphoreType.DMA((chunks,)),
            pltpu.SemaphoreType.DMA((chunks, 2)),
            pltpu.SemaphoreType.DMA((chunks, 2, 2)),
            pltpu.SemaphoreType.DMA((chunks, 2)),
            pltpu.SemaphoreType.DMA((chunks,)),
        ]

    def partner_send(self, chip):
        slot = chip * 2 + (self.p.core + 1) % 2
        send(
            self.part.at[slot],
            self.xbuf.at[chip],
            self.psem.at[chip],
            self.xsem.at[chip],
            {"tensor": self.p.slot(0, 0, 1)},
        )

    def partner_add(self, chip):
        arrived(self.xbuf.at[chip], self.xsem.at[chip])
        slot = chip * 2 + self.p.core
        self.part[slot] = self.part[slot] + self.xbuf[chip]

    def _send(self, key, src, dst, recv_sem, target):
        index, _ = self.sent.setdefault(key, (len(self.sent), src.shape[0]))
        send(src, dst, self.ssem.at[index], recv_sem, {"tensor": target})

    def all_rows(self, chunk):
        return pl.ds(chunk * self.rows, self.rows)

    def half_rows(self, chunk, which):
        return pl.ds(chunk * self.rows + which * self.half, self.half)

    def send_yfar(self):
        slot = self.p.slot(1, 2)
        for chunk in range(self.chunks):
            rows = self.all_rows(chunk)
            self._send(
                ("yfar", chunk),
                self.part.at[slot, rows],
                self.yfar.at[rows],
                self.yfar_sem.at[chunk],
                self.p.slot(1, 0),
            )

    def send_side(self, way):
        dz = (1, 3)[way]
        slot = self.p.slot(1, dz)
        for chunk in range(self.chunks):
            rows = self.all_rows(chunk)
            self._send(
                ("side", chunk, way),
                self.part.at[slot, rows],
                self.finy.at[way, rows],
                self.finy_sem.at[chunk, way],
                self.p.slot(0, dz),
            )

    def _near(self, chunk, way, which):
        dz = (1, 3)[way]
        rows = self.half_rows(chunk, which)
        self._send(
            ("near", chunk, way, which),
            self.part.at[self.p.slot(0, dz), rows],
            self.fin.at[way, rows],
            self.fin_sem.at[chunk, way, which],
            self.p.slot(0, dz),
        )

    def send_near(self, chunk, ways=(0, 1)):
        for way in ways:
            for which in (0, 1):
                self._near(chunk, way, which)

    def send_role(self, chip):
        p = self.p
        dy, dz = (chip // 4 + p.y) % 2, (chip % 4 + 4 - p.z) % 4

        def when(row, column, action):
            @pl.when(jnp.logical_and(dy == row, dz == column))
            def _():
                action()

        when(1, 2, self.send_yfar)
        for way, column in ((0, 1), (1, 3)):
            when(1, column, functools.partial(self.send_side, way))
            when(0, column, lambda way=way: [self.send_near(c, (way,)) for c in range(self.chunks)])

    def far(self, chunk):
        rows = self.all_rows(chunk)
        slot = self.p.slot(0, 2)
        arrived(self.yfar.at[rows], self.yfar_sem.at[chunk])
        self.part[slot, rows, :] = self.part[slot, rows, :] + self.yfar[rows, :]
        if self.direct:
            self._send(
                ("far", chunk),
                self.part.at[slot, rows],
                self.relay.at[rows],
                self.relay_sem.at[chunk, 0],
                slot,
            )
            return
        self._near(chunk, 0, 1)
        self._near(chunk, 1, 0)
        for way in (0, 1):
            self._send(
                ("far", chunk, way),
                self.part.at[slot, self.half_rows(chunk, way)],
                self.relay.at[self.half_rows(chunk, way)],
                self.relay_sem.at[chunk, way],
                self.p.slot(0, (1, 3)[way]),
            )

    def cross_sum(self, chunk):
        rows = self.all_rows(chunk)
        for way in (0, 1):
            arrived(self.finy.at[way, rows], self.finy_sem.at[chunk, way])
        total = self.part[self.p.slot(1, 0), rows, :].astype(F32)
        total = total + self.finy[0, rows, :].astype(F32) + self.finy[1, rows, :].astype(F32)
        self.ysend[rows, :] = total.astype(BF16)

    def cross_send(self, chunk):
        rows = self.all_rows(chunk)
        self._send(
            ("cross", chunk),
            self.ysend.at[rows],
            self.yrec.at[rows],
            self.yrec_sem.at[chunk],
            self.p.slot(1, 0),
        )

    def relay_add(self, chunk):
        for way in (0, 1):
            slot, rows = self.p.slot(0, (1, 3)[way]), self.half_rows(chunk, way)
            arrived(self.relay.at[rows], self.relay_sem.at[chunk, way])
            self.part[slot, rows, :] = self.part[slot, rows, :] + self.relay[rows, :]

    def relay_send(self, chunk):
        for way in (0, 1):
            self._near(chunk, way, way)

    def total(self, chunk):
        rows = self.all_rows(chunk)
        for way in (0, 1):
            for which in (0, 1):
                arrived(
                    self.fin.at[way, self.half_rows(chunk, which)],
                    self.fin_sem.at[chunk, way, which],
                )
        own = self.part[self.p.me, rows, :].astype(F32)
        own = own + self.fin[0, rows, :].astype(F32) + self.fin[1, rows, :].astype(F32)
        if self.direct:
            arrived(self.relay.at[rows], self.relay_sem.at[chunk, 0])
            own = own + self.relay[rows, :].astype(F32)
        arrived(self.yrec.at[rows], self.yrec_sem.at[chunk])
        return own + self.yrec[rows, :].astype(F32)

    def run(self, *stages):
        if self.direct:
            steps = (self.cross_sum, self.cross_send) + stages
        else:
            steps = (
                self.far,
                self.cross_sum,
                lambda chunk: (self.cross_send(chunk), self.relay_add(chunk)),
                self.relay_send,
            ) + stages
        for time in range(self.chunks + len(steps) - 1):
            for index, stage in enumerate(steps):
                if 0 <= time - index < self.chunks:
                    stage(time - index)

    def drain(self):
        for chip in range(8):
            slot = chip * 2 + (self.p.core + 1) % 2
            arrived(self.part.at[slot], self.psem.at[chip])
        for index, rows in self.sent.values():
            arrived(self.part.at[0, pl.ds(0, rows)], self.ssem.at[index])


def dot(left, right):
    return jnp.dot(left, right, preferred_element_type=F32)


def dot_t(left, right):
    return lax.dot_general(left, right, (((1,), (1,)), ((), ())), preferred_element_type=F32)


def softmax_weights(scores):
    row_max = jnp.max(scores, axis=-1, keepdims=True)
    exponent = jnp.exp(scores - row_max)
    return (exponent * (1.0 / jnp.sum(exponent, axis=-1, keepdims=True))).astype(BF16)


def layer_kernel(*refs):
    refs = list(refs)

    def take(count):
        taken, refs[:count] = refs[:count], []
        return taken

    small_hbm, hbm = take(11), take(10)
    memory_out, dec_out = take(2)
    small = take(10)
    lengths, gain, bias, mem_gain, dec_tokens = small[:5]
    tags, table, cross_gain, ffn_gain, tgt_length = small[5:]
    (small_sem,) = take(1)
    weights = take(10)
    (weight_sem,) = take(1)
    wq, wk, wv, wo, cq, ck, cv, co, win, wout = weights
    grid, q_s, k_s, v_s, s_s, w_s, ctx = take(7)
    hop, back_sem, swap_sem = take(3)
    inp, q_all, cross_ctx, act, hidden = take(5)
    place = Place()
    enc_refs, mem_refs, dec_refs, ffn_refs = take(4), take(4), take(4), take(4)
    enc = Gather.make(place, enc_refs, ROW_CHUNKS)
    mem = Gather.make(place, mem_refs, MEM_CHUNKS)
    (dec,) = Gather.make(place, dec_refs, 1, True)
    ffn = Gather.make(place, ffn_refs, DEC_CHUNKS, True)
    enc_sum = Scatter(place, ENC_CHUNKS, True, *take(16))
    cross_sum = Scatter(place, DEC_CHUNKS, True, *take(16))
    ffn_sum = Scatter(place, DEC_CHUNKS, True, *take(16))

    def events(gathers, *numbers):
        for number in numbers:
            for gather in gathers:
                gather.event(number)

    loads = [
        pltpu.make_async_copy(src, dst, weight_sem.at[index])
        for index, (src, dst) in enumerate(zip(hbm, weights))
    ]
    owner = place.slot(0, 4 - place.x)
    enc_buf, mem_buf, dec_buf, ffn_buf = enc_refs[0], mem_refs[0], dec_refs[0], ffn_refs[0]
    fetch = [
        pltpu.make_async_copy(src, dst, small_sem.at[index])
        for index, (src, dst) in enumerate(zip(small_hbm[1:], small))
    ]
    own_rows = pltpu.make_async_copy(small_hbm[0].at[0], enc_buf.at[place.me], small_sem.at[10])
    own_rows.start()
    for copy in fetch:
        copy.start()
    for load in loads[:4]:
        load.start()
    swap_dp = ((place.z + 4 - place.x) % 4) * 2 + place.core
    swap_t = place.y * 8 + place.z * 2 + place.y_lo
    stays = jnp.logical_and(swap_dp == place.dp, swap_t == place.me)
    moves = jnp.logical_not(stays)

    barrier = pltpu.get_barrier_semaphore()
    for target in (
        place.slot(0, 0, 1),
        place.slot(0, 1),
        place.slot(0, 3),
        place.slot(0, 2),
        place.slot(1, 0),
    ):
        pl.semaphore_signal(barrier, inc=1, device_id={"tensor": target}, device_id_type=MESH)

    @pl.when(moves)
    def _():
        pl.semaphore_signal(barrier, inc=1, device_id=(swap_dp, swap_t), device_id_type=MESH)

    own_rows.wait()

    @pl.when(moves)
    def _():
        pl.semaphore_wait(barrier, 6)

    @pl.when(stays)
    def _():
        pl.semaphore_wait(barrier, 5)

    for gather in enc:
        gather.start()
    for copy in fetch:
        copy.wait()
    tag = tags[place.me]
    lang = jnp.zeros((1, D), F32)
    for index in range(LANGS):
        lang = jnp.where(tag == index, table[index : index + 1, :].astype(F32), lang)
    value = dec_tokens[0].astype(F32) + lang
    inp[...] = value
    dec_buf[place.me] = rms(value, cross_gain[...]).astype(BF16)

    keys = lax.broadcasted_iota(jnp.int32, (SRC, SRC), 1)
    bucket = jnp.clip(keys - lax.broadcasted_iota(jnp.int32, (SRC, SRC), 0), -MAXREL, MAXREL) + MAXREL
    for head in range(HEADS):
        values = jnp.zeros((SRC, SRC), F32)
        for index in range(NB):
            values = jnp.where(bucket == index, bias[head, index], values)
        grid[head] = values
    for load in loads[:4]:
        load.wait()

    items = [(ex, head) for ex in range(2) for head in range(HEADS)]

    def sum_chip(index):
        chip = chip_at(place, GATHER_ORDER, index)
        return chip // 4 * 4 + (chip % 4 + place.x) % 4

    def enc_step(index, carry):
        @pl.when(index == 1)
        def _():
            events(enc, 1, 2, 3)
            for load in loads[4:]:
                load.start()

        @pl.when(index == 4)
        def _():
            events(enc, 4, 5, 6)

        @pl.when(index == 7)
        def _():
            events(enc, 7)

        def attend():
            chip = chip_at(place, GATHER_ORDER, index)
            for gather in enc:
                gather.partner_wait(chip)
            raw = enc_buf[pl.ds(chip * 2, 2)].reshape(2 * SRC, D)
            rows = rms(raw.astype(F32), gain[...]).astype(BF16)
            q_s[...] = dot(rows, wq[...]).astype(BF16)
            k_s[...] = dot(rows, wk[...]).astype(BF16)
            v_s[...] = dot(rows, wv[...]).astype(BF16)
            columns = lax.broadcasted_iota(jnp.int32, (SRC, SRC), 1)
            for item, (ex, head) in enumerate(items):
                here, cols = slice(ex * SRC, (ex + 1) * SRC), slice(head * HD, (head + 1) * HD)
                s_s[item] = dot_t(q_s[here, cols], k_s[here, cols])
            for item, (ex, head) in enumerate(items):
                length = lengths[place.dp * 16 + chip * 2 + ex]
                scores = s_s[item] * SCALE + grid[head]
                w_s[item] = softmax_weights(jnp.where(columns < length, scores, NEG_FILL))
            for item, (ex, head) in enumerate(items):
                here, cols = slice(ex * SRC, (ex + 1) * SRC), slice(head * HD, (head + 1) * HD)
                ctx[here, cols] = dot(w_s[item], v_s[here, cols]).astype(BF16)

        attend()

        @pl.when(index > 1)
        def _():
            done = sum_chip(index - 2)
            enc_sum.partner_add(done)
            enc_sum.send_role(done)

        terms = dot(ctx[...], wo[...]).astype(BF16).reshape(2, SRC, D)
        enc_sum.part[pl.ds(sum_chip(index) * 2, 2)] = terms

        @pl.when(index > 0)
        def _():
            enc_sum.partner_send(sum_chip(index - 1))

        return carry

    lax.fori_loop(0, 8, enc_step, 0)
    enc_sum.partner_send(sum_chip(7))
    for index in (6, 7):
        done = sum_chip(index)
        enc_sum.partner_add(done)
        enc_sum.send_role(done)
    for chunk in range(ENC_CHUNKS):
        enc_sum.far(chunk)
    dec.start_far()
    dec.start()

    def finish_memory(chunk):
        rows = enc_sum.all_rows(chunk)
        value = enc_buf[owner, rows, :].astype(F32) + enc_sum.total(chunk)
        hop[rows, :] = rms(value, mem_gain[...]).astype(BF16)

    def give_back():
        @pl.when(place.x == 0)
        def _():
            pltpu.make_async_copy(hop, memory_out.at[0], back_sem.at[1]).start()

        @pl.when(place.x > 0)
        def _():
            send(hop, memory_out.at[0], back_sem.at[0], back_sem.at[1], {"tensor": owner})

    def swap_send(chunk):
        rows = enc_sum.all_rows(chunk)

        if chunk == ENC_CHUNKS - 2:
            events([dec], 4, 1, 2, 3)

        @pl.when(stays)
        def _():
            pltpu.make_async_copy(
                hop.at[rows], mem_buf.at[place.me, rows], swap_sem.at[1, chunk]
            ).start()

        @pl.when(moves)
        def _():
            send(
                hop.at[rows],
                mem_buf.at[swap_t, rows],
                swap_sem.at[0, chunk],
                swap_sem.at[1, chunk],
                (swap_dp, swap_t),
            )

    def spread(chunk):
        rows = enc_sum.all_rows(chunk)
        if chunk == ENC_CHUNKS - 1:
            events([dec], 5, 6, 7)
        arrived(mem_buf.at[place.me, rows], swap_sem.at[1, chunk])
        each = ENC_CHUNKS // MEM_CHUNKS
        if chunk % each == each - 1:
            mem[chunk // each].start()

    enc_sum.run(finish_memory, swap_send, spread)

    for chip in range(8):
        dec.partner_wait(chip)
    for load in loads[4:8]:
        load.wait()

    def q_step(index, carry):
        rows = dec_buf[pl.ds(index * 4, 4)].reshape(4 * TGT, D)
        q_all[pl.ds(index * 4, 4)] = dot(rows, cq[...]).astype(BF16).reshape(4, TGT, HW)
        return carry

    lax.fori_loop(0, 4, q_step, 0)

    def cross_chip(dz):
        return (place.z + dz + 4 - place.x) % 4 * 2

    def sum_cross(dz):
        for chip in (cross_chip(dz), cross_chip(dz) + 1):
            cross_sum.partner_add(chip)
            cross_sum.send_role(chip)

    def cross_step(index, carry):
        @pl.when(index == 1)
        def _():
            events(mem, 1, 2, 3)

        @pl.when(index == 4)
        def _():
            events(mem, 4, 5, 6)

        @pl.when(index == 7)
        def _():
            events(mem, 7)

        chip = chip_at(place, GATHER_ORDER, index)
        for gather in mem:
            gather.partner_wait(chip)
        rows = mem_buf[pl.ds(chip * 2, 2)].reshape(2 * SRC, D)
        k_s[...] = dot(rows, ck[...]).astype(BF16)
        v_s[...] = dot(rows, cv[...]).astype(BF16)
        columns = lax.broadcasted_iota(jnp.int32, (TGT, SRC), 1)
        base = ((chip % 4 + 4 - place.x) % 4) * 4 + chip // 4
        for item, (ex, head) in enumerate(items):
            here, cols = slice(ex * SRC, (ex + 1) * SRC), slice(head * HD, (head + 1) * HD)
            s_s[item, :TGT, :] = dot_t(q_all[base + 2 * ex, :, cols], k_s[here, cols])
        for item, (ex, head) in enumerate(items):
            row = base + 2 * ex
            length = lengths[(row // 2) * 16 + (row % 2) * 8 + place.dp]
            scores = s_s[item, :TGT, :] * SCALE
            w_s[item, :TGT, :] = softmax_weights(jnp.where(columns < length, scores, NEG_FILL))
        for item, (ex, head) in enumerate(items):
            here, cols = slice(ex * SRC, (ex + 1) * SRC), slice(head * HD, (head + 1) * HD)
            cross_ctx[base + 2 * ex, :, cols] = dot(w_s[item, :TGT, :], v_s[here, cols]).astype(BF16)

        @pl.when(jnp.logical_or(index == 3, index > 4))
        def _():
            @pl.when(index > 3)
            def _():
                sum_cross((PAIR_BEFORE >> (2 * index)) & 3)

            first = cross_chip((PAIR_DZ >> (2 * index)) & 3)
            block = cross_ctx[pl.ds(first * 2, 4)].reshape(4 * TGT, HW)
            cross_sum.part[pl.ds(first * 2, 4)] = dot(block, co[...]).astype(BF16).reshape(4, TGT, D)
            cross_sum.partner_send(first)
            cross_sum.partner_send(first + 1)

        return carry

    lax.fori_loop(0, 8, cross_step, 0)
    sum_cross(2)
    for chunk in range(DEC_CHUNKS):
        cross_sum.far(chunk)

    def finish_hidden(chunk):
        rows = cross_sum.all_rows(chunk)
        value = inp[rows, :] + cross_sum.total(chunk)
        hidden[rows, :] = value
        ffn_buf[place.me, rows, :] = rms(value, ffn_gain[...]).astype(BF16)

    cross_sum.run(finish_hidden, lambda chunk: ffn[chunk].start())
    for gather in ffn:
        gather.start_far()
    for load in loads[8:]:
        load.wait()

    def ffn_chips(chips):
        rows = [ffn_buf[pl.ds(chip * 2, 2)].reshape(2 * TGT, D) for chip in chips]
        rows = rows[0] if len(chips) == 1 else jnp.concatenate(rows, axis=0)
        count = rows.shape[0]
        for tile in range(FF // 512):
            cols = slice(tile * 512, (tile + 1) * 512)
            act[:count, cols] = jnp.maximum(dot(rows, win[:, cols]), 0.0).astype(BF16)
        yield
        for tile in range(D // 256):
            cols = slice(tile * 256, (tile + 1) * 256)
            result = dot(act[:count, :], wout[:, cols]).astype(BF16)
            for index, chip in enumerate(chips):
                here = slice(index * 2 * TGT, (index + 1) * 2 * TGT)
                ffn_sum.part[pl.ds(chip * 2, 2), :, cols] = result[here].reshape(2, TGT, 256)
        for chip in chips:
            ffn_sum.partner_send(chip)

    def ready(*chips):
        for chip in chips:
            for gather in ffn:
                gather.partner_wait(chip)

    own = place.chip(0, 0)
    ready(own)
    for _ in ffn_chips([own]):
        pass

    def ffn_step(index, carry):
        @pl.when(index == 0)
        def _():
            events(ffn, 1, 2, 3)
            give_back()

        @pl.when(index == 1)
        def _():
            events(ffn, 4, 5, 6)

        @pl.when(index == 2)
        def _():
            events(ffn, 7)
            ready(place.chip(0, 3))

        chips = [chip_at(place, FFN_ORDER, index * 2 + item) for item in range(2)]
        ready(*chips)
        halfway = ffn_chips(chips)
        next(halfway)

        @pl.when(index == 0)
        def _():
            ffn_sum.partner_add(own)

        @pl.when(index > 0)
        def _():
            for item in range(2):
                ffn_sum.partner_add(chip_at(place, FFN_ORDER, index * 2 - 2 + item))

        @pl.when(index == 1)
        def _():
            for chunk in range(DEC_CHUNKS):
                ffn_sum.send_near(chunk, (0,))

        @pl.when(index == 2)
        def _():
            ffn_sum.send_side(0)
            ffn_sum.send_side(1)

        for _ in halfway:
            pass
        return carry

    lax.fori_loop(0, 3, ffn_step, 0)
    last = ffn_chips([place.chip(0, 3)])
    next(last)
    for item in (4, 5):
        ffn_sum.partner_add(place.chip(*FFN_ORDER[item]))
    ffn_sum.send_yfar()
    for _ in last:
        pass
    for chunk in range(DEC_CHUNKS):
        ffn_sum.far(chunk)
    ffn_sum.partner_add(place.chip(0, 3))
    for chunk in range(DEC_CHUNKS):
        ffn_sum.send_near(chunk, (1,))

    def finish_out(chunk):
        rows = ffn_sum.all_rows(chunk)
        value = hidden[rows, :] + ffn_sum.total(chunk)
        position = lax.broadcasted_iota(jnp.int32, value.shape, 0) + chunk * ffn_sum.rows
        dec_out[0, rows, :] = jnp.where(position < tgt_length[0], value, 0.0).astype(BF16)

    ffn_sum.run(finish_out)

    arrived(memory_out.at[0], back_sem.at[1])

    @pl.when(place.x > 0)
    def _():
        arrived(hop, back_sem.at[0])

    @pl.when(moves)
    def _():
        for chunk in range(ENC_CHUNKS):
            arrived(hop.at[enc_sum.all_rows(chunk)], swap_sem.at[0, chunk])

    for stage in [*enc, dec, *mem, *ffn, enc_sum, cross_sum, ffn_sum]:
        stage.drain()


def leave_kernel(memory, dec, memory_out, dec_out):
    memory_out[...] = memory[...]
    dec_out[...] = dec[...]


VM = pltpu.VMEM
SM = pltpu.SMEM


def on_device(
    enc_tokens,
    src_lengths,
    enc_gain,
    enc_query,
    enc_key,
    enc_value,
    enc_output,
    enc_bias,
    mem_gain,
    dec_tokens,
    tgt_lengths,
    lang_tags,
    lang_table,
    cross_gain,
    cross_query,
    cross_key,
    cross_value,
    cross_output,
    ffn_gain,
    ffn_in,
    ffn_out,
):
    weights = [
        enc_query,
        enc_key,
        enc_value,
        enc_output,
        cross_query,
        cross_key,
        cross_value,
        cross_output,
        ffn_in,
        ffn_out,
    ]
    small = [
        enc_tokens,
        src_lengths,
        enc_gain,
        enc_bias,
        mem_gain,
        dec_tokens,
        lang_tags,
        lang_table,
        cross_gain,
        ffn_gain,
        tgt_lengths,
    ]
    spaces = [SM, VM, SM, VM, VM, SM, VM, VM, VM, SM]
    scratch = [space(value.shape, value.dtype) for space, value in zip(spaces, small[1:])]
    scratch += [pltpu.SemaphoreType.DMA((len(small),))]
    scratch += [pltpu.VMEM(weight.shape, BF16) for weight in weights]
    scratch += [
        pltpu.SemaphoreType.DMA((len(weights),)),
        pltpu.VMEM((HEADS, SRC, SRC), F32),
        pltpu.VMEM((2 * SRC, HW), BF16),
        pltpu.VMEM((2 * SRC, HW), BF16),
        pltpu.VMEM((2 * SRC, HW), BF16),
        pltpu.VMEM((2 * HEADS, SRC, SRC), F32),
        pltpu.VMEM((2 * HEADS, SRC, SRC), BF16),
        pltpu.VMEM((2 * SRC, HW), BF16),
        pltpu.VMEM((SRC, D), BF16),
        pltpu.SemaphoreType.DMA((2,)),
        pltpu.SemaphoreType.DMA((2, ENC_CHUNKS)),
        pltpu.VMEM((TGT, D), F32),
        pltpu.VMEM((16, TGT, HW), BF16),
        pltpu.VMEM((16, TGT, HW), BF16),
        pltpu.VMEM((4 * TGT, FF), BF16),
        pltpu.VMEM((TGT, D), F32),
    ]
    scratch += Gather.scratch(SRC, ROW_CHUNKS)
    scratch += Gather.scratch(SRC, MEM_CHUNKS)
    scratch += Gather.scratch(TGT, 1)
    scratch += Gather.scratch(TGT, DEC_CHUNKS)
    scratch += Scatter.scratch(SRC, ENC_CHUNKS)
    scratch += Scatter.scratch(TGT, DEC_CHUNKS)
    scratch += Scatter.scratch(TGT, DEC_CHUNKS)
    memory, dec = pl.pallas_call(
        layer_kernel,
        out_shape=(
            jax.ShapeDtypeStruct((1, SRC, D), BF16),
            jax.ShapeDtypeStruct((1, TGT, D), BF16),
        ),
        in_specs=[pl.BlockSpec(memory_space=pl.ANY)] * (len(small) + len(weights)),
        out_specs=(pl.BlockSpec(memory_space=VM), pl.BlockSpec(memory_space=VM)),
        scratch_shapes=scratch,
        compiler_params=pltpu.CompilerParams(
            collective_id=1, has_side_effects=True, vmem_limit_bytes=67_043_328
        ),
    )(*small, *weights)
    return pl.pallas_call(
        leave_kernel,
        out_shape=(
            jax.ShapeDtypeStruct(memory.shape, BF16),
            jax.ShapeDtypeStruct(dec.shape, BF16),
        ),
        in_specs=[pl.BlockSpec(memory_space=VM)] * 2,
        out_specs=(pl.BlockSpec(memory_space=VM), pl.BlockSpec(memory_space=VM)),
    )(memory, dec)


def solution(mesh):
    in_specs = (
        P(("dp", "tensor"), None, None),
        P(),
        P(),
        P(None, "tensor"),
        P(None, "tensor"),
        P(None, "tensor"),
        P("tensor", None),
        P("tensor", None),
        P(),
        P(("dp", "tensor"), None, None),
        P(("dp", "tensor")),
        P("dp"),
        P(),
        P(),
        P(None, "tensor"),
        P(None, "tensor"),
        P(None, "tensor"),
        P("tensor", None),
        P(),
        P(None, "tensor"),
        P("tensor", None),
    )
    out_specs = (P(("dp", "tensor"), None, None), P(("dp", "tensor"), None, None))
    return jax.shard_map(
        on_device, mesh=mesh, in_specs=in_specs, out_specs=out_specs, check_vma=False
    )
```
